128 devices in a mesh: gx: 4 (over x), gy: 8 (over z, core), gz: 4 (over y).
Axes of the slice: x: 4, y: 4, z: 4, core: 2. Of those that a mesh axis runs over, the one named last changes fastest.
Arguments:
- starting_warmth: float32 [32, 1024, 1024], P('gz', 'gx', 'gy'), may hold values from -6 to 6
- sheet_stratum_number: int32 [32], replicated, may hold values from 0 to 15
- stratum_heat_conduction: float32 [16], replicated, may hold values from 1 to 16
- substance_kind: int32 [32, 1024, 1024], P('gz', 'gx', 'gy'), may hold values from 0 to 3
- substance_kind_scaling: float32 [4], replicated, may hold values from 0.5 to 1.5
- wire_piece_amperes: float32 [524288], P(('gx', 'gy', 'gz')), may hold values from -6 to 6
- wire_piece_ohms_base: float32 [524288], P(('gx', 'gy', 'gz')), may hold values from 0.5 to 2
- wire_piece_tile: int32 [524288, 1], P(('gx', 'gy', 'gz')), may hold values from 0 to 127; in each aligned block of 4096 rows (0 to 4095, 4096 to 8191, ...) at most 64 rows name the same one
- wire_piece_voxel: int32 [524288], P(('gx', 'gy', 'gz')), may hold values from 0 to 262143
Outputs:
- warmed: float32 [32, 1024, 1024], P('gz', 'gx', 'gy')
- ohmic_power_final: float32 [32, 1024, 1024], P('gz', 'gx', 'gy')
The draws below stay inside these ranges and needn't reach their ends.
Inputs may be any that keep to these rules, and one draw needn't show every extreme that they name: `wire_piece_tile`: among the 4096 segments of one device, at most 64 name the same block, and some block is named by exactly 64 of them.
All inputs are finite; a program needn't handle non-finite values.
Results may differ from the reference program's by a relative error of at most 0.0029.
Values sent between devices are 32-bit elements; how exact they have to be, the bound alone decides.
A program may use at most 128 MiB of HBM per device.

```python
import math
import jax
import jax.numpy as jnp
import numpy as np
from jax import lax

CX = 256
CY = 128
CZ = 8
S_DEV = 4096
LAYERS = 16
CLASSES = 4
STEPS = 2
GRID_WIDE_SIZE = 1024
GRID_DEEP_SIZE = 1024
GRID_TALL_SIZE = 32
SEGS = 524288
MOST = 64
N_GY = 8
N_GZ = 4
DEVICES = 128


def plant(drawn, stream_key, smallest, largest):
    longest = drawn.shape.index(max(drawn.shape))
    spots = []
    for shift in (0, 1):
        where = [jax.random.randint(jax.random.fold_in(stream_key, axis), (), 0, length) for axis, length in enumerate(drawn.shape)]
        where[longest] = (where[longest] + shift) % drawn.shape[longest]
        spots.append(tuple(where))
    return drawn.at[spots[0]].set(smallest).at[spots[1]].set(largest)


def block_levels(own_key, extent, cuts, least, top_value):
    level, own = 1.0, jax.random.fold_in(own_key, 6)
    for axis_at, parts in cuts:
        draws = jnp.exp(jax.random.uniform(jax.random.fold_in(own, axis_at), (parts,), jnp.float32, least / len(cuts), top_value / len(cuts)))
        level = level * jnp.repeat(draws, extent[axis_at] // parts).reshape([-1 if axis == axis_at else 1 for axis in range(len(extent))])
    return level


def deal_out(own_key, own, number, rows, count, top, most, lean):
    order = jax.random.permutation(own_key, count)
    packed, ordinary = shares(count, rows * top, most, lean, True), shares(count, rows * top, most, lean, False)
    places = jnp.arange(count)

    def named(lengths, rotation):
        used = int((lengths > 0).sum())
        fixed = max(1, used // 4)
        shifted = fixed + (places - fixed + rotation * (used - fixed)) % max(1, count - fixed)
        return jnp.zeros((count,), jnp.int32).at[order[jnp.where(places < fixed, places, shifted)]].set(jnp.asarray(lengths, jnp.int32))

    lengths = jnp.where(number % 4 == 0, named(packed, number // 4), named(ordinary, number - number // 4 - 1))
    mixed = jax.random.permutation(jax.random.fold_in(own, 3), count)
    source_of, receiver = mixed[0:count // 2 * 2:2], mixed[1:count // 2 * 2:2]
    room = jnp.minimum(lengths[source_of] - 1, most - lengths[receiver]) // 2
    room = jnp.where((source_of == order[0]) | (receiver == order[0]) | (lengths[receiver] == 0), 0, jnp.maximum(room, 0))
    shifted = jax.random.randint(jax.random.fold_in(own, 4), (count // 2,), 0, 1 << 20) % (room + 1)
    lengths = lengths.at[source_of].add(-shifted).at[receiver].add(shifted)
    labels = jnp.searchsorted(jnp.cumsum(lengths), jnp.arange(rows * top), side="right").astype(jnp.int32)
    table = labels.reshape(top, rows).T
    table = table[jax.random.permutation(jax.random.fold_in(own, 1), rows)]
    rotation = jax.random.randint(jax.random.fold_in(own, 2), (rows, 1), 0, top)
    return jnp.take_along_axis(table, (jnp.arange(top)[None, :] + rotation) % top, axis=1)


def shares(amount, total, limit, lean, full):
    weights = [(1 << 20) // math.isqrt(grade ** lean) + 1 for grade in range(1, amount + 1)]
    largest = limit if full else min(limit, max(-(-total // amount), total * weights[0] // sum(weights)))
    least = 1 if total - largest >= amount - 1 else 0
    given, spare = [largest] + [least] * (amount - 1), total - largest - least * (amount - 1)
    while spare > 0:
        movable = [i for i in range(1, amount) if given[i] < largest] or [i for i in range(1, amount) if given[i] < limit]
        pool, remaining = sum([weights[i] for i in movable]), spare
        for i in movable:
            more = min(limit - given[i], max(1, remaining * weights[i] // pool), spare)
            given[i] = given[i] + more
            spare = spare - more
    return np.array(given)


def scatter_about(own_key, extent, width, most, split=(), held_as=jnp.bfloat16):
    drawn = width * jax.random.normal(own_key, extent, jnp.float32)
    if split:
        drawn = drawn * block_levels(own_key, extent, split, -0.22, 0.18)
    return jnp.clip(drawn, -most, most).astype(held_as)


def setup_inputs(seed: int = 0) -> dict:
    arg_keys = jax.random.split(jax.random.key(seed), 10)
    starting_warmth = scatter_about(arg_keys[0], (GRID_TALL_SIZE, GRID_WIDE_SIZE, GRID_DEEP_SIZE), 1.0, 6.0, ((0, 4), (1, 4), (2, 8)), jnp.float32)
    sheet_stratum_number = plant(jax.random.randint(arg_keys[1], (GRID_TALL_SIZE,), 0, LAYERS), jax.random.fold_in(arg_keys[1], 1), 0, LAYERS - 1).astype(jnp.int32)
    stratum_heat_conduction = jnp.clip(jnp.exp(jax.random.uniform(arg_keys[2], (LAYERS,), jnp.float32, math.log(1.0), math.log(16.0))), 1.0, 16.0)
    substance_kind = plant(jax.random.randint(arg_keys[3], (GRID_TALL_SIZE, GRID_WIDE_SIZE, GRID_DEEP_SIZE), 0, CLASSES), jax.random.fold_in(arg_keys[3], 1), 0, CLASSES - 1).astype(jnp.int32)
    substance_kind_scaling = jnp.clip(1.0 + 0.1 * jax.random.normal(arg_keys[4], (CLASSES,), jnp.float32), 0.5, 1.5)
    wire_piece_amperes = scatter_about(arg_keys[5], (SEGS,), 1.0, 6.0, ((0, 128),), jnp.float32)
    wire_piece_ohms_base = jnp.clip(jnp.exp(math.log(2.0) - 1.3862944 * jax.random.uniform(arg_keys[6], (SEGS,), jnp.float32) ** block_levels(arg_keys[6], (SEGS,), ((0, 128),), -0.2, 0.2)), 0.5, 2.0)
    wire_piece_tile_keys = jax.random.split(jax.random.fold_in(arg_keys[7], 1), SEGS // S_DEV)
    wire_piece_tile_turns = jax.random.permutation(jax.random.fold_in(arg_keys[7], 3), SEGS // S_DEV)
    wire_piece_tile = jax.vmap(lambda own, number: deal_out(jax.random.fold_in(arg_keys[7], 2), own, number, S_DEV, DEVICES, 1, MOST, 1))(wire_piece_tile_keys, wire_piece_tile_turns).reshape((SEGS, 1))
    wire_piece_voxel = plant(jax.random.randint(arg_keys[8], (SEGS,), 0, CZ * CX * CY), jax.random.fold_in(arg_keys[8], 1), 0, (CZ * CX * CY) - 1).astype(jnp.int32)
    return {"starting_warmth": starting_warmth, "sheet_stratum_number": sheet_stratum_number, "stratum_heat_conduction": stratum_heat_conduction, "substance_kind": substance_kind, "substance_kind_scaling": substance_kind_scaling, "wire_piece_amperes": wire_piece_amperes, "wire_piece_ohms_base": wire_piece_ohms_base, "wire_piece_tile": wire_piece_tile, "wire_piece_voxel": wire_piece_voxel}


HEAT_SPREADING = 1000.0
STIFF = 1.5
WARMING_SLOPE = 0.1
OHMIC_POWER = 8.0


def solve_lines(conductance, power_input):
    sub_band = -HEAT_SPREADING * conductance[:-1]
    super_band = -HEAT_SPREADING * conductance[1:]
    main_band = 1.0 + HEAT_SPREADING * (conductance[:-1] + conductance[1:])

    def forward(running, entries):
        factor_before, value_before = running
        lower_entry, middle, upper_entry, right_side = entries
        divisor = middle - lower_entry * factor_before
        factor_now = upper_entry / divisor
        value_now = (right_side - lower_entry * value_before) / divisor
        return (factor_now, value_now), (factor_now, value_now)

    initial = (jnp.zeros(conductance.shape[1:], jnp.float32), jnp.zeros(power_input.shape[1:], jnp.float32))
    ignored, (factors, values) = lax.scan(forward, initial, (sub_band, main_band, super_band, power_input))

    def backward(running, entries):
        factor_now, value_now = entries
        solved = value_now - factor_now * running
        return solved, solved

    ignored, solution = lax.scan(backward, jnp.zeros(power_input.shape[1:], jnp.float32), (factors, values), reverse=True)
    return solution


def outflow_balance(field, conduct, along, to_sink):
    length = field.shape[along]
    lead_field = lax.slice_in_dim(field, 0, length - 1, axis=along)
    next_field = lax.slice_in_dim(field, 1, length, axis=along)
    lead_cond = lax.slice_in_dim(conduct, 0, length - 1, axis=along)
    next_cond = lax.slice_in_dim(conduct, 1, length, axis=along)
    fluxes = 0.5 * (lead_cond + next_cond) * (next_field - lead_field)
    nothing = jnp.zeros_like(lax.slice_in_dim(field, 0, 1, axis=along))
    if to_sink:
        bottom = lax.slice_in_dim(conduct, 0, 1, axis=along) * lax.slice_in_dim(field, 0, 1, axis=along)
    else:
        bottom = nothing
    under = jnp.concatenate([bottom, fluxes], axis=along)
    over = jnp.concatenate([fluxes, nothing], axis=along)
    return over - under


def reference(starting_warmth, sheet_stratum_number, stratum_heat_conduction, substance_kind, substance_kind_scaling, wire_piece_amperes, wire_piece_ohms_base, wire_piece_tile, wire_piece_voxel):
    plane_cond = stratum_heat_conduction[sheet_stratum_number]
    voxel_conductance = plane_cond[:, None, None] * substance_kind_scaling[substance_kind]
    owner_block = wire_piece_tile[:, 0]
    owner_row = owner_block // (N_GY * N_GZ)
    owner_column = (owner_block // N_GZ) % N_GY
    owner_slab = owner_block % N_GZ
    inner_slab = wire_piece_voxel // (CX * CY)
    inner_row = (wire_piece_voxel // CY) % CX
    inner_column = wire_piece_voxel % CY
    flat_index = ((owner_slab * CZ + inner_slab) * GRID_WIDE_SIZE + owner_row * CX + inner_row) * GRID_DEEP_SIZE + owner_column * CY + inner_column
    power = wire_piece_amperes * wire_piece_amperes * wire_piece_ohms_base
    ohmic_loss = jnp.zeros((GRID_TALL_SIZE * GRID_WIDE_SIZE * GRID_DEEP_SIZE,), jnp.float32).at[flat_index.astype(jnp.int32)].add(power).reshape(GRID_TALL_SIZE, GRID_WIDE_SIZE, GRID_DEEP_SIZE)
    edge_zero = jnp.zeros((1, GRID_TALL_SIZE, 1), jnp.float32)
    lateral = STIFF * plane_cond[None, :, None]
    row_faces = jnp.concatenate([edge_zero, jnp.broadcast_to(lateral, (GRID_WIDE_SIZE - 1, GRID_TALL_SIZE, 1)), edge_zero], axis=0)
    column_faces = jnp.concatenate([edge_zero, jnp.broadcast_to(lateral, (GRID_DEEP_SIZE - 1, GRID_TALL_SIZE, 1)), edge_zero], axis=0)
    slab_faces = STIFF * jnp.concatenate([plane_cond[:1], 0.5 * (plane_cond[:-1] + plane_cond[1:]), jnp.zeros((1,), jnp.float32)])
    slab_faces = slab_faces[:, None, None]
    warmth_excess = starting_warmth
    for repeat in range(STEPS):
        warming_energy = (1.0 + WARMING_SLOPE * warmth_excess) * ohmic_loss
        diffusion_term = outflow_balance(warmth_excess, voxel_conductance, 0, True) + outflow_balance(warmth_excess, voxel_conductance, 1, False) + outflow_balance(warmth_excess, voxel_conductance, 2, False)
        power_input = HEAT_SPREADING * diffusion_term + OHMIC_POWER * warming_energy
        first_pass = jnp.moveaxis(solve_lines(row_faces, jnp.moveaxis(power_input, 1, 0)), 0, 1)
        second_pass = jnp.moveaxis(solve_lines(column_faces, jnp.moveaxis(first_pass, 2, 0)), 0, 2)
        vertical_sweep_final = solve_lines(slab_faces, second_pass)
        warmth_excess = warmth_excess + vertical_sweep_final
    ohmic_power_final = (1.0 + WARMING_SLOPE * warmth_excess) * ohmic_loss
    return warmth_excess, ohmic_power_final
```

```python
import functools

import jax
import jax.numpy as jnp
from jax import lax
from jax.experimental import pallas as pl
from jax.experimental.pallas import tpu as pltpu
from jax.sharding import PartitionSpec as P

STEPS = 2
HEAT_SPREADING = 1000.0
STIFF = 1.5
WARMING_SLOPE = 0.1
OHMIC_POWER = 8.0

F32 = jnp.float32
BF16 = jnp.bfloat16
MESH = pl.DeviceIdType.MESH

CZ, CX, CY = 8, 256, 128
LEN = 1024
PLANES = 32
NX, NY, NZ = 4, 8, 4
SEGS = 4096
TOP = 64
DEVS = 128
PAD = 8
WIDE = CX + 2 * PAD
NCH = 4
CH = CX // NCH
NACC = 4
UNROLL = 32
VMEM_BYTES = 60 * 1024 * 1024


def dot(a, b):
    return jnp.dot(a, b, preferred_element_type=F32)


def halves(x):
    high = x.astype(BF16)
    return high, (x - high.astype(F32)).astype(BF16)


def pack_kernel(amp_ref, ohm_ref, tile_ref, cell_ref, out_ref, acc):
    width = 256
    row = lax.broadcasted_iota(jnp.int32, (width, width + DEVS), 0)
    col = lax.broadcasted_iota(jnp.int32, (width, width + DEVS), 1)
    before = jnp.where((row < col) | (col >= width), 1.0, 0.0).astype(BF16)
    owner = lax.broadcasted_iota(jnp.int32, (DEVS, width), 0)
    place = lax.broadcasted_iota(jnp.int32, (TOP, width), 0).astype(F32)
    acc[...] = jnp.zeros_like(acc)
    carry = jnp.zeros((DEVS, DEVS), F32)
    for j in range(SEGS // width):
        mine = owner == tile_ref[j : j + 1, :]
        hot = jnp.where(mine, 1.0, 0.0).astype(BF16)
        found = dot(hot, before)
        ahead = found[:, :width] + jnp.concatenate([carry, carry], axis=1)
        rank = jnp.sum(jnp.where(mine, ahead, 0.0), axis=0, keepdims=True)
        carry = carry + found[:, width:]
        amp = amp_ref[j : j + 1, :]
        power = amp * amp * ohm_ref[j : j + 1, :]
        p0 = power.astype(BF16).astype(F32)
        p1 = (power - p0).astype(BF16).astype(F32)
        p2 = power - p0 - p1
        cell = cell_ref[j : j + 1, :]
        c0 = (cell >> 12).astype(F32)
        c1 = ((cell >> 6) & 63).astype(F32)
        c2 = (cell & 63).astype(F32)
        here = place == rank
        parts = jnp.concatenate(
            [jnp.where(here, part, 0.0).astype(BF16) for part in (p0, c0, p1, c1, p2, c2)], axis=0
        )
        acc[...] += lax.dot_general(
            hot, parts, (((1,), (1,)), ((), ())), preferred_element_type=F32
        )
    a, b, c = (acc[:, 128 * k : 128 * (k + 1)] for k in range(3))
    powers = a + b + c
    cells = a * 4096.0 + b * 64.0 + c
    lane = lax.broadcasted_iota(jnp.int32, (DEVS, DEVS), 1)
    out_ref[...] = jnp.where(lane < TOP, powers, cells)


def packed(amp, ohm, tile, cell):
    return pl.pallas_call(
        pack_kernel,
        out_shape=jax.ShapeDtypeStruct((DEVS, DEVS), F32),
        scratch_shapes=[pltpu.VMEM((DEVS, 384), F32)],
        compiler_params=pltpu.CompilerParams(vmem_limit_bytes=VMEM_BYTES),
        name="pack",
    )(amp, ohm, tile, cell)


def add_kernel(row_ref, got_ref, out_ref, spread, *accs):
    turned = jnp.transpose(got_ref[...])
    lane = lax.broadcasted_iota(jnp.int32, (TOP, 128), 1)
    powers = turned[:TOP]
    cells = turned[TOP:].astype(jnp.int32) & 127
    for s in range(DEVS):
        spread[TOP * s : TOP * (s + 1), :] = jnp.where(
            lane == cells[:, s : s + 1], powers[:, s : s + 1], 0.0
        )
    for acc in accs:
        acc[...] = jnp.zeros_like(acc)

    def some(i, carry):
        for k in range(UNROLL):
            s = i * UNROLL + k
            acc = accs[k % NACC]
            r = row_ref[s]
            acc[pl.ds(r, 1), :] += spread[pl.ds(s, 1), :]
        return carry

    lax.fori_loop(0, DEVS * TOP // UNROLL, some, 0)
    total = accs[0][...]
    for acc in accs[1:]:
        total = total + acc[...]
    out_ref[...] = total


def added(rows, got):
    return pl.pallas_call(
        add_kernel,
        out_shape=jax.ShapeDtypeStruct((CZ * CX, CY), F32),
        in_specs=[
            pl.BlockSpec(memory_space=pltpu.SMEM),
            pl.BlockSpec(memory_space=pltpu.VMEM),
        ],
        out_specs=pl.BlockSpec(memory_space=pltpu.VMEM),
        scratch_shapes=[pltpu.VMEM((DEVS * TOP, 128), F32)]
        + [pltpu.VMEM((CZ * CX, CY), F32)] * NACC,
        compiler_params=pltpu.CompilerParams(vmem_limit_bytes=VMEM_BYTES),
        name="add",
    )(rows, got)


def line_weights(theta, scale, me, count, length):
    whole = 2 * LEN
    out = []
    for m in range(count):

        def tile(exponent, keep):
            return jnp.where(keep, jnp.exp(-theta * exponent.astype(F32)) * scale, 0.0)

        lower, same = m < me, me == m
        gap = jnp.where(lower, me - m, m - me)
        near, far = length * (gap - 1) + 1, whole - length * gap - (length - 1)
        apart = jnp.logical_not(same)
        out.append(
            (
                tile(jnp.where(lower, near, far), apart),
                tile(length * (me + m) + 1, True),
                tile(whole - length * (me + m + 2) + 1, True),
                tile(jnp.where(lower, far, near), apart),
            )
        )
    return out


def adi_kernel(
    sheet_ref,
    cond_ref,
    scale_ref,
    u_ref,
    kind_ref,
    joule_ref,
    warm_ref,
    ohmic_ref,
    upad,
    cpad,
    gxl,
    gxu,
    gyl,
    gyu,
    gz,
    gself,
    thi,
    tlo,
    y1,
    y2,
    lp,
    ln,
    rowp,
    rown,
    tables,
    xw,
    yw,
    pq,
    first,
    work,
    third,
    turn,
    xs,
    xr,
    ys,
    yr,
    xm,
    ym,
    zup,
    zdown,
    sup,
    sdown,
    xs_sem,
    xr_sem,
    ys_sem,
    yr_sem,
    zs_sem,
    zr_sem,
    xms_sem,
    xmr_sem,
    yms_sem,
    ymr_sem,
    ups_sem,
    upr_sem,
    dns_sem,
    dnr_sem,
):
    kx, ky, kz = lax.axis_index("gx"), lax.axis_index("gy"), lax.axis_index("gz")

    def around(me, shift, count):
        return lax.rem(me + shift + count, count)

    barrier = pltpu.get_barrier_semaphore()
    for axis, me, count in (("gx", kx, NX), ("gy", ky, NY), ("gz", kz, NZ)):
        for shift in range(1, count):
            pl.semaphore_signal(
                barrier, inc=1, device_id={axis: around(me, shift, count)}, device_id_type=MESH
            )

    def sent(src, dst, send, recv, axis, to):
        return pltpu.make_async_remote_copy(
            src_ref=src,
            dst_ref=dst,
            send_sem=send,
            recv_sem=recv,
            device_id={axis: to},
            device_id_type=MESH,
        )

    sub8 = lax.broadcasted_iota(jnp.int32, (8, 128), 0)
    lane8 = lax.broadcasted_iota(jnp.int32, (8, 128), 1)
    lane = lax.broadcasted_iota(jnp.int32, (CX, CY), 1)
    leaving = []

    for z in range(CZ):
        here = cond_ref[sheet_ref[CZ * kz + z]]
        kind = kind_ref[z]
        factor = jnp.where(kind == 0, scale_ref[0], 0.0)
        for category in range(1, 4):
            factor = jnp.where(kind == category, scale_ref[category], factor)
        cpad[z + 1, PAD : PAD + CX, :] = factor * here
        upad[z + 1, PAD : PAD + CX, :] = u_ref[z]

    def edge_columns(ref):
        out = jnp.zeros((CX, CY), F32)
        for z in range(CZ):
            rolled = pltpu.roll(ref[z + 1, PAD : PAD + CX, :], 2 * z + 1, 1)
            out = jnp.where((lane >> 1) == z, rolled, out)
        return jnp.transpose(out)[:16]

    def edge_rows(step, part, ref):
        at = pl.ds(8 * part, 8)
        xs[step, 0, at, :] = ref[1 : CZ + 1, PAD + CX - 1, :]
        xs[step, 1, at, :] = ref[1 : CZ + 1, PAD, :]
        ys[step, pl.ds(16 * part, 16), :] = edge_columns(ref)

    def edges_out(step):
        for side, to in ((0, 1), (1, -1)):
            leaving.append(
                sent(
                    xs.at[step, side],
                    xr.at[step, side],
                    xs_sem.at[step, side],
                    xr_sem.at[step, side],
                    "gx",
                    around(kx, to, NX),
                )
            )
            leaving[-1].start()
            leaving.append(
                sent(
                    ys.at[step],
                    yr.at[step, side],
                    ys_sem.at[step, side],
                    yr_sem.at[step, side],
                    "gy",
                    around(ky, to, NY),
                )
            )
            leaving[-1].start()

    edge_rows(0, 0, upad)
    edge_rows(0, 1, cpad)
    pl.semaphore_wait(barrier, NX + NY + NZ - 3)
    planes = []
    middle = pl.ds(PAD, CX)
    for k, (ref, side, source, target, to) in enumerate(
        (
            (upad, 0, CZ, 0, 1),
            (upad, 1, 1, CZ + 1, -1),
            (cpad, 0, CZ, 0, 1),
            (cpad, 1, 1, CZ + 1, -1),
        )
    ):
        planes.append(
            sent(
                ref.at[source, middle, :],
                ref.at[target, middle, :],
                zs_sem.at[k],
                zr_sem.at[k],
                "gz",
                around(kz, to, NZ),
            )
        )
    edges_out(0)
    for copy in planes:
        copy.start()

    own = jnp.zeros((8, 128), F32)
    for z in range(CZ):
        own = jnp.where(sub8 == z, cond_ref[sheet_ref[CZ * kz + z]], own)
    a = HEAT_SPREADING * STIFF * own
    s = 0.5 * lax.rsqrt(a)
    s = 0.5 * (s + 0.25 / (a * s))
    s2 = s * s
    theta = 2.0 * s * (1.0 - s2 * (1.0 / 6.0 - s2 * (3.0 / 40.0 - s2 * (15.0 / 336.0))))
    whole = jnp.exp(-theta * (2.0 * LEN))
    root = jnp.sqrt(a + 0.25)
    scale = 0.5 / (root * (1.0 - whole))
    tables[0] = theta
    tables[1] = scale
    tables[2] = scale * whole
    tables[3] = jnp.exp(-theta * (CX - 1.0))
    tables[4] = jnp.exp(-theta * (CY - 1.0))
    last_x, last_y = tables[3], tables[4]
    for h in range(2):
        at = (lane8 + 128 * h).astype(F32)
        rowp[h] = jnp.exp(-theta * at)
        rown[h] = jnp.exp(theta * at)
    for m, tiles in enumerate(line_weights(theta, scale, kx, NX, CX)):
        for k, tile in enumerate(tiles):
            xw[m, k] = tile if k < 2 else tile * last_x
    for m, tiles in enumerate(line_weights(theta, scale, ky, NY, CY)):
        for k, tile in enumerate(tiles):
            yw[m, k] = tile if k < 2 else tile * last_y

    conds = [jnp.full((8, 128), cond_ref[sheet_ref[z]], F32) for z in range(PLANES)]
    stiff = HEAT_SPREADING * STIFF
    links = [0.5 * stiff * (conds[z] + conds[z + 1]) for z in range(PLANES - 1)]
    up = [1.0 + stiff * conds[0]]
    grow = [jnp.ones((8, 128), F32)]
    for z in range(PLANES - 1):
        grow.append(grow[z] * (1.0 + up[z] / links[z]))
        up.append(1.0 + links[z] * (up[z] / (up[z] + links[z])))
    down = [None] * PLANES
    down[-1] = jnp.ones((8, 128), F32)
    for z in range(PLANES - 2, -1, -1):
        down[z] = 1.0 + links[z] * (down[z + 1] / (down[z + 1] + links[z]))
    nothing = jnp.zeros((8, 128), F32)
    pq[0, 0] = nothing
    pq[1, 0] = nothing
    pq[0, PLANES + 1] = nothing
    pq[1, PLANES + 1] = nothing
    for z in range(PLANES):
        pq[0, z + 1] = 1.0 / ((up[z] + down[z] - 1.0) * grow[z])
        pq[1, z + 1] = grow[z]

    row = lax.broadcasted_iota(jnp.int32, (CX, CY), 0).astype(F32)
    sub16 = lax.broadcasted_iota(jnp.int32, (16, 128), 0)
    lane_y = lax.broadcasted_iota(jnp.int32, (CY, CY), 1)

    def weights(z, carry):
        one = pl.ds(z, 1)
        th = tables[0, one, :]
        fall = jnp.exp(-th * row)
        rise = jnp.exp(th * row)
        lp[z] = fall
        ln[z] = rise
        c1, c2 = tables[1, one, :], tables[2, one, :]
        for h in range(2):
            x, y = fall * rown[h, one, :], rise * rowp[h, one, :]
            t = c1 * jnp.minimum(x, y) + c2 * jnp.maximum(x, y)
            cols = pl.ds(128 * h, 128)
            ends = jnp.where(
                sub16 == 0,
                tables[3, one, :] * rown[h, one, :],
                jnp.where(sub16 == 1, rowp[h, one, :], 0.0),
            )
            hi, lo = halves(t)
            thi[z, :CX, cols] = hi
            tlo[z, :CX, cols] = lo
            if h == 0:
                y1[z, :CY, :CY] = hi[:CY]
                y1[z, CY:, :CY] = hi[:CY]
                y2[z, :, :CY] = lo[:CY]
            hi, lo = halves(ends)
            thi[z, CX:, cols] = hi
            tlo[z, CX:, cols] = lo
        w = jnp.where(
            lane_y == z,
            rise[:CY] * tables[4, one, :],
            jnp.where(lane_y == z + 8, fall[:CY], 0.0),
        )
        hi, lo = halves(w)
        y1[z, :CY, CY:] = hi
        y1[z, CY:, CY:] = hi
        y2[z, :, CY:] = lo
        return carry

    lax.fori_loop(0, CZ, weights, 0)
    turn[...] = jnp.zeros_like(turn)

    def edges_in(step):
        for side in range(2):
            copy = leaving_by[step][2 * side]
            copy.wait_recv()
            leaving_by[step][2 * side + 1].wait_recv()

    def y_edges(step, part):
        at = pl.ds(16 * part, 16)
        low = pltpu.roll(yr[step, 0, at, :], 1, 0)
        high = pltpu.roll(yr[step, 1, at, :], 15, 0)
        odd = (lax.broadcasted_iota(jnp.int32, (16, CX), 0) & 1) == 1
        turn[:16, :] = jnp.where(odd, low, high)
        return jnp.transpose(turn[...])

    leaving_by = {0: leaving[:4]}
    edges_in(0)
    for copy in planes:
        copy.wait_recv()
        copy.wait_send()

    half = 0.5 * HEAT_SPREADING
    cpad[1 : CZ + 1, PAD - 1, :] = jnp.where(
        kx == 0, -cpad[1 : CZ + 1, PAD, :], xr[0, 0, 8:16, :]
    )
    cpad[1 : CZ + 1, PAD + CX, :] = jnp.where(
        kx == NX - 1, -cpad[1 : CZ + 1, PAD + CX - 1, :], xr[0, 1, 8:16, :]
    )
    work[0] = y_edges(0, 1)
    inner = pl.ds(PAD, CX)
    gz[0] = jnp.where(kz == 0, 0.0, half * (cpad[0, inner, :] + cpad[1, inner, :]))
    gz[CZ] = jnp.where(
        kz == NZ - 1, 0.0, half * (cpad[CZ, inner, :] + cpad[CZ + 1, inner, :])
    )
    for z in range(CZ - 1):
        gz[z + 1] = half * (cpad[z + 1, inner, :] + cpad[z + 2, inner, :])
    for z in range(CZ):
        c = cpad[z + 1, inner, :]
        edge = pltpu.roll(work[0], CY - (2 * z + 1), 1)
        low = jnp.where(lane == 0, jnp.where(ky == 0, -c, edge), pltpu.roll(c, 1, 1))
        high = jnp.where(
            lane == CY - 1, jnp.where(ky == NY - 1, -c, edge), pltpu.roll(c, CY - 1, 1)
        )
        xl = half * (c + cpad[z + 1, PAD - 1 : PAD + CX - 1, :])
        xu = half * (c + cpad[z + 1, PAD + 1 : PAD + CX + 1, :])
        yl, yu = half * (c + low), half * (c + high)
        gxl[z], gxu[z], gyl[z], gyu[z] = xl, xu, yl, yu
        every = xl + xu + yl + yu + gz[z] + gz[z + 1]
        if z == 0:
            every = every + jnp.where(kz == 0, HEAT_SPREADING * c, 0.0)
        gself[z] = (OHMIC_POWER * WARMING_SLOPE) * joule_ref[z] - every

    for step in range(STEPS):
        if step:
            leaving_by[step] = leaving[edges_at : edges_at + 4]
            edges_in(step)
        upad[1 : CZ + 1, PAD - 1, :] = xr[step, 0, 0:8, :]
        upad[1 : CZ + 1, PAD + CX, :] = xr[step, 1, 0:8, :]
        work[0] = y_edges(step, 0)

        def source_and_x(z, carry):
            u = upad[z + 1, inner, :]
            edge = pltpu.roll(work[0], CY - (2 * z + 1), 1)
            low = jnp.where(lane == 0, edge, pltpu.roll(u, 1, 1))
            high = jnp.where(lane == CY - 1, edge, pltpu.roll(u, CY - 1, 1))
            b = gself[z] * u + OHMIC_POWER * joule_ref[z]
            b = b + gyl[z] * low + gyu[z] * high
            b = b + gxl[z] * upad[z + 1, PAD - 1 : PAD + CX - 1, :]
            b = b + gxu[z] * upad[z + 1, PAD + 1 : PAD + CX + 1, :]
            b = b + gz[z] * upad[z, inner, :] + gz[z + 1] * upad[z + 2, inner, :]
            hi, lo = halves(b)
            r = dot(thi[z], jnp.concatenate([hi, lo], axis=1))
            r = r[:, :CY] + r[:, CY:] + dot(tlo[z], hi)
            first[z] = r[:CX]
            xm[step, kx, pl.ds(z, 1), :] = r[CX : CX + 1]
            xm[step, kx, pl.ds(z + 8, 1), :] = r[CX + 1 : CX + 2]
            return carry

        for z in range(CZ):
            source_and_x(z, 0)

        moments = []
        for shift in range(1, NX):
            moments.append(
                sent(
                    xm.at[step, kx],
                    xm.at[step, kx],
                    xms_sem.at[step, shift],
                    xmr_sem.at[step, shift],
                    "gx",
                    around(kx, shift, NX),
                )
            )
            moments[-1].start()
        leaving.extend(moments)
        for copy in moments:
            copy.wait_recv()
        below = jnp.zeros((8, CY), F32)
        above = jnp.zeros((8, CY), F32)
        for m in range(NX):
            plus, minus = xm[step, m, 0:8, :], xm[step, m, 8:16, :]
            below = below + xw[m, 0] * plus + xw[m, 1] * minus
            above = above + xw[m, 2] * plus + xw[m, 3] * minus

        ends = jnp.zeros((CX, CY), F32)
        for z in range(CZ):
            f = first[z] + lp[z] * below[z : z + 1] + ln[z] * above[z : z + 1]
            hi, lo = halves(f)
            r = dot(jnp.concatenate([hi, lo], axis=1), y1[z]) + dot(hi, y2[z])
            work[z] = r[:, :CY]
            ends = ends + r[:, CY:]
        ym[step, ky] = jnp.transpose(ends)[:16]
        moments = []
        for shift in range(1, NY):
            moments.append(
                sent(
                    ym.at[step, ky],
                    ym.at[step, ky],
                    yms_sem.at[step, shift],
                    ymr_sem.at[step, shift],
                    "gy",
                    around(ky, shift, NY),
                )
            )
            moments[-1].start()
        leaving.extend(moments)
        for copy in moments:
            copy.wait_recv()
        below = [jnp.zeros((8, 128), F32) for _ in range(2)]
        above = [jnp.zeros((8, 128), F32) for _ in range(2)]
        for m in range(NY):
            for h in range(2):
                cols = slice(128 * h, 128 * (h + 1))
                plus, minus = ym[step, m, 0:8, cols], ym[step, m, 8:16, cols]
                below[h] = below[h] + yw[m, 0] * plus + yw[m, 1] * minus
                above[h] = above[h] + yw[m, 2] * plus + yw[m, 3] * minus
        for h in range(2):
            cols = slice(128 * h, 128 * (h + 1))
            turn[0:8, cols] = below[h]
            turn[8:16, cols] = above[h]
        columns = jnp.transpose(turn[...])
        base = CZ * kz + 1

        def upward(c):
            return sent(
                sup.at[step, pl.ds(CH * c, CH), :],
                zup.at[step, pl.ds(CH * c, CH), :],
                ups_sem.at[step, c],
                upr_sem.at[step, c],
                "gz",
                around(kz, 1, NZ),
            )

        def downward(c):
            return sent(
                sdown.at[step, pl.ds(CH * c, CH), :],
                zdown.at[step, pl.ds(CH * c, CH), :],
                dns_sem.at[step, c],
                dnr_sem.at[step, c],
                "gz",
                around(kz, -1, NZ),
            )

        for c in range(NCH):
            rows = slice(CH * c, CH * (c + 1))
            w = jnp.zeros((CH, CY), F32)
            v = jnp.zeros((CH, CY), F32)
            for z in range(CZ):
                value = (
                    work[z, rows, :]
                    + columns[rows, z : z + 1] * rowp[0, z : z + 1, :]
                    + columns[rows, z + 8 : z + 9] * rown[0, z : z + 1, :]
                )
                work[z, rows, :] = value
                w = w + pq[1, base + z, 0:1, :] * value
                v = v + pq[0, base + z, 0:1, :] * value
            sup[step, rows, :] = w
            sdown[step, rows, :] = v

            @pl.when(kz == 0)
            def _():
                upward(c).start()
                zup[step, rows, :] = jnp.zeros((CH, CY), F32)

            @pl.when(kz == NZ - 1)
            def _():
                downward(c).start()
                zdown[step, rows, :] = jnp.zeros((CH, CY), F32)

        def relay_up():
            for c in range(NCH):
                rows = slice(CH * c, CH * (c + 1))
                up = upward(c)
                up.wait_recv()

                @pl.when(kz < NZ - 1)
                def _():
                    sup[step, rows, :] = sup[step, rows, :] + zup[step, rows, :]
                    up.start()

        def relay_down():
            for c in range(NCH):
                rows = slice(CH * c, CH * (c + 1))
                down = downward(c)
                down.wait_recv()

                @pl.when(kz > 0)
                def _():
                    sdown[step, rows, :] = sdown[step, rows, :] + zdown[step, rows, :]
                    down.start()

        @pl.when(kz == 0)
        def _():
            relay_down()

        @pl.when(kz == 1)
        def _():
            relay_up()
            relay_down()

        @pl.when(kz == 2)
        def _():
            relay_down()
            relay_up()

        @pl.when(kz == NZ - 1)
        def _():
            relay_up()

        last = step == STEPS - 1
        for c in range(NCH):
            rows = slice(CH * c, CH * (c + 1))
            padded = slice(PAD + CH * c, PAD + CH * (c + 1))
            lower, upper = zup[step, rows, :], zdown[step, rows, :]
            run = lower
            part = []
            for z in range(CZ):
                run = run + pq[1, base + z, 0:1, :] * work[z, rows, :]
                third[z, rows, :] = pq[0, base + z, 0:1, :] * run
            if not last:
                top = base + CZ
                upad[CZ + 1, padded, :] = (
                    upad[CZ + 1, padded, :]
                    + pq[0, top, 0:1, :] * run
                    + pq[1, top, 0:1, :] * upper
                )
            run = upper
            for z in range(CZ - 1, -1, -1):
                u = (
                    upad[z + 1, padded, :]
                    + third[z, rows, :]
                    + pq[1, base + z, 0:1, :] * run
                )
                run = run + pq[0, base + z, 0:1, :] * work[z, rows, :]
                if last:
                    warm_ref[z, rows, :] = u
                    ohmic_ref[z, rows, :] = (1.0 + WARMING_SLOPE * u) * joule_ref[z, rows, :]
                else:
                    upad[z + 1, padded, :] = u
            if not last:
                upad[0, padded, :] = (
                    upad[0, padded, :]
                    + pq[0, base - 1, 0:1, :] * lower
                    + pq[1, base - 1, 0:1, :] * run
                )
        if not last:
            edge_rows(step + 1, 0, upad)
            edges_at = len(leaving)
            edges_out(step + 1)

        for c in range(NCH):

            @pl.when(kz < NZ - 1)
            def _():
                upward(c).wait_send()

            @pl.when(kz > 0)
            def _():
                downward(c).wait_send()

    for copy in leaving:
        copy.wait_send()


def stepped(sheet, cond, scaling, u, kind, joule):
    block = jax.ShapeDtypeStruct((CZ, CX, CY), F32)
    smem = pl.BlockSpec(memory_space=pltpu.SMEM)
    vmem = pl.BlockSpec(memory_space=pltpu.VMEM)
    dma = pltpu.SemaphoreType.DMA
    tall = pltpu.VMEM((CZ, CX, CY), F32)
    return pl.pallas_call(
        adi_kernel,
        out_shape=(block, block),
        in_specs=[smem] * 3 + [vmem] * 3,
        out_specs=(vmem, vmem),
        scratch_shapes=[
            pltpu.VMEM((CZ + 2, WIDE, CY), F32),
            pltpu.VMEM((CZ + 2, WIDE, CY), F32),
            tall,
            tall,
            tall,
            tall,
            pltpu.VMEM((CZ + 1, CX, CY), F32),
            tall,
            pltpu.VMEM((CZ, CX + 16, CX), BF16),
            pltpu.VMEM((CZ, CX + 16, CX), BF16),
            pltpu.VMEM((CZ, 2 * CY, 2 * CY), BF16),
            pltpu.VMEM((CZ, CY, 2 * CY), BF16),
            tall,
            tall,
            pltpu.VMEM((2, 8, 128), F32),
            pltpu.VMEM((2, 8, 128), F32),
            pltpu.VMEM((5, 8, 128), F32),
            pltpu.VMEM((NX, 4, 8, 128), F32),
            pltpu.VMEM((NY, 4, 8, 128), F32),
            pltpu.VMEM((2, PLANES + 2, 8, 128), F32),
            tall,
            tall,
            tall,
            pltpu.VMEM((CY, CX), F32),
            pltpu.VMEM((STEPS, 2, 16, CY), F32),
            pltpu.VMEM((STEPS, 2, 16, CY), F32),
            pltpu.VMEM((STEPS, 32, CX), F32),
            pltpu.VMEM((STEPS, 2, 32, CX), F32),
            pltpu.VMEM((STEPS, NX, 16, CY), F32),
            pltpu.VMEM((STEPS, NY, 16, CX), F32),
            pltpu.VMEM((STEPS, CX, CY), F32),
            pltpu.VMEM((STEPS, CX, CY), F32),
            pltpu.VMEM((STEPS, CX, CY), F32),
            pltpu.VMEM((STEPS, CX, CY), F32),
            dma((STEPS, 2)),
            dma((STEPS, 2)),
            dma((STEPS, 2)),
            dma((STEPS, 2)),
            dma((4,)),
            dma((4,)),
            dma((STEPS, NX)),
            dma((STEPS, NX)),
            dma((STEPS, NY)),
            dma((STEPS, NY)),
            dma((STEPS, NCH)),
            dma((STEPS, NCH)),
            dma((STEPS, NCH)),
            dma((STEPS, NCH)),
        ],
        compiler_params=pltpu.CompilerParams(
            collective_id=0, has_side_effects=True, vmem_limit_bytes=VMEM_BYTES
        ),
        name="steps",
    )(sheet, cond, scaling, u, kind, joule)


def per_device(
    starting_warmth,
    sheet_stratum_number,
    stratum_heat_conduction,
    substance_kind,
    substance_kind_scaling,
    wire_piece_amperes,
    wire_piece_ohms_base,
    wire_piece_tile,
    wire_piece_voxel,
):
    shape = (SEGS // 256, 256)
    sent = packed(
        wire_piece_amperes.reshape(shape),
        wire_piece_ohms_base.reshape(shape),
        wire_piece_tile.reshape(shape),
        wire_piece_voxel.reshape(shape),
    )
    got = lax.all_to_all(sent, ("gx", "gy", "gz"), split_axis=0, concat_axis=0, tiled=True)
    rows = (got[:, TOP:].astype(jnp.int32) >> 7).reshape(-1)
    joule = added(rows, got).reshape(CZ, CX, CY)
    return stepped(
        sheet_stratum_number,
        stratum_heat_conduction,
        substance_kind_scaling,
        starting_warmth,
        substance_kind,
        joule,
    )


def solution(mesh):
    return jax.shard_map(
        per_device,
        mesh=mesh,
        in_specs=(
            P("gz", "gx", "gy"),
            P(),
            P(),
            P("gz", "gx", "gy"),
            P(),
            P(("gx", "gy", "gz")),
            P(("gx", "gy", "gz")),
            P(("gx", "gy", "gz"), None),
            P(("gx", "gy", "gz")),
        ),
        out_specs=(P("gz", "gx", "gy"), P("gz", "gx", "gy")),
        check_vma=False,
    )
```

```python
import functools

import jax
import jax.numpy as jnp
from jax import lax
from jax.experimental import pallas as pl
from jax.experimental.pallas import tpu as pltpu
from jax.sharding import PartitionSpec as P

STEPS = 2
HEAT_SPREADING = 1000.0
STIFF = 1.5
WARMING_SLOPE = 0.1
OHMIC_POWER = 8.0

F32 = jnp.float32
BF16 = jnp.bfloat16
MESH = pl.DeviceIdType.MESH

CZ, CX, CY = 8, 256, 128
LEN = 1024
PLANES = 32
NX, NY, NZ = 4, 8, 4
SEGS = 4096
TOP = 64
DEVS = 128
PAD = 8
WIDE = CX + 2 * PAD
NCH = 4
CH = CX // NCH
NACC = 8
VMEM_BYTES = 60 * 1024 * 1024


def dot(a, b):
    return jnp.dot(a, b, preferred_element_type=F32)


def halves(x):
    high = x.astype(BF16)
    return high, (x - high.astype(F32)).astype(BF16)


def place_segments(amp_ref, ohm_ref, tile_ref, cell_ref, acc):
    width = 256
    row = lax.broadcasted_iota(jnp.int32, (width, width + DEVS), 0)
    col = lax.broadcasted_iota(jnp.int32, (width, width + DEVS), 1)
    before = jnp.where((row < col) | (col >= width), 1.0, 0.0).astype(BF16)
    owner = lax.broadcasted_iota(jnp.int32, (DEVS, width), 0)
    place = lax.broadcasted_iota(jnp.int32, (TOP, width), 0).astype(F32)
    acc[...] = jnp.zeros_like(acc)
    carry = jnp.zeros((DEVS, DEVS), F32)

    def line(ref, j):
        return jnp.concatenate([ref[2 * j : 2 * j + 1, :], ref[2 * j + 1 : 2 * j + 2, :]], axis=1)

    for j in range(SEGS // width):
        tile = tile_ref[:, width * j : width * (j + 1)]
        tile = ((tile & 3) << 5) + ((tile >> 5) << 3) + ((tile >> 2) & 7)
        mine = owner == tile
        hot = jnp.where(mine, 1.0, 0.0).astype(BF16)
        found = dot(hot, before)
        ahead = found[:, :width] + jnp.concatenate([carry, carry], axis=1)
        rank = jnp.sum(jnp.where(mine, ahead, 0.0), axis=0, keepdims=True)
        carry = carry + found[:, width:]
        amp = line(amp_ref, j)
        power = amp * amp * line(ohm_ref, j)
        p0 = power.astype(BF16).astype(F32)
        p1 = (power - p0).astype(BF16).astype(F32)
        p2 = power - p0 - p1
        cell = line(cell_ref, j)
        c0 = (cell >> 12).astype(F32)
        c1 = ((cell >> 6) & 63).astype(F32)
        c2 = (cell & 63).astype(F32)
        here = place == rank
        parts = jnp.concatenate(
            [jnp.where(here, part, 0.0).astype(BF16) for part in (p0, c0, p1, c1, p2, c2)], axis=0
        )
        acc[...] += lax.dot_general(
            hot, parts, (((1,), (1,)), ((), ())), preferred_element_type=F32
        )
    a, b, c = (acc[:, 128 * k : 128 * (k + 1)] for k in range(3))
    lane = lax.broadcasted_iota(jnp.int32, (DEVS, DEVS), 1)
    return jnp.where(lane < TOP, a + b + c, a * 4096.0 + b * 64.0 + c)


def around(me, shift, count):
    return lax.rem(me + shift + count, count)


def sent(src, dst, send, recv, axis, to):
    return pltpu.make_async_remote_copy(
        src_ref=src,
        dst_ref=dst,
        send_sem=send,
        recv_sem=recv,
        device_id={axis: to},
        device_id_type=MESH,
    )


def greet(places):
    barrier = pltpu.get_barrier_semaphore()
    for axis, me, count in places:
        for shift in range(1, count):
            pl.semaphore_signal(
                barrier, inc=1, device_id={axis: around(me, shift, count)}, device_id_type=MESH
            )
    return barrier


def cell_conductance(cond_ref, sheet_ref, scale_ref, kind, plane):
    factor = jnp.where(kind == 0, scale_ref[0], 0.0)
    for category in range(1, 4):
        factor = jnp.where(kind == category, scale_ref[category], factor)
    return factor * cond_ref[sheet_ref[plane]]


def edge_columns(planes):
    lane = lax.broadcasted_iota(jnp.int32, (CX, CY), 1)
    out = jnp.zeros((CX, CY), F32)
    for z, plane in enumerate(planes):
        out = jnp.where((lane >> 1) == z, pltpu.roll(plane, 2 * z + 1, 1), out)
    return jnp.transpose(out)[:16]


def spread_kernel(
    sheet_ref,
    cond_ref,
    scale_ref,
    amp_ref,
    ohm_ref,
    tile_ref,
    cell_ref,
    u_hbm,
    kind_hbm,
    power_ref,
    column_ref,
    row_ref,
    zr,
    xr,
    yr,
    u,
    kind,
    c,
    acc,
    one,
    two,
    three,
    four,
    five,
    zs,
    xs,
    ys,
    load_sem,
    one_send,
    one_recv,
    two_send,
    two_recv,
    three_send,
    three_recv,
    zs_sem,
    zr_sem,
    xs_sem,
    xr_sem,
    ys_sem,
    yr_sem,
):
    kx, ky, kz = lax.axis_index("gx"), lax.axis_index("gy"), lax.axis_index("gz")
    barrier = greet((("gx", kx, NX), ("gy", ky, NY), ("gz", kz, NZ)))
    loads = [
        pltpu.make_async_copy(u_hbm, u, load_sem.at[0]),
        pltpu.make_async_copy(kind_hbm, kind, load_sem.at[1]),
    ]
    for copy in loads:
        copy.start()
    one[...] = place_segments(amp_ref, ohm_ref, tile_ref, cell_ref, acc).reshape(
        NZ, NX, NY, DEVS
    )
    pl.semaphore_wait(barrier, NX + NY + NZ - 3)
    leaving = []

    def exchange(source, target, send, recv, axis, me, count):
        copies = []
        for shift in range(1, count):
            to = around(me, shift, count)
            copies.append(
                sent(source(to), target.at[me], send.at[shift], recv.at[shift], axis, to)
            )
            copies[-1].start()
        leaving.extend(copies)
        return copies

    copies = exchange(lambda to: one.at[to], two, one_send, one_recv, "gz", kz, NZ)
    two[kz] = one[kz]

    for copy in loads:
        copy.wait()
    for z in range(CZ):
        c[z] = cell_conductance(cond_ref, sheet_ref, scale_ref, kind[z], CZ * kz + z)
    for part, ref in ((0, u), (1, c)):
        zs[part, 0] = ref[CZ - 1]
        zs[part, 1] = ref[0]
        for side, to in ((0, 1), (1, -1)):
            leaving.append(
                sent(
                    zs.at[part, side],
                    zr.at[part, side],
                    zs_sem.at[part, side],
                    zr_sem.at[part, side],
                    "gz",
                    around(kz, to, NZ),
                )
            )
            leaving[-1].start()
    for copy in copies:
        copy.wait_recv()
    copies = exchange(lambda to: two.at[:, to], three, two_send, two_recv, "gx", kx, NX)
    three[kx] = two[:, kx]
    for part, ref in ((0, u), (1, c)):
        xs[0, pl.ds(8 * part, 8), :] = ref[:, CX - 1, :]
        xs[1, pl.ds(8 * part, 8), :] = ref[:, 0, :]
        ys[pl.ds(16 * part, 16), :] = edge_columns([ref[z] for z in range(CZ)])
    for side, to in ((0, 1), (1, -1)):
        leaving.append(
            sent(
                xs.at[side],
                xr.at[side],
                xs_sem.at[side],
                xr_sem.at[side],
                "gx",
                around(kx, to, NX),
            )
        )
        leaving.append(
            sent(ys, yr.at[side], ys_sem.at[side], yr_sem.at[side], "gy", around(ky, to, NY))
        )
    for copy in leaving[-4:]:
        copy.start()
    edges = leaving[-4:]
    for copy in copies:
        copy.wait_recv()
    for to in range(NY):
        four[to] = three[:, :, to, :].reshape(NX * NZ, DEVS)
    copies = exchange(lambda to: four.at[to], five, three_send, three_recv, "gy", ky, NY)
    five[ky] = four[ky]
    for copy in copies:
        copy.wait_recv()
    got = five[...].reshape(DEVS, DEVS)
    turned = pltpu.roll(got, TOP, 1)
    lane = lax.broadcasted_iota(jnp.int32, (DEVS // 2, DEVS), 1)
    left = lane < TOP
    power_ref[...] = jnp.where(left, got[: DEVS // 2], turned[DEVS // 2 :])
    cells = jnp.where(left, turned[: DEVS // 2], got[DEVS // 2 :]).astype(jnp.int32)
    column_ref[...] = cells & 127
    row_ref[...] = cells >> 7
    for part in range(2):
        for side, to in ((0, 1), (1, -1)):
            sent(
                zs.at[part, side],
                zr.at[part, side],
                zs_sem.at[part, side],
                zr_sem.at[part, side],
                "gz",
                around(kz, to, NZ),
            ).wait_recv()
    for copy in edges:
        copy.wait_recv()
    for copy in leaving:
        copy.wait_send()


def spread_out(sheet, cond, scaling, amp, ohm, tile, cell, u, kind):
    smem = pl.BlockSpec(memory_space=pltpu.SMEM)
    vmem = pl.BlockSpec(memory_space=pltpu.VMEM)
    whole = pl.BlockSpec(memory_space=pl.ANY)
    dma = pltpu.SemaphoreType.DMA
    half = (DEVS // 2, DEVS)
    return pl.pallas_call(
        spread_kernel,
        out_shape=(
            jax.ShapeDtypeStruct(half, F32),
            jax.ShapeDtypeStruct(half, jnp.int32),
            jax.ShapeDtypeStruct(half, jnp.int32),
            jax.ShapeDtypeStruct((2, 2, CX, CY), F32),
            jax.ShapeDtypeStruct((2, 16, CY), F32),
            jax.ShapeDtypeStruct((2, 32, CX), F32),
        ),
        in_specs=[smem] * 3 + [vmem] * 4 + [whole] * 2,
        out_specs=(vmem,) * 6,
        scratch_shapes=[
            pltpu.VMEM((CZ, CX, CY), F32),
            pltpu.VMEM((CZ, CX, CY), jnp.int32),
            pltpu.VMEM((CZ, CX, CY), F32),
            pltpu.VMEM((DEVS, 384), F32),
            pltpu.VMEM((NZ, NX, NY, DEVS), F32),
            pltpu.VMEM((NZ, NX, NY, DEVS), F32),
            pltpu.VMEM((NX, NZ, NY, DEVS), F32),
            pltpu.VMEM((NY, NX * NZ, DEVS), F32),
            pltpu.VMEM((NY, NX * NZ, DEVS), F32),
            pltpu.VMEM((2, 2, CX, CY), F32),
            pltpu.VMEM((2, 16, CY), F32),
            pltpu.VMEM((32, CX), F32),
            dma((2,)),
            dma((NZ,)),
            dma((NZ,)),
            dma((NX,)),
            dma((NX,)),
            dma((NY,)),
            dma((NY,)),
            dma((2, 2)),
            dma((2, 2)),
            dma((2,)),
            dma((2,)),
            dma((2,)),
            dma((2,)),
        ],
        compiler_params=pltpu.CompilerParams(
            collective_id=1, has_side_effects=True, vmem_limit_bytes=VMEM_BYTES
        ),
        name="spread",
    )(sheet, cond, scaling, amp, ohm, tile, cell, u, kind)


def add_kernel(row_ref, power_ref, column_ref, out_ref, spread, *accs):
    for acc in accs:
        acc[...] = jnp.zeros_like(acc)
    sub = lax.broadcasted_iota(jnp.int32, (CY, 128), 0)
    for j in range(DEVS // 2):
        spread[128 * j : 128 * (j + 1), :] = jnp.transpose(
            jnp.where(sub == column_ref[j : j + 1, :], power_ref[j : j + 1, :], 0.0)
        )

    def some(i, carry):
        for k in range(128):
            acc = accs[k % NACC]
            acc[pl.ds(row_ref[i, k], 1), :] += spread[pl.ds(128 * i + k, 1), :]
        return carry

    lax.fori_loop(0, DEVS // 2, some, 0)
    total = accs[0][...]
    for acc in accs[1:]:
        total = total + acc[...]
    out_ref[...] = total


def added(rows, powers, columns):
    vmem = pl.BlockSpec(memory_space=pltpu.VMEM)
    return pl.pallas_call(
        add_kernel,
        out_shape=jax.ShapeDtypeStruct((CZ * CX, CY), F32),
        in_specs=[pl.BlockSpec(memory_space=pltpu.SMEM), vmem, vmem],
        out_specs=vmem,
        scratch_shapes=[pltpu.VMEM((DEVS * TOP, 128), F32)]
        + [pltpu.VMEM((CZ * CX, CY), F32)] * NACC,
        compiler_params=pltpu.CompilerParams(vmem_limit_bytes=VMEM_BYTES),
        name="add",
    )(rows, powers, columns)


def line_weights(theta, scale, me, count, length):
    whole = 2 * LEN
    out = []
    for m in range(count):

        def tile(exponent, keep):
            return jnp.where(keep, jnp.exp(-theta * exponent.astype(F32)) * scale, 0.0)

        lower, same = m < me, me == m
        gap = jnp.where(lower, me - m, m - me)
        near, far = length * (gap - 1) + 1, whole - length * gap - (length - 1)
        apart = jnp.logical_not(same)
        out.append(
            (
                tile(jnp.where(lower, near, far), apart),
                tile(length * (me + m) + 1, True),
                tile(whole - length * (me + m + 2) + 1, True),
                tile(jnp.where(lower, far, near), apart),
            )
        )
    return out


def adi_kernel(
    sheet_ref,
    cond_ref,
    scale_ref,
    u_ref,
    kind_ref,
    joule_ref,
    z_edge,
    x_edge,
    y_edge,
    rise_ref,
    upad,
    cpad,
    gxl,
    gxu,
    gyl,
    gyu,
    gz,
    gself,
    thi,
    tlo,
    y1,
    y2,
    lp,
    ln,
    rowp,
    rown,
    tables,
    xw,
    yw,
    pq,
    first,
    work,
    third,
    turn,
    xs,
    xr,
    ys,
    yr,
    xm,
    ym,
    zup,
    zdown,
    sup,
    sdown,
    xs_sem,
    xr_sem,
    ys_sem,
    yr_sem,
    xms_sem,
    xmr_sem,
    yms_sem,
    ymr_sem,
    ups_sem,
    upr_sem,
    dns_sem,
    dnr_sem,
):
    kx, ky, kz = lax.axis_index("gx"), lax.axis_index("gy"), lax.axis_index("gz")
    barrier = greet((("gx", kx, NX), ("gy", ky, NY), ("gz", kz, NZ)))
    sub8 = lax.broadcasted_iota(jnp.int32, (8, 128), 0)
    lane8 = lax.broadcasted_iota(jnp.int32, (8, 128), 1)
    lane = lax.broadcasted_iota(jnp.int32, (CX, CY), 1)
    leaving = []

    inner = pl.ds(PAD, CX)
    for z in range(CZ):
        cpad[z + 1, inner, :] = cell_conductance(
            cond_ref, sheet_ref, scale_ref, kind_ref[z], CZ * kz + z
        )
        upad[z + 1, inner, :] = u_ref[z]
    for ref, part in ((upad, 0), (cpad, 1)):
        ref[0, inner, :] = z_edge[part, 0]
        ref[CZ + 1, inner, :] = z_edge[part, 1]

    def edges_out():
        xs[0] = upad[1 : CZ + 1, PAD + CX - 1, :]
        xs[1] = upad[1 : CZ + 1, PAD, :]
        ys[...] = edge_columns([upad[z + 1, inner, :] for z in range(CZ)])
        copies = []
        for side, to in ((0, 1), (1, -1)):
            copies.append(
                sent(
                    xs.at[side],
                    xr.at[side],
                    xs_sem.at[side],
                    xr_sem.at[side],
                    "gx",
                    around(kx, to, NX),
                )
            )
            copies.append(
                sent(
                    ys, yr.at[side], ys_sem.at[side], yr_sem.at[side], "gy", around(ky, to, NY)
                )
            )
        for copy in copies:
            copy.start()
        leaving.extend(copies)
        return copies

    own = jnp.zeros((8, 128), F32)
    for z in range(CZ):
        own = jnp.where(sub8 == z, cond_ref[sheet_ref[CZ * kz + z]], own)
    a = HEAT_SPREADING * STIFF * own
    s = 0.5 * lax.rsqrt(a)
    s = 0.5 * (s + 0.25 / (a * s))
    s2 = s * s
    theta = 2.0 * s * (1.0 - s2 * (1.0 / 6.0 - s2 * (3.0 / 40.0 - s2 * (15.0 / 336.0))))
    whole = jnp.exp(-theta * (2.0 * LEN))
    root = jnp.sqrt(a + 0.25)
    scale = 0.5 / (root * (1.0 - whole))
    tables[0] = theta
    tables[1] = scale
    tables[2] = scale * whole
    tables[3] = jnp.exp(-theta * (CX - 1.0))
    tables[4] = jnp.exp(-theta * (CY - 1.0))
    last_x, last_y = tables[3], tables[4]
    for h in range(2):
        at = (lane8 + 128 * h).astype(F32)
        rowp[h] = jnp.exp(-theta * at)
        rown[h] = jnp.exp(theta * at)
    for m, tiles in enumerate(line_weights(theta, scale, kx, NX, CX)):
        for k, tile in enumerate(tiles):
            xw[m, k] = tile if k < 2 else tile * last_x
    for m, tiles in enumerate(line_weights(theta, scale, ky, NY, CY)):
        for k, tile in enumerate(tiles):
            yw[m, k] = tile if k < 2 else tile * last_y

    conds = [jnp.full((8, 128), cond_ref[sheet_ref[z]], F32) for z in range(PLANES)]
    stiff = HEAT_SPREADING * STIFF
    links = [0.5 * stiff * (conds[z] + conds[z + 1]) for z in range(PLANES - 1)]
    up = [1.0 + stiff * conds[0]]
    grow = [jnp.ones((8, 128), F32)]
    for z in range(PLANES - 1):
        grow.append(grow[z] * (1.0 + up[z] / links[z]))
        up.append(1.0 + links[z] * (up[z] / (up[z] + links[z])))
    down = [None] * PLANES
    down[-1] = jnp.ones((8, 128), F32)
    for z in range(PLANES - 2, -1, -1):
        down[z] = 1.0 + links[z] * (down[z + 1] / (down[z + 1] + links[z]))
    nothing = jnp.zeros((8, 128), F32)
    pq[0, 0] = nothing
    pq[1, 0] = nothing
    pq[0, PLANES + 1] = nothing
    pq[1, PLANES + 1] = nothing
    for z in range(PLANES):
        pq[0, z + 1] = 1.0 / ((up[z] + down[z] - 1.0) * grow[z])
        pq[1, z + 1] = grow[z]

    row = lax.broadcasted_iota(jnp.int32, (CX, CY), 0).astype(F32)
    sub16 = lax.broadcasted_iota(jnp.int32, (16, 128), 0)
    lane_y = lax.broadcasted_iota(jnp.int32, (CY, CY), 1)

    def weights(z, carry):
        one = pl.ds(z, 1)
        th = tables[0, one, :]
        fall = jnp.exp(-th * row)
        rise = jnp.exp(th * row)
        lp[z] = fall
        ln[z] = rise
        c1, c2 = tables[1, one, :], tables[2, one, :]
        for h in range(2):
            x, y = fall * rown[h, one, :], rise * rowp[h, one, :]
            t = c1 * jnp.minimum(x, y) + c2 * jnp.maximum(x, y)
            cols = pl.ds(128 * h, 128)
            ends = jnp.where(
                sub16 == 0,
                tables[3, one, :] * rown[h, one, :],
                jnp.where(sub16 == 1, rowp[h, one, :], 0.0),
            )
            hi, lo = halves(t)
            thi[z, :CX, cols] = hi
            tlo[z, :CX, cols] = lo
            if h == 0:
                y1[z, :CY, :CY] = hi[:CY]
                y1[z, CY:, :CY] = hi[:CY]
                y2[z, :, :CY] = lo[:CY]
            hi, lo = halves(ends)
            thi[z, CX:, cols] = hi
            tlo[z, CX:, cols] = lo
        w = jnp.where(
            lane_y == z,
            rise[:CY] * tables[4, one, :],
            jnp.where(lane_y == z + 8, fall[:CY], 0.0),
        )
        hi, lo = halves(w)
        y1[z, :CY, CY:] = hi
        y1[z, CY:, CY:] = hi
        y2[z, :, CY:] = lo
        return carry

    lax.fori_loop(0, CZ, weights, 0)
    turn[...] = jnp.zeros_like(turn)

    def y_edges(low, high):
        odd = (lax.broadcasted_iota(jnp.int32, (16, CX), 0) & 1) == 1
        turn[:16, :] = jnp.where(odd, pltpu.roll(low, 1, 0), pltpu.roll(high, 15, 0))
        return jnp.transpose(turn[...])

    half = 0.5 * HEAT_SPREADING
    cpad[1 : CZ + 1, PAD - 1, :] = jnp.where(
        kx == 0, -cpad[1 : CZ + 1, PAD, :], x_edge[0, 8:16, :]
    )
    cpad[1 : CZ + 1, PAD + CX, :] = jnp.where(
        kx == NX - 1, -cpad[1 : CZ + 1, PAD + CX - 1, :], x_edge[1, 8:16, :]
    )
    work[0] = y_edges(y_edge[0, 16:32, :], y_edge[1, 16:32, :])
    gz[0] = jnp.where(kz == 0, 0.0, half * (cpad[0, inner, :] + cpad[1, inner, :]))
    gz[CZ] = jnp.where(
        kz == NZ - 1, 0.0, half * (cpad[CZ, inner, :] + cpad[CZ + 1, inner, :])
    )
    for z in range(CZ - 1):
        gz[z + 1] = half * (cpad[z + 1, inner, :] + cpad[z + 2, inner, :])
    for z in range(CZ):
        c = cpad[z + 1, inner, :]
        edge = pltpu.roll(work[0], CY - (2 * z + 1), 1)
        low = jnp.where(lane == 0, jnp.where(ky == 0, -c, edge), pltpu.roll(c, 1, 1))
        high = jnp.where(
            lane == CY - 1, jnp.where(ky == NY - 1, -c, edge), pltpu.roll(c, CY - 1, 1)
        )
        xl = half * (c + cpad[z + 1, PAD - 1 : PAD + CX - 1, :])
        xu = half * (c + cpad[z + 1, PAD + 1 : PAD + CX + 1, :])
        yl, yu = half * (c + low), half * (c + high)
        gxl[z], gxu[z], gyl[z], gyu[z] = xl, xu, yl, yu
        every = xl + xu + yl + yu + gz[z] + gz[z + 1]
        if z == 0:
            every = every + jnp.where(kz == 0, HEAT_SPREADING * c, 0.0)
        gself[z] = (OHMIC_POWER * WARMING_SLOPE) * joule_ref[z] - every

    for step in range(STEPS):
        if step:
            for copy in edges:
                copy.wait_recv()
            x_low, x_high, y_low, y_high = xr[0], xr[1], yr[0], yr[1]
        else:
            x_low, x_high = x_edge[0, 0:8, :], x_edge[1, 0:8, :]
            y_low, y_high = y_edge[0, 0:16, :], y_edge[1, 0:16, :]
        upad[1 : CZ + 1, PAD - 1, :] = x_low
        upad[1 : CZ + 1, PAD + CX, :] = x_high
        work[0] = y_edges(y_low, y_high)

        def source_and_x(z, carry):
            u = upad[z + 1, inner, :]
            edge = pltpu.roll(work[0], CY - (2 * z + 1), 1)
            low = jnp.where(lane == 0, edge, pltpu.roll(u, 1, 1))
            high = jnp.where(lane == CY - 1, edge, pltpu.roll(u, CY - 1, 1))
            b = gself[z] * u + OHMIC_POWER * joule_ref[z]
            b = b + gyl[z] * low + gyu[z] * high
            b = b + gxl[z] * upad[z + 1, PAD - 1 : PAD + CX - 1, :]
            b = b + gxu[z] * upad[z + 1, PAD + 1 : PAD + CX + 1, :]
            b = b + gz[z] * upad[z, inner, :] + gz[z + 1] * upad[z + 2, inner, :]
            hi, lo = halves(b)
            r = dot(thi[z], jnp.concatenate([hi, lo], axis=1))
            r = r[:, :CY] + r[:, CY:] + dot(tlo[z], hi)
            first[z] = r[:CX]
            xm[step, kx, pl.ds(z, 1), :] = r[CX : CX + 1]
            xm[step, kx, pl.ds(z + 8, 1), :] = r[CX + 1 : CX + 2]
            return carry

        for z in range(CZ):
            source_and_x(z, 0)

        if not step:
            pl.semaphore_wait(barrier, NX + NY + NZ - 3)
        moments = []
        for shift in range(1, NX):
            moments.append(
                sent(
                    xm.at[step, kx],
                    xm.at[step, kx],
                    xms_sem.at[step, shift],
                    xmr_sem.at[step, shift],
                    "gx",
                    around(kx, shift, NX),
                )
            )
            moments[-1].start()
        leaving.extend(moments)
        for copy in moments:
            copy.wait_recv()
        below = jnp.zeros((8, CY), F32)
        above = jnp.zeros((8, CY), F32)
        for m in range(NX):
            plus, minus = xm[step, m, 0:8, :], xm[step, m, 8:16, :]
            below = below + xw[m, 0] * plus + xw[m, 1] * minus
            above = above + xw[m, 2] * plus + xw[m, 3] * minus

        ends = jnp.zeros((CX, CY), F32)
        for z in range(CZ):
            f = first[z] + lp[z] * below[z : z + 1] + ln[z] * above[z : z + 1]
            hi, lo = halves(f)
            r = dot(jnp.concatenate([hi, lo], axis=1), y1[z]) + dot(hi, y2[z])
            work[z] = r[:, :CY]
            ends = ends + r[:, CY:]
        ym[step, ky] = jnp.transpose(ends)[:16]
        moments = []
        for shift in range(1, NY):
            moments.append(
                sent(
                    ym.at[step, ky],
                    ym.at[step, ky],
                    yms_sem.at[step, shift],
                    ymr_sem.at[step, shift],
                    "gy",
                    around(ky, shift, NY),
                )
            )
            moments[-1].start()
        leaving.extend(moments)
        for copy in moments:
            copy.wait_recv()
        below = [jnp.zeros((8, 128), F32) for _ in range(2)]
        above = [jnp.zeros((8, 128), F32) for _ in range(2)]
        for m in range(NY):
            for h in range(2):
                cols = slice(128 * h, 128 * (h + 1))
                plus, minus = ym[step, m, 0:8, cols], ym[step, m, 8:16, cols]
                below[h] = below[h] + yw[m, 0] * plus + yw[m, 1] * minus
                above[h] = above[h] + yw[m, 2] * plus + yw[m, 3] * minus
        for h in range(2):
            cols = slice(128 * h, 128 * (h + 1))
            turn[0:8, cols] = below[h]
            turn[8:16, cols] = above[h]
        columns = jnp.transpose(turn[...])
        base = CZ * kz + 1

        def upward(c):
            return sent(
                sup.at[step, pl.ds(CH * c, CH), :],
                zup.at[step, pl.ds(CH * c, CH), :],
                ups_sem.at[step, c],
                upr_sem.at[step, c],
                "gz",
                around(kz, 1, NZ),
            )

        def downward(c):
            return sent(
                sdown.at[step, pl.ds(CH * c, CH), :],
                zdown.at[step, pl.ds(CH * c, CH), :],
                dns_sem.at[step, c],
                dnr_sem.at[step, c],
                "gz",
                around(kz, -1, NZ),
            )

        for c in range(NCH):
            rows = slice(CH * c, CH * (c + 1))
            w = jnp.zeros((CH, CY), F32)
            v = jnp.zeros((CH, CY), F32)
            for z in range(CZ):
                value = (
                    work[z, rows, :]
                    + columns[rows, z : z + 1] * rowp[0, z : z + 1, :]
                    + columns[rows, z + 8 : z + 9] * rown[0, z : z + 1, :]
                )
                work[z, rows, :] = value
                w = w + pq[1, base + z, 0:1, :] * value
                v = v + pq[0, base + z, 0:1, :] * value
            sup[step, rows, :] = w
            sdown[step, rows, :] = v

            @pl.when(kz == 0)
            def _():
                upward(c).start()
                zup[step, rows, :] = jnp.zeros((CH, CY), F32)

            @pl.when(kz == NZ - 1)
            def _():
                downward(c).start()
                zdown[step, rows, :] = jnp.zeros((CH, CY), F32)

        def relay_up():
            for c in range(NCH):
                rows = slice(CH * c, CH * (c + 1))
                up = upward(c)
                up.wait_recv()

                @pl.when(kz < NZ - 1)
                def _():
                    sup[step, rows, :] = sup[step, rows, :] + zup[step, rows, :]
                    up.start()

        def relay_down():
            for c in range(NCH):
                rows = slice(CH * c, CH * (c + 1))
                down = downward(c)
                down.wait_recv()

                @pl.when(kz > 0)
                def _():
                    sdown[step, rows, :] = sdown[step, rows, :] + zdown[step, rows, :]
                    down.start()

        @pl.when(kz == 0)
        def _():
            relay_down()

        @pl.when(kz == 1)
        def _():
            relay_up()
            relay_down()

        @pl.when(kz == 2)
        def _():
            relay_down()
            relay_up()

        @pl.when(kz == NZ - 1)
        def _():
            relay_up()

        last = step == STEPS - 1
        for c in range(NCH):
            rows = slice(CH * c, CH * (c + 1))
            padded = slice(PAD + CH * c, PAD + CH * (c + 1))
            lower, upper = zup[step, rows, :], zdown[step, rows, :]
            run = lower
            part = []
            for z in range(CZ):
                run = run + pq[1, base + z, 0:1, :] * work[z, rows, :]
                third[z, rows, :] = pq[0, base + z, 0:1, :] * run
            if not last:
                top = base + CZ
                upad[CZ + 1, padded, :] = (
                    upad[CZ + 1, padded, :]
                    + pq[0, top, 0:1, :] * run
                    + pq[1, top, 0:1, :] * upper
                )
            run = upper
            for z in range(CZ - 1, -1, -1):
                u = (
                    upad[z + 1, padded, :]
                    + third[z, rows, :]
                    + pq[1, base + z, 0:1, :] * run
                )
                run = run + pq[0, base + z, 0:1, :] * work[z, rows, :]
                if last:
                    rise_ref[z, rows, :] = u - u_ref[z, rows, :]
                else:
                    upad[z + 1, padded, :] = u
            if not last:
                upad[0, padded, :] = (
                    upad[0, padded, :]
                    + pq[0, base - 1, 0:1, :] * lower
                    + pq[1, base - 1, 0:1, :] * run
                )
        if not last:
            edges = edges_out()

        for c in range(NCH):

            @pl.when(kz < NZ - 1)
            def _():
                upward(c).wait_send()

            @pl.when(kz > 0)
            def _():
                downward(c).wait_send()

    for copy in leaving:
        copy.wait_send()


def stepped(sheet, cond, scaling, u, kind, joule, z_edge, x_edge, y_edge):
    block = jax.ShapeDtypeStruct((CZ, CX, CY), F32)
    smem = pl.BlockSpec(memory_space=pltpu.SMEM)
    vmem = pl.BlockSpec(memory_space=pltpu.VMEM)
    dma = pltpu.SemaphoreType.DMA
    tall = pltpu.VMEM((CZ, CX, CY), F32)
    return pl.pallas_call(
        adi_kernel,
        out_shape=block,
        in_specs=[smem] * 3 + [vmem] * 6,
        out_specs=vmem,
        scratch_shapes=[
            pltpu.VMEM((CZ + 2, WIDE, CY), F32),
            pltpu.VMEM((CZ + 2, WIDE, CY), F32),
            tall,
            tall,
            tall,
            tall,
            pltpu.VMEM((CZ + 1, CX, CY), F32),
            tall,
            pltpu.VMEM((CZ, CX + 16, CX), BF16),
            pltpu.VMEM((CZ, CX + 16, CX), BF16),
            pltpu.VMEM((CZ, 2 * CY, 2 * CY), BF16),
            pltpu.VMEM((CZ, CY, 2 * CY), BF16),
            tall,
            tall,
            pltpu.VMEM((2, 8, 128), F32),
            pltpu.VMEM((2, 8, 128), F32),
            pltpu.VMEM((5, 8, 128), F32),
            pltpu.VMEM((NX, 4, 8, 128), F32),
            pltpu.VMEM((NY, 4, 8, 128), F32),
            pltpu.VMEM((2, PLANES + 2, 8, 128), F32),
            tall,
            tall,
            tall,
            pltpu.VMEM((CY, CX), F32),
            pltpu.VMEM((2, 8, CY), F32),
            pltpu.VMEM((2, 8, CY), F32),
            pltpu.VMEM((16, CX), F32),
            pltpu.VMEM((2, 16, CX), F32),
            pltpu.VMEM((STEPS, NX, 16, CY), F32),
            pltpu.VMEM((STEPS, NY, 16, CX), F32),
            pltpu.VMEM((STEPS, CX, CY), F32),
            pltpu.VMEM((STEPS, CX, CY), F32),
            pltpu.VMEM((STEPS, CX, CY), F32),
            pltpu.VMEM((STEPS, CX, CY), F32),
            dma((2,)),
            dma((2,)),
            dma((2,)),
            dma((2,)),
            dma((STEPS, NX)),
            dma((STEPS, NX)),
            dma((STEPS, NY)),
            dma((STEPS, NY)),
            dma((STEPS, NCH)),
            dma((STEPS, NCH)),
            dma((STEPS, NCH)),
            dma((STEPS, NCH)),
        ],
        compiler_params=pltpu.CompilerParams(
            collective_id=0, has_side_effects=True, vmem_limit_bytes=VMEM_BYTES
        ),
        name="steps",
    )(sheet, cond, scaling, u, kind, joule, z_edge, x_edge, y_edge)


def per_device(
    starting_warmth,
    sheet_stratum_number,
    stratum_heat_conduction,
    substance_kind,
    substance_kind_scaling,
    wire_piece_amperes,
    wire_piece_ohms_base,
    wire_piece_tile,
    wire_piece_voxel,
):
    shape = (SEGS // 128, 128)
    small = (sheet_stratum_number, stratum_heat_conduction, substance_kind_scaling)
    powers, columns, rows, *edges = spread_out(
        *small,
        wire_piece_amperes.reshape(shape),
        wire_piece_ohms_base.reshape(shape),
        wire_piece_tile.T,
        wire_piece_voxel.reshape(shape),
        starting_warmth,
        substance_kind,
    )
    joule = added(rows, powers, columns).reshape(CZ, CX, CY)
    rise = stepped(*small, starting_warmth, substance_kind, joule, *edges)
    warmed = starting_warmth + rise
    return warmed, (1.0 + WARMING_SLOPE * warmed) * joule


def solution(mesh):
    return jax.shard_map(
        per_device,
        mesh=mesh,
        in_specs=(
            P("gz", "gx", "gy"),
            P(),
            P(),
            P("gz", "gx", "gy"),
            P(),
            P(("gx", "gy", "gz")),
            P(("gx", "gy", "gz")),
            P(("gx", "gy", "gz"), None),
            P(("gx", "gy", "gz")),
        ),
        out_specs=(P("gz", "gx", "gy"), P("gz", "gx", "gy")),
        check_vma=False,
    )
```

```python
import functools

import jax
import jax.numpy as jnp
from jax import lax
from jax.experimental import pallas as pl
from jax.experimental.pallas import tpu as pltpu
from jax.sharding import PartitionSpec as P

STEPS = 2
HEAT_SPREADING = 1000.0
STIFF = 1.5
WARMING_SLOPE = 0.1
OHMIC_POWER = 8.0

F32 = jnp.float32
BF16 = jnp.bfloat16
MESH = pl.DeviceIdType.MESH

CZ, CX, CY = 8, 256, 128
LEN = 1024
PLANES = 32
NX, NY, NZ = 4, 8, 4
SEGS = 4096
TOP = 64
DEVS = 128
PAD = 8
WIDE = CX + 2 * PAD
NCH = 4
CH = CX // NCH
NACC = 8
VMEM_BYTES = 60 * 1024 * 1024


def dot(a, b):
    return jnp.dot(a, b, preferred_element_type=F32)


def halves(x):
    high = x.astype(BF16)
    return high, (x - high.astype(F32)).astype(BF16)


def place_segments(amp_ref, ohm_ref, tile_ref, cell_ref, acc):
    width = 256
    row = lax.broadcasted_iota(jnp.int32, (width, width + DEVS), 0)
    col = lax.broadcasted_iota(jnp.int32, (width, width + DEVS), 1)
    before = jnp.where((row < col) | (col >= width), 1.0, 0.0).astype(BF16)
    owner = lax.broadcasted_iota(jnp.int32, (DEVS, width), 0)
    place = lax.broadcasted_iota(jnp.int32, (TOP, width), 0).astype(F32)
    acc[...] = jnp.zeros_like(acc)
    carry = jnp.zeros((DEVS, DEVS), F32)

    def line(ref, j):
        return jnp.concatenate([ref[2 * j : 2 * j + 1, :], ref[2 * j + 1 : 2 * j + 2, :]], axis=1)

    for j in range(SEGS // width):
        tile = tile_ref[:, width * j : width * (j + 1)]
        tile = ((tile & 3) << 5) + ((tile >> 5) << 3) + ((tile >> 2) & 7)
        mine = owner == tile
        hot = jnp.where(mine, 1.0, 0.0).astype(BF16)
        found = dot(hot, before)
        ahead = found[:, :width] + jnp.concatenate([carry, carry], axis=1)
        rank = jnp.sum(jnp.where(mine, ahead, 0.0), axis=0, keepdims=True)
        carry = carry + found[:, width:]
        amp = line(amp_ref, j)
        power = amp * amp * line(ohm_ref, j)
        p0 = power.astype(BF16).astype(F32)
        p1 = (power - p0).astype(BF16).astype(F32)
        p2 = power - p0 - p1
        cell = line(cell_ref, j)
        c0 = (cell >> 12).astype(F32)
        c1 = ((cell >> 6) & 63).astype(F32)
        c2 = (cell & 63).astype(F32)
        here = place == rank
        parts = jnp.concatenate(
            [jnp.where(here, part, 0.0).astype(BF16) for part in (p0, c0, p1, c1, p2, c2)], axis=0
        )
        acc[...] += lax.dot_general(
            hot, parts, (((1,), (1,)), ((), ())), preferred_element_type=F32
        )
    a, b, c = (acc[:, 128 * k : 128 * (k + 1)] for k in range(3))
    lane = lax.broadcasted_iota(jnp.int32, (DEVS, DEVS), 1)
    return jnp.where(lane < TOP, a + b + c, a * 4096.0 + b * 64.0 + c)


def around(me, shift, count):
    return lax.rem(me + shift + count, count)


def sent(src, dst, send, recv, axis, to):
    return pltpu.make_async_remote_copy(
        src_ref=src,
        dst_ref=dst,
        send_sem=send,
        recv_sem=recv,
        device_id={axis: to},
        device_id_type=MESH,
    )


def greet(places):
    barrier = pltpu.get_barrier_semaphore()
    for axis, me, count in places:
        for shift in range(1, count):
            pl.semaphore_signal(
                barrier, inc=1, device_id={axis: around(me, shift, count)}, device_id_type=MESH
            )
    return barrier


def cell_conductance(cond_ref, sheet_ref, scale_ref, kind, plane):
    factor = jnp.where(kind == 0, scale_ref[0], 0.0)
    for category in range(1, 4):
        factor = jnp.where(kind == category, scale_ref[category], factor)
    return factor * cond_ref[sheet_ref[plane]]


def edge_columns(planes):
    lane = lax.broadcasted_iota(jnp.int32, (CX, CY), 1)
    out = jnp.zeros((CX, CY), F32)
    for z, plane in enumerate(planes):
        out = jnp.where((lane >> 1) == z, pltpu.roll(plane, 2 * z + 1, 1), out)
    return jnp.transpose(out)[:16]


def spread_kernel(
    sheet_ref,
    cond_ref,
    scale_ref,
    amp_ref,
    ohm_ref,
    tile_ref,
    cell_ref,
    u_hbm,
    kind_hbm,
    power_ref,
    column_ref,
    row_ref,
    zr,
    xr,
    yr,
    u,
    kind,
    c,
    acc,
    one,
    two,
    three,
    four,
    five,
    zs,
    xs,
    ys,
    load_sem,
    one_send,
    one_recv,
    two_send,
    two_recv,
    three_send,
    three_recv,
    zs_sem,
    zr_sem,
    xs_sem,
    xr_sem,
    ys_sem,
    yr_sem,
):
    kx, ky, kz = lax.axis_index("gx"), lax.axis_index("gy"), lax.axis_index("gz")
    barrier = greet((("gx", kx, NX), ("gy", ky, NY), ("gz", kz, NZ)))
    loads = [
        pltpu.make_async_copy(u_hbm, u, load_sem.at[0]),
        pltpu.make_async_copy(kind_hbm, kind, load_sem.at[1]),
    ]
    for copy in loads:
        copy.start()
    one[...] = place_segments(amp_ref, ohm_ref, tile_ref, cell_ref, acc).reshape(
        NZ, NX, NY, DEVS
    )
    pl.semaphore_wait(barrier, NX + NY + NZ - 3)
    leaving = []

    def exchange(source, target, send, recv, axis, me, count):
        copies = []
        for shift in range(1, count):
            to = around(me, shift, count)
            copies.append(
                sent(source(to), target.at[me], send.at[shift], recv.at[shift], axis, to)
            )
            copies[-1].start()
        leaving.extend(copies)
        return copies

    copies = exchange(lambda to: one.at[to], two, one_send, one_recv, "gz", kz, NZ)
    two[kz] = one[kz]

    for copy in loads:
        copy.wait()
    for z in range(CZ):
        c[z] = cell_conductance(cond_ref, sheet_ref, scale_ref, kind[z], CZ * kz + z)
    for part, ref in ((0, u), (1, c)):
        zs[part, 0] = ref[CZ - 1]
        zs[part, 1] = ref[0]
        for side, to in ((0, 1), (1, -1)):
            leaving.append(
                sent(
                    zs.at[part, side],
                    zr.at[part, side],
                    zs_sem.at[part, side],
                    zr_sem.at[part, side],
                    "gz",
                    around(kz, to, NZ),
                )
            )
            leaving[-1].start()
    for copy in copies:
        copy.wait_recv()
    copies = exchange(lambda to: two.at[:, to], three, two_send, two_recv, "gx", kx, NX)
    three[kx] = two[:, kx]
    for part, ref in ((0, u), (1, c)):
        xs[0, pl.ds(8 * part, 8), :] = ref[:, CX - 1, :]
        xs[1, pl.ds(8 * part, 8), :] = ref[:, 0, :]
        ys[pl.ds(16 * part, 16), :] = edge_columns([ref[z] for z in range(CZ)])
    for side, to in ((0, 1), (1, -1)):
        leaving.append(
            sent(
                xs.at[side],
                xr.at[side],
                xs_sem.at[side],
                xr_sem.at[side],
                "gx",
                around(kx, to, NX),
            )
        )
        leaving.append(
            sent(ys, yr.at[side], ys_sem.at[side], yr_sem.at[side], "gy", around(ky, to, NY))
        )
    for copy in leaving[-4:]:
        copy.start()
    edges = leaving[-4:]
    for copy in copies:
        copy.wait_recv()
    for to in range(NY):
        four[to] = three[:, :, to, :].reshape(NX * NZ, DEVS)
    copies = exchange(lambda to: four.at[to], five, three_send, three_recv, "gy", ky, NY)
    five[ky] = four[ky]
    for copy in copies:
        copy.wait_recv()
    got = five[...].reshape(DEVS, DEVS)
    turned = pltpu.roll(got, TOP, 1)
    lane = lax.broadcasted_iota(jnp.int32, (DEVS // 2, DEVS), 1)
    left = lane < TOP
    power_ref[...] = jnp.where(left, got[: DEVS // 2], turned[DEVS // 2 :])
    cells = jnp.where(left, turned[: DEVS // 2], got[DEVS // 2 :]).astype(jnp.int32)
    column_ref[...] = cells & 127
    row_ref[...] = cells >> 7
    for part in range(2):
        for side, to in ((0, 1), (1, -1)):
            sent(
                zs.at[part, side],
                zr.at[part, side],
                zs_sem.at[part, side],
                zr_sem.at[part, side],
                "gz",
                around(kz, to, NZ),
            ).wait_recv()
    for copy in edges:
        copy.wait_recv()
    for copy in leaving:
        copy.wait_send()


def spread_out(sheet, cond, scaling, amp, ohm, tile, cell, u, kind):
    smem = pl.BlockSpec(memory_space=pltpu.SMEM)
    vmem = pl.BlockSpec(memory_space=pltpu.VMEM)
    whole = pl.BlockSpec(memory_space=pl.ANY)
    dma = pltpu.SemaphoreType.DMA
    half = (DEVS // 2, DEVS)
    return pl.pallas_call(
        spread_kernel,
        out_shape=(
            jax.ShapeDtypeStruct(half, F32),
            jax.ShapeDtypeStruct(half, jnp.int32),
            jax.ShapeDtypeStruct(half, jnp.int32),
            jax.ShapeDtypeStruct((2, 2, CX, CY), F32),
            jax.ShapeDtypeStruct((2, 16, CY), F32),
            jax.ShapeDtypeStruct((2, 32, CX), F32),
        ),
        in_specs=[smem] * 3 + [vmem] * 4 + [whole] * 2,
        out_specs=(vmem,) * 6,
        scratch_shapes=[
            pltpu.VMEM((CZ, CX, CY), F32),
            pltpu.VMEM((CZ, CX, CY), jnp.int32),
            pltpu.VMEM((CZ, CX, CY), F32),
            pltpu.VMEM((DEVS, 384), F32),
            pltpu.VMEM((NZ, NX, NY, DEVS), F32),
            pltpu.VMEM((NZ, NX, NY, DEVS), F32),
            pltpu.VMEM((NX, NZ, NY, DEVS), F32),
            pltpu.VMEM((NY, NX * NZ, DEVS), F32),
            pltpu.VMEM((NY, NX * NZ, DEVS), F32),
            pltpu.VMEM((2, 2, CX, CY), F32),
            pltpu.VMEM((2, 16, CY), F32),
            pltpu.VMEM((32, CX), F32),
            dma((2,)),
            dma((NZ,)),
            dma((NZ,)),
            dma((NX,)),
            dma((NX,)),
            dma((NY,)),
            dma((NY,)),
            dma((2, 2)),
            dma((2, 2)),
            dma((2,)),
            dma((2,)),
            dma((2,)),
            dma((2,)),
        ],
        compiler_params=pltpu.CompilerParams(
            collective_id=1, has_side_effects=True, vmem_limit_bytes=VMEM_BYTES
        ),
        name="spread",
    )(sheet, cond, scaling, amp, ohm, tile, cell, u, kind)


def add_kernel(row_ref, power_ref, column_ref, out_ref, spread, *accs):
    for acc in accs:
        acc[...] = jnp.zeros_like(acc)
    sub = lax.broadcasted_iota(jnp.int32, (CY, 128), 0)
    for j in range(DEVS // 2):
        spread[128 * j : 128 * (j + 1), :] = jnp.transpose(
            jnp.where(sub == column_ref[j : j + 1, :], power_ref[j : j + 1, :], 0.0)
        )

    def some(i, carry):
        for k in range(128):
            acc = accs[k % NACC]
            acc[pl.ds(row_ref[i, k], 1), :] += spread[pl.ds(128 * i + k, 1), :]
        return carry

    lax.fori_loop(0, DEVS // 2, some, 0)
    total = accs[0][...]
    for acc in accs[1:]:
        total = total + acc[...]
    out_ref[...] = total


def added(rows, powers, columns):
    vmem = pl.BlockSpec(memory_space=pltpu.VMEM)
    return pl.pallas_call(
        add_kernel,
        out_shape=jax.ShapeDtypeStruct((CZ * CX, CY), F32),
        in_specs=[pl.BlockSpec(memory_space=pltpu.SMEM), vmem, vmem],
        out_specs=vmem,
        scratch_shapes=[pltpu.VMEM((DEVS * TOP, 128), F32)]
        + [pltpu.VMEM((CZ * CX, CY), F32)] * NACC,
        compiler_params=pltpu.CompilerParams(vmem_limit_bytes=VMEM_BYTES),
        name="add",
    )(rows, powers, columns)


def line_weights(theta, scale, me, count, length):
    whole = 2 * LEN
    out = []
    for m in range(count):

        def tile(exponent, keep):
            return jnp.where(keep, jnp.exp(-theta * exponent.astype(F32)) * scale, 0.0)

        lower, same = m < me, me == m
        gap = jnp.where(lower, me - m, m - me)
        near, far = length * (gap - 1) + 1, whole - length * gap - (length - 1)
        apart = jnp.logical_not(same)
        out.append(
            (
                tile(jnp.where(lower, near, far), apart),
                tile(length * (me + m) + 1, True),
                tile(whole - length * (me + m + 2) + 1, True),
                tile(jnp.where(lower, far, near), apart),
            )
        )
    return out


def adi_kernel(
    sheet_ref,
    cond_ref,
    scale_ref,
    u_ref,
    kind_ref,
    joule_ref,
    z_edge,
    x_edge,
    y_edge,
    rise_ref,
    upad,
    cpad,
    gxl,
    gxu,
    gyl,
    gyu,
    gz,
    gself,
    thi,
    tlo,
    y1,
    y2,
    lp,
    ln,
    rowp,
    rown,
    tables,
    xw,
    yw,
    pq,
    first,
    work,
    third,
    turn,
    mixed,
    rhs,
    coef,
    zm,
    xs,
    xr,
    ys,
    yr,
    xm,
    ym,
    zup,
    zdown,
    sup,
    sdown,
    xs_sem,
    xr_sem,
    ys_sem,
    yr_sem,
    xms_sem,
    xmr_sem,
    yms_sem,
    ymr_sem,
    zms_sem,
    zmr_sem,
    ups_sem,
    upr_sem,
    dns_sem,
    dnr_sem,
):
    kx, ky, kz = lax.axis_index("gx"), lax.axis_index("gy"), lax.axis_index("gz")
    barrier = greet((("gx", kx, NX), ("gy", ky, NY), ("gz", kz, NZ)))
    sub8 = lax.broadcasted_iota(jnp.int32, (8, 128), 0)
    lane8 = lax.broadcasted_iota(jnp.int32, (8, 128), 1)
    lane = lax.broadcasted_iota(jnp.int32, (CX, CY), 1)
    leaving = []

    inner = pl.ds(PAD, CX)
    for z in range(CZ):
        cpad[z + 1, inner, :] = cell_conductance(
            cond_ref, sheet_ref, scale_ref, kind_ref[z], CZ * kz + z
        )
        upad[z + 1, inner, :] = u_ref[z]
    for ref, part in ((upad, 0), (cpad, 1)):
        ref[0, inner, :] = z_edge[part, 0]
        ref[CZ + 1, inner, :] = z_edge[part, 1]

    def edges_out():
        xs[0] = upad[1 : CZ + 1, PAD + CX - 1, :]
        xs[1] = upad[1 : CZ + 1, PAD, :]
        ys[...] = edge_columns([upad[z + 1, inner, :] for z in range(CZ)])
        copies = []
        for side, to in ((0, 1), (1, -1)):
            copies.append(
                sent(
                    xs.at[side],
                    xr.at[side],
                    xs_sem.at[side],
                    xr_sem.at[side],
                    "gx",
                    around(kx, to, NX),
                )
            )
            copies.append(
                sent(
                    ys, yr.at[side], ys_sem.at[side], yr_sem.at[side], "gy", around(ky, to, NY)
                )
            )
        for copy in copies:
            copy.start()
        leaving.extend(copies)
        return copies

    own = jnp.zeros((8, 128), F32)
    for z in range(CZ):
        own = jnp.where(sub8 == z, cond_ref[sheet_ref[CZ * kz + z]], own)

    def decay(plane_cond):
        a = HEAT_SPREADING * STIFF * plane_cond
        s = 0.5 * lax.rsqrt(a)
        s = 0.5 * (s + 0.25 / (a * s))
        s2 = s * s
        return a, 2.0 * s * (
            1.0 - s2 * (1.0 / 6.0 - s2 * (3.0 / 40.0 - s2 * (15.0 / 336.0)))
        )

    a, theta = decay(own)
    whole = jnp.exp(-theta * (2.0 * LEN))
    root = jnp.sqrt(a + 0.25)
    scale = 0.5 / (root * (1.0 - whole))
    tables[0] = theta
    tables[1] = scale
    tables[2] = scale * whole
    tables[3] = jnp.exp(-theta * (CX - 1.0))
    tables[4] = jnp.exp(-theta * (CY - 1.0))
    last_x, last_y = tables[3], tables[4]
    for h in range(2):
        at = (lane8 + 128 * h).astype(F32)
        rowp[h] = jnp.exp(-theta * at)
        rown[h] = jnp.exp(theta * at)
    for m, tiles in enumerate(line_weights(theta, scale, kx, NX, CX)):
        for k, tile in enumerate(tiles):
            xw[m, k] = tile if k < 2 else tile * last_x
    for m, tiles in enumerate(line_weights(theta, scale, ky, NY, CY)):
        for k, tile in enumerate(tiles):
            yw[m, k] = tile if k < 2 else tile * last_y

    conds = [jnp.full((8, 128), cond_ref[sheet_ref[z]], F32) for z in range(PLANES)]
    stiff = HEAT_SPREADING * STIFF
    links = [0.5 * stiff * (conds[z] + conds[z + 1]) for z in range(PLANES - 1)]
    up = [1.0 + stiff * conds[0]]
    grow = [jnp.ones((8, 128), F32)]
    for z in range(PLANES - 1):
        grow.append(grow[z] * (1.0 + up[z] / links[z]))
        up.append(1.0 + links[z] * (up[z] / (up[z] + links[z])))
    down = [None] * PLANES
    down[-1] = jnp.ones((8, 128), F32)
    for z in range(PLANES - 2, -1, -1):
        down[z] = 1.0 + links[z] * (down[z + 1] / (down[z + 1] + links[z]))
    nothing = jnp.zeros((8, 128), F32)
    pq[0, 0] = nothing
    pq[1, 0] = nothing
    pq[0, PLANES + 1] = nothing
    pq[1, PLANES + 1] = nothing
    fade = [1.0 / ((up[z] + down[z] - 1.0) * grow[z]) for z in range(PLANES)]
    for z in range(PLANES):
        pq[0, z + 1] = fade[z]
        pq[1, z + 1] = grow[z]

    for m in range(NZ):
        cond, low, high = nothing, nothing, nothing
        for z in range(CZ):
            here = sub8 == z
            cond = jnp.where(here, conds[CZ * m + z], cond)
            low = jnp.where(here, grow[CZ * m + z], low)
            high = jnp.where(here, fade[CZ * m + z], high)
        _, th = decay(cond)
        low = jnp.where(m < kz, low, 0.0)
        high = jnp.where(m > kz, high, 0.0)
        for part in range(2):
            at = pl.ds(16 * m + 8 * part, 8)
            below_at = pl.ds(64 + 16 * m + 8 * part, 8)
            th = -th
            for h in range(2):
                wave = jnp.exp(th * (lane8 + 128 * h).astype(F32))
                mixed[at, pl.ds(128 * h, 128)] = wave
                if h == 0:
                    rhs[below_at, pl.ds(0, 128)] = low * wave
                    rhs[below_at, pl.ds(128, 128)] = high * wave
            coef[m, 0, pl.ds(8 * part, 8), :] = low
            coef[m, 1, pl.ds(8 * part, 8), :] = high

    row = lax.broadcasted_iota(jnp.int32, (CX, CY), 0).astype(F32)
    sub16 = lax.broadcasted_iota(jnp.int32, (16, 128), 0)
    lane_y = lax.broadcasted_iota(jnp.int32, (CY, CY), 1)

    def weights(z, carry):
        one = pl.ds(z, 1)
        th = tables[0, one, :]
        fall = jnp.exp(-th * row)
        rise = jnp.exp(th * row)
        lp[z] = fall
        ln[z] = rise
        c1, c2 = tables[1, one, :], tables[2, one, :]
        for h in range(2):
            x, y = fall * rown[h, one, :], rise * rowp[h, one, :]
            t = c1 * jnp.minimum(x, y) + c2 * jnp.maximum(x, y)
            cols = pl.ds(128 * h, 128)
            ends = jnp.where(
                sub16 == 0,
                tables[3, one, :] * rown[h, one, :],
                jnp.where(sub16 == 1, rowp[h, one, :], 0.0),
            )
            hi, lo = halves(t)
            thi[z, :CX, cols] = hi
            tlo[z, :CX, cols] = lo
            if h == 0:
                y1[z, :CY, :CY] = hi[:CY]
                y1[z, CY:, :CY] = hi[:CY]
                y2[z, :, :CY] = lo[:CY]
            hi, lo = halves(ends)
            thi[z, CX:, cols] = hi
            tlo[z, CX:, cols] = lo
        w = jnp.where(
            lane_y == z,
            rise[:CY] * tables[4, one, :],
            jnp.where(lane_y == z + 8, fall[:CY], 0.0),
        )
        hi, lo = halves(w)
        y1[z, :CY, CY:] = hi
        y1[z, CY:, CY:] = hi
        y2[z, :, CY:] = lo
        return carry

    lax.fori_loop(0, CZ, weights, 0)
    turn[...] = jnp.zeros_like(turn)

    def y_edges(low, high):
        odd = (lax.broadcasted_iota(jnp.int32, (16, CX), 0) & 1) == 1
        turn[:16, :] = jnp.where(odd, pltpu.roll(low, 1, 0), pltpu.roll(high, 15, 0))
        return jnp.transpose(turn[...])

    half = 0.5 * HEAT_SPREADING
    cpad[1 : CZ + 1, PAD - 1, :] = jnp.where(
        kx == 0, -cpad[1 : CZ + 1, PAD, :], x_edge[0, 8:16, :]
    )
    cpad[1 : CZ + 1, PAD + CX, :] = jnp.where(
        kx == NX - 1, -cpad[1 : CZ + 1, PAD + CX - 1, :], x_edge[1, 8:16, :]
    )
    work[0] = y_edges(y_edge[0, 16:32, :], y_edge[1, 16:32, :])
    gz[0] = jnp.where(kz == 0, 0.0, half * (cpad[0, inner, :] + cpad[1, inner, :]))
    gz[CZ] = jnp.where(
        kz == NZ - 1, 0.0, half * (cpad[CZ, inner, :] + cpad[CZ + 1, inner, :])
    )
    for z in range(CZ - 1):
        gz[z + 1] = half * (cpad[z + 1, inner, :] + cpad[z + 2, inner, :])
    for z in range(CZ):
        c = cpad[z + 1, inner, :]
        edge = pltpu.roll(work[0], CY - (2 * z + 1), 1)
        low = jnp.where(lane == 0, jnp.where(ky == 0, -c, edge), pltpu.roll(c, 1, 1))
        high = jnp.where(
            lane == CY - 1, jnp.where(ky == NY - 1, -c, edge), pltpu.roll(c, CY - 1, 1)
        )
        xl = half * (c + cpad[z + 1, PAD - 1 : PAD + CX - 1, :])
        xu = half * (c + cpad[z + 1, PAD + 1 : PAD + CX + 1, :])
        yl, yu = half * (c + low), half * (c + high)
        gxl[z], gxu[z], gyl[z], gyu[z] = xl, xu, yl, yu
        every = xl + xu + yl + yu + gz[z] + gz[z + 1]
        if z == 0:
            every = every + jnp.where(kz == 0, HEAT_SPREADING * c, 0.0)
        gself[z] = (OHMIC_POWER * WARMING_SLOPE) * joule_ref[z] - every

    for step in range(STEPS):
        if step:
            for copy in edges:
                copy.wait_recv()
            x_low, x_high, y_low, y_high = xr[0], xr[1], yr[0], yr[1]
        else:
            x_low, x_high = x_edge[0, 0:8, :], x_edge[1, 0:8, :]
            y_low, y_high = y_edge[0, 0:16, :], y_edge[1, 0:16, :]
        upad[1 : CZ + 1, PAD - 1, :] = x_low
        upad[1 : CZ + 1, PAD + CX, :] = x_high
        work[0] = y_edges(y_low, y_high)

        def source_and_x(z, carry):
            u = upad[z + 1, inner, :]
            edge = pltpu.roll(work[0], CY - (2 * z + 1), 1)
            low = jnp.where(lane == 0, edge, pltpu.roll(u, 1, 1))
            high = jnp.where(lane == CY - 1, edge, pltpu.roll(u, CY - 1, 1))
            b = gself[z] * u + OHMIC_POWER * joule_ref[z]
            b = b + gyl[z] * low + gyu[z] * high
            b = b + gxl[z] * upad[z + 1, PAD - 1 : PAD + CX - 1, :]
            b = b + gxu[z] * upad[z + 1, PAD + 1 : PAD + CX + 1, :]
            b = b + gz[z] * upad[z, inner, :] + gz[z + 1] * upad[z + 2, inner, :]
            hi, lo = halves(b)
            r = dot(thi[z], jnp.concatenate([hi, lo], axis=1))
            r = r[:, :CY] + r[:, CY:] + dot(tlo[z], hi)
            first[z] = r[:CX]
            xm[step, kx, pl.ds(z, 1), :] = r[CX : CX + 1]
            xm[step, kx, pl.ds(z + 8, 1), :] = r[CX + 1 : CX + 2]
            return carry

        for z in range(CZ):
            source_and_x(z, 0)

        if not step:
            pl.semaphore_wait(barrier, NX + NY + NZ - 3)
        moments = []
        for shift in range(1, NX):
            moments.append(
                sent(
                    xm.at[step, kx],
                    xm.at[step, kx],
                    xms_sem.at[step, shift],
                    xmr_sem.at[step, shift],
                    "gx",
                    around(kx, shift, NX),
                )
            )
            moments[-1].start()
        leaving.extend(moments)
        x_moments = moments
        ends = jnp.zeros((CX, CY), F32)
        for z in range(CZ):
            hi, lo = halves(first[z])
            r = dot(jnp.concatenate([hi, lo], axis=1), y1[z]) + dot(hi, y2[z])
            work[z] = r[:, :CY]
            ends = ends + r[:, CY:]
        ends = jnp.transpose(ends)[:16]
        base = CZ * kz + 1

        def upward(c):
            return sent(
                sup.at[step, pl.ds(CH * c, CH), :],
                zup.at[step, pl.ds(CH * c, CH), :],
                ups_sem.at[step, c],
                upr_sem.at[step, c],
                "gz",
                around(kz, 1, NZ),
            )

        def downward(c):
            return sent(
                sdown.at[step, pl.ds(CH * c, CH), :],
                zdown.at[step, pl.ds(CH * c, CH), :],
                dns_sem.at[step, c],
                dnr_sem.at[step, c],
                "gz",
                around(kz, -1, NZ),
            )

        for c in range(NCH):
            rows = slice(CH * c, CH * (c + 1))
            w = jnp.zeros((CH, CY), F32)
            v = jnp.zeros((CH, CY), F32)
            for z in range(CZ):
                value = work[z, rows, :]
                w = w + pq[1, base + z, 0:1, :] * value
                v = v + pq[0, base + z, 0:1, :] * value
            sup[step, rows, :] = w
            sdown[step, rows, :] = v

            @pl.when(kz == 0)
            def _():
                upward(c).start()
                zup[step, rows, :] = jnp.zeros((CH, CY), F32)

            @pl.when(kz == NZ - 1)
            def _():
                downward(c).start()
                zdown[step, rows, :] = jnp.zeros((CH, CY), F32)

        def relay_up():
            for c in range(NCH):
                rows = slice(CH * c, CH * (c + 1))
                up = upward(c)
                up.wait_recv()

                @pl.when(kz < NZ - 1)
                def _():
                    sup[step, rows, :] = sup[step, rows, :] + zup[step, rows, :]
                    up.start()

        def relay_down():
            for c in range(NCH):
                rows = slice(CH * c, CH * (c + 1))
                down = downward(c)
                down.wait_recv()

                @pl.when(kz > 0)
                def _():
                    sdown[step, rows, :] = sdown[step, rows, :] + zdown[step, rows, :]
                    down.start()

        for copy in x_moments:
            copy.wait_recv()
        below = jnp.zeros((8, CY), F32)
        above = jnp.zeros((8, CY), F32)
        for m in range(NX):
            plus, minus = xm[step, m, 0:8, :], xm[step, m, 8:16, :]
            below = below + xw[m, 0] * plus + xw[m, 1] * minus
            above = above + xw[m, 2] * plus + xw[m, 3] * minus
        both = jnp.concatenate([below, above], axis=0)
        r = jnp.zeros((16, 2 * CY), F32)
        for z in range(CZ):
            hi, lo = halves(jnp.where((sub16 & 7) == z, both, 0.0))
            r = r + dot(jnp.concatenate([hi, lo], axis=1), y1[z]) + dot(hi, y2[z])
        waves = r[:, :CY]
        zm[step, kz, 0:16, :] = waves

        def taken(rows, shift):
            return jnp.sum(
                jnp.where(lane8 == sub8 + shift, rows, 0.0), axis=1, keepdims=True
            )

        for part in range(2):
            of_below, of_above = taken(r[:8, CY:], 8 * part), taken(r[8:, CY:], 8 * part)
            for h in range(2):
                cols = slice(128 * h, 128 * (h + 1))
                ym[step, ky, 8 * part : 8 * part + 8, cols] = (
                    ends[8 * part : 8 * part + 8, cols]
                    + rowp[h] * of_below
                    + rown[h] * of_above
                )
        y_moments = []
        for shift in range(1, NY):
            y_moments.append(
                sent(
                    ym.at[step, ky],
                    ym.at[step, ky],
                    yms_sem.at[step, shift],
                    ymr_sem.at[step, shift],
                    "gy",
                    around(ky, shift, NY),
                )
            )
            y_moments[-1].start()
        leaving.extend(y_moments)

        @pl.when(kz == 0)
        def _():
            relay_down()

        @pl.when(kz == 1)
        def _():
            relay_up()
            relay_down()

        @pl.when(kz == 2)
        def _():
            relay_down()
            relay_up()

        @pl.when(kz == NZ - 1)
        def _():
            relay_up()

        for copy in y_moments:
            copy.wait_recv()
        below = [jnp.zeros((8, 128), F32) for _ in range(2)]
        above = [jnp.zeros((8, 128), F32) for _ in range(2)]
        for m in range(NY):
            for h in range(2):
                cols = slice(128 * h, 128 * (h + 1))
                plus, minus = ym[step, m, 0:8, cols], ym[step, m, 8:16, cols]
                below[h] = below[h] + yw[m, 0] * plus + yw[m, 1] * minus
                above[h] = above[h] + yw[m, 2] * plus + yw[m, 3] * minus
        for h in range(2):
            zm[step, kz, 16 + 16 * h : 24 + 16 * h, :] = below[h]
            zm[step, kz, 24 + 16 * h : 32 + 16 * h, :] = above[h]
        z_waves = []
        for shift in range(1, NZ):
            z_waves.append(
                sent(
                    zm.at[step, kz],
                    zm.at[step, kz],
                    zms_sem.at[step, shift],
                    zmr_sem.at[step, shift],
                    "gz",
                    around(kz, shift, NZ),
                )
            )
            z_waves[-1].start()
        leaving.extend(z_waves)
        for h in range(2):
            cols = slice(128 * h, 128 * (h + 1))
            turn[0:8, cols] = below[h]
            turn[8:16, cols] = above[h]
        columns = jnp.transpose(turn[...])
        for z in range(CZ):
            work[z] = (
                work[z]
                + lp[z] * waves[z : z + 1]
                + ln[z] * waves[z + 8 : z + 9]
                + columns[:, z : z + 1] * rowp[0, z : z + 1, :]
                + columns[:, z + 8 : z + 9] * rown[0, z : z + 1, :]
            )
        for copy in z_waves:
            copy.wait_recv()
        for m in range(NZ):
            for side in range(2):
                rhs[16 * m : 16 * m + 16, 128 * side : 128 * side + 128] = (
                    coef[m, side] * zm[step, m, 0:16, :]
                )
                mixed[64 + 16 * m : 80 + 16 * m, 128 * side : 128 * side + 128] = zm[
                    step, m, 16 + 16 * side : 32 + 16 * side, :
                ]
        hi, lo = halves(jnp.transpose(mixed[...]))
        rhi, rlo = halves(rhs[...])
        turn_in = (
            dot(jnp.concatenate([hi, lo], axis=1), jnp.concatenate([rhi, rhi], axis=0))
            + dot(hi, rlo)
        )

        last = step == STEPS - 1
        for c in range(NCH):
            rows = slice(CH * c, CH * (c + 1))
            padded = slice(PAD + CH * c, PAD + CH * (c + 1))
            lower = zup[step, rows, :] + turn_in[rows, :CY]
            upper = zdown[step, rows, :] + turn_in[rows, CY:]
            run = lower
            for z in range(CZ):
                run = run + pq[1, base + z, 0:1, :] * work[z, rows, :]
                third[z, rows, :] = pq[0, base + z, 0:1, :] * run
            if not last:
                top = base + CZ
                upad[CZ + 1, padded, :] = (
                    upad[CZ + 1, padded, :]
                    + pq[0, top, 0:1, :] * run
                    + pq[1, top, 0:1, :] * upper
                )
            run = upper
            for z in range(CZ - 1, -1, -1):
                u = (
                    upad[z + 1, padded, :]
                    + third[z, rows, :]
                    + pq[1, base + z, 0:1, :] * run
                )
                run = run + pq[0, base + z, 0:1, :] * work[z, rows, :]
                if last:
                    rise_ref[z, rows, :] = u - u_ref[z, rows, :]
                else:
                    upad[z + 1, padded, :] = u
            if not last:
                upad[0, padded, :] = (
                    upad[0, padded, :]
                    + pq[0, base - 1, 0:1, :] * lower
                    + pq[1, base - 1, 0:1, :] * run
                )
        if not last:
            edges = edges_out()

        for c in range(NCH):

            @pl.when(kz < NZ - 1)
            def _():
                upward(c).wait_send()

            @pl.when(kz > 0)
            def _():
                downward(c).wait_send()

    for copy in leaving:
        copy.wait_send()


def stepped(sheet, cond, scaling, u, kind, joule, z_edge, x_edge, y_edge):
    block = jax.ShapeDtypeStruct((CZ, CX, CY), F32)
    smem = pl.BlockSpec(memory_space=pltpu.SMEM)
    vmem = pl.BlockSpec(memory_space=pltpu.VMEM)
    dma = pltpu.SemaphoreType.DMA
    tall = pltpu.VMEM((CZ, CX, CY), F32)
    return pl.pallas_call(
        adi_kernel,
        out_shape=block,
        in_specs=[smem] * 3 + [vmem] * 6,
        out_specs=vmem,
        scratch_shapes=[
            pltpu.VMEM((CZ + 2, WIDE, CY), F32),
            pltpu.VMEM((CZ + 2, WIDE, CY), F32),
            tall,
            tall,
            tall,
            tall,
            pltpu.VMEM((CZ + 1, CX, CY), F32),
            tall,
            pltpu.VMEM((CZ, CX + 16, CX), BF16),
            pltpu.VMEM((CZ, CX + 16, CX), BF16),
            pltpu.VMEM((CZ, 2 * CY, 2 * CY), BF16),
            pltpu.VMEM((CZ, CY, 2 * CY), BF16),
            tall,
            tall,
            pltpu.VMEM((2, 8, 128), F32),
            pltpu.VMEM((2, 8, 128), F32),
            pltpu.VMEM((5, 8, 128), F32),
            pltpu.VMEM((NX, 4, 8, 128), F32),
            pltpu.VMEM((NY, 4, 8, 128), F32),
            pltpu.VMEM((2, PLANES + 2, 8, 128), F32),
            tall,
            tall,
            tall,
            pltpu.VMEM((CY, CX), F32),
            pltpu.VMEM((128, CX), F32),
            pltpu.VMEM((128, 2 * CY), F32),
            pltpu.VMEM((NZ, 2, 16, 128), F32),
            pltpu.VMEM((STEPS, NZ, 48, 128), F32),
            pltpu.VMEM((2, 8, CY), F32),
            pltpu.VMEM((2, 8, CY), F32),
            pltpu.VMEM((16, CX), F32),
            pltpu.VMEM((2, 16, CX), F32),
            pltpu.VMEM((STEPS, NX, 16, CY), F32),
            pltpu.VMEM((STEPS, NY, 16, CX), F32),
            pltpu.VMEM((STEPS, CX, CY), F32),
            pltpu.VMEM((STEPS, CX, CY), F32),
            pltpu.VMEM((STEPS, CX, CY), F32),
            pltpu.VMEM((STEPS, CX, CY), F32),
            dma((2,)),
            dma((2,)),
            dma((2,)),
            dma((2,)),
            dma((STEPS, NX)),
            dma((STEPS, NX)),
            dma((STEPS, NY)),
            dma((STEPS, NY)),
            dma((STEPS, NZ)),
            dma((STEPS, NZ)),
            dma((STEPS, NCH)),
            dma((STEPS, NCH)),
            dma((STEPS, NCH)),
            dma((STEPS, NCH)),
        ],
        compiler_params=pltpu.CompilerParams(
            collective_id=0, has_side_effects=True, vmem_limit_bytes=VMEM_BYTES
        ),
        name="steps",
    )(sheet, cond, scaling, u, kind, joule, z_edge, x_edge, y_edge)


def per_device(
    starting_warmth,
    sheet_stratum_number,
    stratum_heat_conduction,
    substance_kind,
    substance_kind_scaling,
    wire_piece_amperes,
    wire_piece_ohms_base,
    wire_piece_tile,
    wire_piece_voxel,
):
    shape = (SEGS // 128, 128)
    small = (sheet_stratum_number, stratum_heat_conduction, substance_kind_scaling)
    powers, columns, rows, *edges = spread_out(
        *small,
        wire_piece_amperes.reshape(shape),
        wire_piece_ohms_base.reshape(shape),
        wire_piece_tile.T,
        wire_piece_voxel.reshape(shape),
        starting_warmth,
        substance_kind,
    )
    joule = added(rows, powers, columns).reshape(CZ, CX, CY)
    rise = stepped(*small, starting_warmth, substance_kind, joule, *edges)
    warmed = starting_warmth + rise
    return warmed, (1.0 + WARMING_SLOPE * warmed) * joule


def solution(mesh):
    return jax.shard_map(
        per_device,
        mesh=mesh,
        in_specs=(
            P("gz", "gx", "gy"),
            P(),
            P(),
            P("gz", "gx", "gy"),
            P(),
            P(("gx", "gy", "gz")),
            P(("gx", "gy", "gz")),
            P(("gx", "gy", "gz"), None),
            P(("gx", "gy", "gz")),
        ),
        out_specs=(P("gz", "gx", "gy"), P("gz", "gx", "gy")),
        check_vma=False,
    )
```

```python
import functools

import jax
import jax.numpy as jnp
from jax import lax
from jax.experimental import pallas as pl
from jax.experimental.pallas import tpu as pltpu
from jax.sharding import PartitionSpec as P

STEPS = 2
HEAT_SPREADING = 1000.0
STIFF = 1.5
WARMING_SLOPE = 0.1
OHMIC_POWER = 8.0

F32 = jnp.float32
BF16 = jnp.bfloat16
MESH = pl.DeviceIdType.MESH

CZ, CX, CY = 8, 256, 128
LEN = 1024
PLANES = 32
NX, NY, NZ = 4, 8, 4
SEGS = 4096
TOP = 64
DEVS = 128
PAD = 8
WIDE = CX + 2 * PAD
NCH = 4
CH = CX // NCH
NACC = 8
DOUBLINGS = (8, 16, 32, 64, 128)
VMEM_BYTES = 60 * 1024 * 1024


def dot(a, b):
    return jnp.dot(a, b, preferred_element_type=F32)


def halves(x):
    high = x.astype(BF16)
    return high, (x - high.astype(F32)).astype(BF16)


def place_segments(amp_ref, ohm_ref, tile_ref, cell_ref, acc):
    width = 256
    row = lax.broadcasted_iota(jnp.int32, (width, width + DEVS), 0)
    col = lax.broadcasted_iota(jnp.int32, (width, width + DEVS), 1)
    before = jnp.where((row < col) | (col >= width), 1.0, 0.0).astype(BF16)
    owner = lax.broadcasted_iota(jnp.int32, (DEVS, width), 0)
    place = lax.broadcasted_iota(jnp.int32, (TOP, width), 0).astype(F32)
    acc[...] = jnp.zeros_like(acc)
    carry = jnp.zeros((DEVS, DEVS), F32)

    def line(ref, j):
        return jnp.concatenate([ref[2 * j : 2 * j + 1, :], ref[2 * j + 1 : 2 * j + 2, :]], axis=1)

    for j in range(SEGS // width):
        tile = tile_ref[:, width * j : width * (j + 1)]
        tile = ((tile & 3) << 5) + ((tile >> 5) << 3) + ((tile >> 2) & 7)
        mine = owner == tile
        hot = jnp.where(mine, 1.0, 0.0).astype(BF16)
        found = dot(hot, before)
        ahead = found[:, :width] + jnp.concatenate([carry, carry], axis=1)
        rank = jnp.sum(jnp.where(mine, ahead, 0.0), axis=0, keepdims=True)
        carry = carry + found[:, width:]
        amp = line(amp_ref, j)
        power = amp * amp * line(ohm_ref, j)
        p0 = power.astype(BF16).astype(F32)
        p1 = (power - p0).astype(BF16).astype(F32)
        p2 = power - p0 - p1
        cell = line(cell_ref, j)
        c0 = (cell >> 12).astype(F32)
        c1 = ((cell >> 6) & 63).astype(F32)
        c2 = (cell & 63).astype(F32)
        here = place == rank
        parts = jnp.concatenate(
            [jnp.where(here, part, 0.0).astype(BF16) for part in (p0, c0, p1, c1, p2, c2)], axis=0
        )
        acc[...] += lax.dot_general(
            hot, parts, (((1,), (1,)), ((), ())), preferred_element_type=F32
        )
    a, b, c = (acc[:, 128 * k : 128 * (k + 1)] for k in range(3))
    lane = lax.broadcasted_iota(jnp.int32, (DEVS, DEVS), 1)
    return jnp.where(lane < TOP, a + b + c, a * 4096.0 + b * 64.0 + c)


def around(me, shift, count):
    return lax.rem(me + shift + count, count)


def sent(src, dst, send, recv, axis, to):
    return pltpu.make_async_remote_copy(
        src_ref=src,
        dst_ref=dst,
        send_sem=send,
        recv_sem=recv,
        device_id={axis: to},
        device_id_type=MESH,
    )


def greet(places):
    barrier = pltpu.get_barrier_semaphore()
    for axis, me, count in places:
        for shift in range(1, count):
            pl.semaphore_signal(
                barrier, inc=1, device_id={axis: around(me, shift, count)}, device_id_type=MESH
            )
    return barrier


def cell_conductance(cond_ref, sheet_ref, scale_ref, kind, plane):
    factor = jnp.where(kind == 0, scale_ref[0], 0.0)
    for category in range(1, 4):
        factor = jnp.where(kind == category, scale_ref[category], factor)
    return factor * cond_ref[sheet_ref[plane]]


def edge_columns(planes):
    lane = lax.broadcasted_iota(jnp.int32, (CX, CY), 1)
    out = jnp.zeros((CX, CY), F32)
    for z, plane in enumerate(planes):
        out = jnp.where((lane >> 1) == z, pltpu.roll(plane, 2 * z + 1, 1), out)
    return jnp.transpose(out)[:16]


def spread_kernel(
    sheet_ref,
    cond_ref,
    scale_ref,
    amp_ref,
    ohm_ref,
    tile_ref,
    cell_ref,
    u_hbm,
    kind_hbm,
    power_ref,
    column_ref,
    row_ref,
    zr,
    xr,
    yr,
    u,
    kind,
    c,
    acc,
    one,
    two,
    three,
    four,
    five,
    zs,
    xs,
    ys,
    load_sem,
    one_send,
    one_recv,
    two_send,
    two_recv,
    three_send,
    three_recv,
    zs_sem,
    zr_sem,
    xs_sem,
    xr_sem,
    ys_sem,
    yr_sem,
):
    kx, ky, kz = lax.axis_index("gx"), lax.axis_index("gy"), lax.axis_index("gz")
    barrier = greet((("gx", kx, NX), ("gy", ky, NY), ("gz", kz, NZ)))
    loads = [
        pltpu.make_async_copy(u_hbm, u, load_sem.at[0]),
        pltpu.make_async_copy(kind_hbm, kind, load_sem.at[1]),
    ]
    for copy in loads:
        copy.start()
    one[...] = place_segments(amp_ref, ohm_ref, tile_ref, cell_ref, acc).reshape(
        NZ, NX, NY, DEVS
    )
    pl.semaphore_wait(barrier, NX + NY + NZ - 3)
    leaving = []

    def exchange(source, target, send, recv, axis, me, count):
        copies = []
        for shift in range(1, count):
            to = around(me, shift, count)
            copies.append(
                sent(source(to), target.at[me], send.at[shift], recv.at[shift], axis, to)
            )
            copies[-1].start()
        leaving.extend(copies)
        return copies

    copies = exchange(lambda to: one.at[to], two, one_send, one_recv, "gz", kz, NZ)
    two[kz] = one[kz]

    for copy in loads:
        copy.wait()
    for z in range(CZ):
        c[z] = cell_conductance(cond_ref, sheet_ref, scale_ref, kind[z], CZ * kz + z)
    for part, ref in ((0, u), (1, c)):
        zs[part, 0] = ref[CZ - 1]
        zs[part, 1] = ref[0]
        for side, to in ((0, 1), (1, -1)):
            leaving.append(
                sent(
                    zs.at[part, side],
                    zr.at[part, side],
                    zs_sem.at[part, side],
                    zr_sem.at[part, side],
                    "gz",
                    around(kz, to, NZ),
                )
            )
            leaving[-1].start()
    for copy in copies:
        copy.wait_recv()
    copies = exchange(lambda to: two.at[:, to], three, two_send, two_recv, "gx", kx, NX)
    three[kx] = two[:, kx]
    for part, ref in ((0, u), (1, c)):
        xs[0, pl.ds(8 * part, 8), :] = ref[:, CX - 1, :]
        xs[1, pl.ds(8 * part, 8), :] = ref[:, 0, :]
        ys[pl.ds(16 * part, 16), :] = edge_columns([ref[z] for z in range(CZ)])
    for side, to in ((0, 1), (1, -1)):
        leaving.append(
            sent(
                xs.at[side],
                xr.at[side],
                xs_sem.at[side],
                xr_sem.at[side],
                "gx",
                around(kx, to, NX),
            )
        )
        leaving.append(
            sent(ys, yr.at[side], ys_sem.at[side], yr_sem.at[side], "gy", around(ky, to, NY))
        )
    for copy in leaving[-4:]:
        copy.start()
    edges = leaving[-4:]
    for copy in copies:
        copy.wait_recv()
    for to in range(NY):
        four[to] = three[:, :, to, :].reshape(NX * NZ, DEVS)
    copies = exchange(lambda to: four.at[to], five, three_send, three_recv, "gy", ky, NY)
    five[ky] = four[ky]
    for copy in copies:
        copy.wait_recv()
    got = five[...].reshape(DEVS, DEVS)
    turned = pltpu.roll(got, TOP, 1)
    lane = lax.broadcasted_iota(jnp.int32, (DEVS // 2, DEVS), 1)
    left = lane < TOP
    power_ref[...] = jnp.where(left, got[: DEVS // 2], turned[DEVS // 2 :])
    cells = jnp.where(left, turned[: DEVS // 2], got[DEVS // 2 :]).astype(jnp.int32)
    column_ref[...] = cells & 127
    row_ref[...] = cells >> 7
    for part in range(2):
        for side, to in ((0, 1), (1, -1)):
            sent(
                zs.at[part, side],
                zr.at[part, side],
                zs_sem.at[part, side],
                zr_sem.at[part, side],
                "gz",
                around(kz, to, NZ),
            ).wait_recv()
    for copy in edges:
        copy.wait_recv()
    for copy in leaving:
        copy.wait_send()


def spread_out(sheet, cond, scaling, amp, ohm, tile, cell, u, kind):
    smem = pl.BlockSpec(memory_space=pltpu.SMEM)
    vmem = pl.BlockSpec(memory_space=pltpu.VMEM)
    whole = pl.BlockSpec(memory_space=pl.ANY)
    dma = pltpu.SemaphoreType.DMA
    half = (DEVS // 2, DEVS)
    return pl.pallas_call(
        spread_kernel,
        out_shape=(
            jax.ShapeDtypeStruct(half, F32),
            jax.ShapeDtypeStruct(half, jnp.int32),
            jax.ShapeDtypeStruct(half, jnp.int32),
            jax.ShapeDtypeStruct((2, 2, CX, CY), F32),
            jax.ShapeDtypeStruct((2, 16, CY), F32),
            jax.ShapeDtypeStruct((2, 32, CX), F32),
        ),
        in_specs=[smem] * 3 + [vmem] * 4 + [whole] * 2,
        out_specs=(vmem,) * 6,
        scratch_shapes=[
            pltpu.VMEM((CZ, CX, CY), F32),
            pltpu.VMEM((CZ, CX, CY), jnp.int32),
            pltpu.VMEM((CZ, CX, CY), F32),
            pltpu.VMEM((DEVS, 384), F32),
            pltpu.VMEM((NZ, NX, NY, DEVS), F32),
            pltpu.VMEM((NZ, NX, NY, DEVS), F32),
            pltpu.VMEM((NX, NZ, NY, DEVS), F32),
            pltpu.VMEM((NY, NX * NZ, DEVS), F32),
            pltpu.VMEM((NY, NX * NZ, DEVS), F32),
            pltpu.VMEM((2, 2, CX, CY), F32),
            pltpu.VMEM((2, 16, CY), F32),
            pltpu.VMEM((32, CX), F32),
            dma((2,)),
            dma((NZ,)),
            dma((NZ,)),
            dma((NX,)),
            dma((NX,)),
            dma((NY,)),
            dma((NY,)),
            dma((2, 2)),
            dma((2, 2)),
            dma((2,)),
            dma((2,)),
            dma((2,)),
            dma((2,)),
        ],
        compiler_params=pltpu.CompilerParams(
            collective_id=1, has_side_effects=True, vmem_limit_bytes=VMEM_BYTES
        ),
        name="spread",
    )(sheet, cond, scaling, amp, ohm, tile, cell, u, kind)


def add_kernel(row_ref, power_ref, column_ref, out_ref, spread, *accs):
    for acc in accs:
        acc[...] = jnp.zeros_like(acc)
    sub = lax.broadcasted_iota(jnp.int32, (CY, 128), 0)
    for j in range(DEVS // 2):
        spread[128 * j : 128 * (j + 1), :] = jnp.transpose(
            jnp.where(sub == column_ref[j : j + 1, :], power_ref[j : j + 1, :], 0.0)
        )

    def some(i, carry):
        for k in range(128):
            acc = accs[k % NACC]
            acc[pl.ds(row_ref[i, k], 1), :] += spread[pl.ds(128 * i + k, 1), :]
        return carry

    lax.fori_loop(0, DEVS // 2, some, 0)
    total = accs[0][...]
    for acc in accs[1:]:
        total = total + acc[...]
    out_ref[...] = total


def added(rows, powers, columns):
    vmem = pl.BlockSpec(memory_space=pltpu.VMEM)
    return pl.pallas_call(
        add_kernel,
        out_shape=jax.ShapeDtypeStruct((CZ * CX, CY), F32),
        in_specs=[pl.BlockSpec(memory_space=pltpu.SMEM), vmem, vmem],
        out_specs=vmem,
        scratch_shapes=[pltpu.VMEM((DEVS * TOP, 128), F32)]
        + [pltpu.VMEM((CZ * CX, CY), F32)] * NACC,
        compiler_params=pltpu.CompilerParams(vmem_limit_bytes=VMEM_BYTES),
        name="add",
    )(rows, powers, columns)


def line_weights(theta, scale, me, count, length):
    whole = 2 * LEN
    out = []
    for m in range(count):

        def tile(exponent, keep):
            return jnp.where(keep, jnp.exp(-theta * exponent.astype(F32)) * scale, 0.0)

        lower, same = m < me, me == m
        gap = jnp.where(lower, me - m, m - me)
        near, far = length * (gap - 1) + 1, whole - length * gap - (length - 1)
        apart = jnp.logical_not(same)
        out.append(
            (
                tile(jnp.where(lower, near, far), apart),
                tile(length * (me + m) + 1, True),
                tile(whole - length * (me + m + 2) + 1, True),
                tile(jnp.where(lower, far, near), apart),
            )
        )
    return out


def adi_kernel(
    sheet_ref,
    cond_ref,
    scale_ref,
    x_edge,
    y_edge,
    u_hbm,
    kind_hbm,
    joule_hbm,
    z_edge,
    rise_hbm,
    u_ref,
    kind_ref,
    joule_ref,
    upad,
    cpad,
    gxl,
    gxu,
    gyl,
    gyu,
    gz,
    gself,
    thi,
    tlo,
    y1,
    y2,
    lp,
    ln,
    rowp,
    rown,
    tables,
    xw,
    yw,
    pq,
    first,
    work,
    third,
    turn,
    mixed,
    rhs,
    coef,
    zm,
    xs,
    xr,
    ys,
    yr,
    xm,
    ym,
    zup,
    zdown,
    zfar,
    sup,
    sdown,
    load_sem,
    xs_sem,
    xr_sem,
    ys_sem,
    yr_sem,
    xms_sem,
    xmr_sem,
    yms_sem,
    ymr_sem,
    zms_sem,
    zmr_sem,
    ups_sem,
    upr_sem,
    dns_sem,
    dnr_sem,
    ons_sem,
    ond_sem,
    onr_sem,
):
    kx, ky, kz = lax.axis_index("gx"), lax.axis_index("gy"), lax.axis_index("gz")
    barrier = greet((("gx", kx, NX), ("gy", ky, NY), ("gz", kz, NZ)))
    inner = pl.ds(PAD, CX)
    loads = [
        pltpu.make_async_copy(src, dst, load_sem.at[k])
        for k, (src, dst) in enumerate(
            (
                (kind_hbm, kind_ref),
                (u_hbm, u_ref),
                (z_edge.at[0, 0], upad.at[0, inner, :]),
                (z_edge.at[0, 1], upad.at[CZ + 1, inner, :]),
                (z_edge.at[1, 0], cpad.at[0, inner, :]),
                (z_edge.at[1, 1], cpad.at[CZ + 1, inner, :]),
                (joule_hbm, joule_ref),
            )
        )
    ]
    for copy in loads:
        copy.start()
    sub8 = lax.broadcasted_iota(jnp.int32, (8, 128), 0)
    lane8 = lax.broadcasted_iota(jnp.int32, (8, 128), 1)
    lane = lax.broadcasted_iota(jnp.int32, (CX, CY), 1)
    leaving = []
    leaving_home = []

    def edges_out():
        xs[0] = upad[1 : CZ + 1, PAD + CX - 1, :]
        xs[1] = upad[1 : CZ + 1, PAD, :]
        ys[...] = edge_columns([upad[z + 1, inner, :] for z in range(CZ)])
        copies = []
        for side, to in ((0, 1), (1, -1)):
            copies.append(
                sent(
                    xs.at[side],
                    xr.at[side],
                    xs_sem.at[side],
                    xr_sem.at[side],
                    "gx",
                    around(kx, to, NX),
                )
            )
            copies.append(
                sent(
                    ys, yr.at[side], ys_sem.at[side], yr_sem.at[side], "gy", around(ky, to, NY)
                )
            )
        for copy in copies:
            copy.start()
        leaving.extend(copies)
        return copies

    own = jnp.zeros((8, 128), F32)
    for z in range(CZ):
        own = jnp.where(sub8 == z, cond_ref[sheet_ref[CZ * kz + z]], own)

    def decay(plane_cond):
        a = HEAT_SPREADING * STIFF * plane_cond
        s = 0.5 * lax.rsqrt(a)
        s = 0.5 * (s + 0.25 / (a * s))
        s2 = s * s
        return a, 2.0 * s * (
            1.0 - s2 * (1.0 / 6.0 - s2 * (3.0 / 40.0 - s2 * (15.0 / 336.0)))
        )

    a, theta = decay(own)
    whole = jnp.exp(-theta * (2.0 * LEN))
    root = jnp.sqrt(a + 0.25)
    scale = 0.5 / (root * (1.0 - whole))
    tables[0] = theta
    tables[1] = scale
    tables[2] = scale * whole
    tables[3] = jnp.exp(-theta * (CX - 1.0))
    tables[4] = jnp.exp(-theta * (CY - 1.0))
    last_x, last_y = tables[3], tables[4]
    for k, hop in enumerate(DOUBLINGS):
        tables[5 + k] = jnp.exp(-theta * float(hop))
        tables[10 + k] = jnp.exp(theta * float(hop))
    for h in range(2):
        at = (lane8 + 128 * h).astype(F32)
        rowp[h] = jnp.exp(-theta * at)
        rown[h] = jnp.exp(theta * at)
    for m, tiles in enumerate(line_weights(theta, scale, kx, NX, CX)):
        for k, tile in enumerate(tiles):
            xw[m, k] = tile if k < 2 else tile * last_x
    for m, tiles in enumerate(line_weights(theta, scale, ky, NY, CY)):
        for k, tile in enumerate(tiles):
            yw[m, k] = tile if k < 2 else tile * last_y

    conds = [jnp.full((8, 128), cond_ref[sheet_ref[z]], F32) for z in range(PLANES)]
    stiff = HEAT_SPREADING * STIFF
    links = [0.5 * stiff * (conds[z] + conds[z + 1]) for z in range(PLANES - 1)]
    up = [1.0 + stiff * conds[0]]
    grow = [jnp.ones((8, 128), F32)]
    for z in range(PLANES - 1):
        grow.append(grow[z] * (1.0 + up[z] / links[z]))
        up.append(1.0 + links[z] * (up[z] / (up[z] + links[z])))
    down = [None] * PLANES
    down[-1] = jnp.ones((8, 128), F32)
    for z in range(PLANES - 2, -1, -1):
        down[z] = 1.0 + links[z] * (down[z + 1] / (down[z + 1] + links[z]))
    nothing = jnp.zeros((8, 128), F32)
    pq[0, 0] = nothing
    pq[1, 0] = nothing
    pq[0, PLANES + 1] = nothing
    pq[1, PLANES + 1] = nothing
    fade = [1.0 / ((up[z] + down[z] - 1.0) * grow[z]) for z in range(PLANES)]
    for z in range(PLANES):
        pq[0, z + 1] = fade[z]
        pq[1, z + 1] = grow[z]

    for m in range(NZ):
        cond, low, high = nothing, nothing, nothing
        for z in range(CZ):
            here = sub8 == z
            cond = jnp.where(here, conds[CZ * m + z], cond)
            low = jnp.where(here, grow[CZ * m + z], low)
            high = jnp.where(here, fade[CZ * m + z], high)
        _, th = decay(cond)
        low = jnp.where(m < kz, low, 0.0)
        high = jnp.where(m > kz, high, 0.0)
        for part in range(2):
            at = pl.ds(16 * m + 8 * part, 8)
            below_at = pl.ds(64 + 16 * m + 8 * part, 8)
            th = -th
            for h in range(2):
                wave = jnp.exp(th * (lane8 + 128 * h).astype(F32))
                mixed[at, pl.ds(128 * h, 128)] = wave
                if h == 0:
                    rhs[below_at, pl.ds(0, 128)] = low * wave
                    rhs[below_at, pl.ds(128, 128)] = high * wave
            coef[m, 0, pl.ds(8 * part, 8), :] = low
            coef[m, 1, pl.ds(8 * part, 8), :] = high

    sub16 = lax.broadcasted_iota(jnp.int32, (16, 128), 0)
    lane_y = lax.broadcasted_iota(jnp.int32, (CY, CY), 1)

    def weights(z, carry):
        one = pl.ds(z, 1)
        th = tables[0, one, :]
        fall = jnp.exp(-th * sub8.astype(F32))
        rise = jnp.exp(th * sub8.astype(F32))
        for k in range(len(DOUBLINGS)):
            fall = jnp.concatenate([fall, fall * tables[5 + k, one, :]], axis=0)
            rise = jnp.concatenate([rise, rise * tables[10 + k, one, :]], axis=0)
        lp[z] = fall
        ln[z] = rise
        c1, c2 = tables[1, one, :], tables[2, one, :]
        for h in range(2):
            x, y = fall * rown[h, one, :], rise * rowp[h, one, :]
            t = c1 * jnp.minimum(x, y) + c2 * jnp.maximum(x, y)
            cols = pl.ds(128 * h, 128)
            ends = jnp.where(
                sub16 == 0,
                tables[3, one, :] * rown[h, one, :],
                jnp.where(sub16 == 1, rowp[h, one, :], 0.0),
            )
            hi, lo = halves(t)
            thi[z, :CX, cols] = hi
            tlo[z, :CX, cols] = lo
            if h == 0:
                y1[z, :CY, :CY] = hi[:CY]
                y1[z, CY:, :CY] = hi[:CY]
                y2[z, :, :CY] = lo[:CY]
            hi, lo = halves(ends)
            thi[z, CX:, cols] = hi
            tlo[z, CX:, cols] = lo
        w = jnp.where(
            lane_y == z,
            rise[:CY] * tables[4, one, :],
            jnp.where(lane_y == z + 8, fall[:CY], 0.0),
        )
        hi, lo = halves(w)
        y1[z, :CY, CY:] = hi
        y1[z, CY:, CY:] = hi
        y2[z, :, CY:] = lo
        return carry

    lax.fori_loop(0, CZ, weights, 0)
    turn[...] = jnp.zeros_like(turn)

    def y_edges(low, high):
        odd = (lax.broadcasted_iota(jnp.int32, (16, CX), 0) & 1) == 1
        turn[:16, :] = jnp.where(odd, pltpu.roll(low, 1, 0), pltpu.roll(high, 15, 0))
        return jnp.transpose(turn[...])

    for copy in loads:
        copy.wait()
    for z in range(CZ):
        cpad[z + 1, inner, :] = cell_conductance(
            cond_ref, sheet_ref, scale_ref, kind_ref[z], CZ * kz + z
        )
        upad[z + 1, inner, :] = u_ref[z]

    half = 0.5 * HEAT_SPREADING
    cpad[1 : CZ + 1, PAD - 1, :] = jnp.where(
        kx == 0, -cpad[1 : CZ + 1, PAD, :], x_edge[0, 8:16, :]
    )
    cpad[1 : CZ + 1, PAD + CX, :] = jnp.where(
        kx == NX - 1, -cpad[1 : CZ + 1, PAD + CX - 1, :], x_edge[1, 8:16, :]
    )
    work[0] = y_edges(y_edge[0, 16:32, :], y_edge[1, 16:32, :])
    gz[0] = jnp.where(kz == 0, 0.0, half * (cpad[0, inner, :] + cpad[1, inner, :]))
    gz[CZ] = jnp.where(
        kz == NZ - 1, 0.0, half * (cpad[CZ, inner, :] + cpad[CZ + 1, inner, :])
    )
    for z in range(CZ - 1):
        gz[z + 1] = half * (cpad[z + 1, inner, :] + cpad[z + 2, inner, :])
    for z in range(CZ):
        c = cpad[z + 1, inner, :]
        edge = pltpu.roll(work[0], CY - (2 * z + 1), 1)
        low = jnp.where(lane == 0, jnp.where(ky == 0, -c, edge), pltpu.roll(c, 1, 1))
        high = jnp.where(
            lane == CY - 1, jnp.where(ky == NY - 1, -c, edge), pltpu.roll(c, CY - 1, 1)
        )
        xl = half * (c + cpad[z + 1, PAD - 1 : PAD + CX - 1, :])
        xu = half * (c + cpad[z + 1, PAD + 1 : PAD + CX + 1, :])
        yl, yu = half * (c + low), half * (c + high)
        gxl[z], gxu[z], gyl[z], gyu[z] = xl, xu, yl, yu
        every = xl + xu + yl + yu + gz[z] + gz[z + 1]
        if z == 0:
            every = every + jnp.where(kz == 0, HEAT_SPREADING * c, 0.0)
        gself[z] = (OHMIC_POWER * WARMING_SLOPE) * joule_ref[z] - every

    for step in range(STEPS):
        if step:
            for copy in edges:
                copy.wait_recv()
            x_low, x_high, y_low, y_high = xr[0], xr[1], yr[0], yr[1]
        else:
            x_low, x_high = x_edge[0, 0:8, :], x_edge[1, 0:8, :]
            y_low, y_high = y_edge[0, 0:16, :], y_edge[1, 0:16, :]
        upad[1 : CZ + 1, PAD - 1, :] = x_low
        upad[1 : CZ + 1, PAD + CX, :] = x_high
        work[0] = y_edges(y_low, y_high)

        def source_and_x(z, carry):
            u = upad[z + 1, inner, :]
            edge = pltpu.roll(work[0], CY - (2 * z + 1), 1)
            low = jnp.where(lane == 0, edge, pltpu.roll(u, 1, 1))
            high = jnp.where(lane == CY - 1, edge, pltpu.roll(u, CY - 1, 1))
            b = gself[z] * u + OHMIC_POWER * joule_ref[z]
            b = b + gyl[z] * low + gyu[z] * high
            b = b + gxl[z] * upad[z + 1, PAD - 1 : PAD + CX - 1, :]
            b = b + gxu[z] * upad[z + 1, PAD + 1 : PAD + CX + 1, :]
            b = b + gz[z] * upad[z, inner, :] + gz[z + 1] * upad[z + 2, inner, :]
            hi, lo = halves(b)
            r = dot(thi[z], jnp.concatenate([hi, lo], axis=1))
            r = r[:, :CY] + r[:, CY:] + dot(tlo[z], hi)
            first[z] = r[:CX]
            xm[step, kx, pl.ds(z, 1), :] = r[CX : CX + 1]
            xm[step, kx, pl.ds(z + 8, 1), :] = r[CX + 1 : CX + 2]
            return carry

        for z in range(CZ):
            source_and_x(z, 0)

        if not step:
            pl.semaphore_wait(barrier, NX + NY + NZ - 3)
        moments = []
        for shift in range(1, NX):
            moments.append(
                sent(
                    xm.at[step, kx],
                    xm.at[step, kx],
                    xms_sem.at[step, shift],
                    xmr_sem.at[step, shift],
                    "gx",
                    around(kx, shift, NX),
                )
            )
            moments[-1].start()
        leaving.extend(moments)
        x_moments = moments
        ends = jnp.zeros((CX, CY), F32)
        for z in range(CZ):
            hi, lo = halves(first[z])
            r = dot(jnp.concatenate([hi, lo], axis=1), y1[z]) + dot(hi, y2[z])
            work[z] = r[:, :CY]
            ends = ends + r[:, CY:]
        ends = jnp.transpose(ends)[:16]
        base = CZ * kz + 1

        def hop(source, target, send, recv, to, c):
            at = pl.ds(CH * c, CH)
            return sent(
                source.at[step, at, :],
                target.at[step, at, :],
                send.at[step, c],
                recv.at[step, c],
                "gz",
                around(kz, to, NZ),
            )

        def upward(c):
            return hop(sup, zup, ups_sem, upr_sem, 1, c)

        def downward(c):
            return hop(sdown, zdown, dns_sem, dnr_sem, -1, c)

        def upward_on(c):
            return hop(zup, zfar, ons_sem, onr_sem, 1, c)

        def downward_on(c):
            return hop(zdown, zfar, ond_sem, onr_sem, -1, c)

        def goes_up(c):
            return (kz == 2) | (kz == (1 if c < NCH // 2 else 0))

        def goes_down(c):
            return (kz == 1) | (kz == (2 if c < NCH // 2 else 3))

        for c in range(NCH):
            rows = slice(CH * c, CH * (c + 1))
            w = jnp.zeros((CH, CY), F32)
            v = jnp.zeros((CH, CY), F32)
            for z in range(CZ):
                value = work[z, rows, :]
                w = w + pq[1, base + z, 0:1, :] * value
                v = v + pq[0, base + z, 0:1, :] * value
            sup[step, rows, :] = jnp.where(kz == NZ - 1, v, w)
            sdown[step, rows, :] = jnp.where(kz == 0, w, v)
            upward(c).start()
            downward(c).start()

        for copy in x_moments:
            copy.wait_recv()
        below = jnp.zeros((8, CY), F32)
        above = jnp.zeros((8, CY), F32)
        for m in range(NX):
            plus, minus = xm[step, m, 0:8, :], xm[step, m, 8:16, :]
            below = below + xw[m, 0] * plus + xw[m, 1] * minus
            above = above + xw[m, 2] * plus + xw[m, 3] * minus
        both = jnp.concatenate([below, above], axis=0)
        r = jnp.zeros((16, 2 * CY), F32)
        for z in range(CZ):
            hi, lo = halves(jnp.where((sub16 & 7) == z, both, 0.0))
            r = r + dot(jnp.concatenate([hi, lo], axis=1), y1[z]) + dot(hi, y2[z])
        waves = r[:, :CY]
        zm[step, kz, 0:16, :] = waves

        def taken(rows, shift):
            return jnp.sum(
                jnp.where(lane8 == sub8 + shift, rows, 0.0), axis=1, keepdims=True
            )

        for part in range(2):
            of_below, of_above = taken(r[:8, CY:], 8 * part), taken(r[8:, CY:], 8 * part)
            for h in range(2):
                cols = slice(128 * h, 128 * (h + 1))
                ym[step, ky, 8 * part : 8 * part + 8, cols] = (
                    ends[8 * part : 8 * part + 8, cols]
                    + rowp[h] * of_below
                    + rown[h] * of_above
                )
        y_moments = []
        for shift in range(1, NY):
            y_moments.append(
                sent(
                    ym.at[step, ky],
                    ym.at[step, ky],
                    yms_sem.at[step, shift],
                    ymr_sem.at[step, shift],
                    "gy",
                    around(ky, shift, NY),
                )
            )
            y_moments[-1].start()
        leaving.extend(y_moments)

        for c in range(NCH):
            upward(c).wait_recv()

            @pl.when(goes_up(c))
            def _():
                upward_on(c).start()

            downward(c).wait_recv()

            @pl.when(goes_down(c))
            def _():
                downward_on(c).start()

        for copy in y_moments:
            copy.wait_recv()
        below = [jnp.zeros((8, 128), F32) for _ in range(2)]
        above = [jnp.zeros((8, 128), F32) for _ in range(2)]
        for m in range(NY):
            for h in range(2):
                cols = slice(128 * h, 128 * (h + 1))
                plus, minus = ym[step, m, 0:8, cols], ym[step, m, 8:16, cols]
                below[h] = below[h] + yw[m, 0] * plus + yw[m, 1] * minus
                above[h] = above[h] + yw[m, 2] * plus + yw[m, 3] * minus
        for h in range(2):
            zm[step, kz, 16 + 16 * h : 24 + 16 * h, :] = below[h]
            zm[step, kz, 24 + 16 * h : 32 + 16 * h, :] = above[h]
        z_waves = []
        for shift in range(1, NZ):
            z_waves.append(
                sent(
                    zm.at[step, kz],
                    zm.at[step, kz],
                    zms_sem.at[step, shift],
                    zmr_sem.at[step, shift],
                    "gz",
                    around(kz, shift, NZ),
                )
            )
            z_waves[-1].start()
        leaving.extend(z_waves)
        for h in range(2):
            cols = slice(128 * h, 128 * (h + 1))
            turn[0:8, cols] = below[h]
            turn[8:16, cols] = above[h]
        columns = jnp.transpose(turn[...])
        for z in range(CZ):
            work[z] = (
                work[z]
                + lp[z] * waves[z : z + 1]
                + ln[z] * waves[z + 8 : z + 9]
                + columns[:, z : z + 1] * rowp[0, z : z + 1, :]
                + columns[:, z + 8 : z + 9] * rown[0, z : z + 1, :]
            )
        for copy in z_waves:
            copy.wait_recv()
        for m in range(NZ):
            for side in range(2):
                rhs[16 * m : 16 * m + 16, 128 * side : 128 * side + 128] = (
                    coef[m, side] * zm[step, m, 0:16, :]
                )
                mixed[64 + 16 * m : 80 + 16 * m, 128 * side : 128 * side + 128] = zm[
                    step, m, 16 + 16 * side : 32 + 16 * side, :
                ]
        hi, lo = halves(jnp.transpose(mixed[...]))
        rhi, rlo = halves(rhs[...])
        turn_in = (
            dot(jnp.concatenate([hi, lo], axis=1), jnp.concatenate([rhi, rhi], axis=0))
            + dot(hi, rlo)
        )

        last = step == STEPS - 1
        for c in range(NCH):
            rows = slice(CH * c, CH * (c + 1))
            padded = slice(PAD + CH * c, PAD + CH * (c + 1))
            downward_on(c).wait_recv()
            lower, upper = turn_in[rows, :CY], turn_in[rows, CY:]
            for buffer, least in ((zup, 1), (zdown, 3), (zfar, 2)):
                value = buffer[step, rows, :]
                lower = lower + jnp.where(kz >= least, value, 0.0)
                upper = upper + jnp.where(kz >= least, 0.0, value)
            run = lower
            for z in range(CZ):
                run = run + pq[1, base + z, 0:1, :] * work[z, rows, :]
                third[z, rows, :] = pq[0, base + z, 0:1, :] * run
            if not last:
                top = base + CZ
                upad[CZ + 1, padded, :] = (
                    upad[CZ + 1, padded, :]
                    + pq[0, top, 0:1, :] * run
                    + pq[1, top, 0:1, :] * upper
                )
            run = upper
            for z in range(CZ - 1, -1, -1):
                u = (
                    upad[z + 1, padded, :]
                    + third[z, rows, :]
                    + pq[1, base + z, 0:1, :] * run
                )
                run = run + pq[0, base + z, 0:1, :] * work[z, rows, :]
                if last:
                    third[z, rows, :] = u - u_ref[z, rows, :]
                else:
                    upad[z + 1, padded, :] = u
            if last:
                store = pltpu.make_async_copy(
                    third.at[:, pl.ds(CH * c, CH), :],
                    rise_hbm.at[:, pl.ds(CH * c, CH), :],
                    load_sem.at[c],
                )
                store.start()
                leaving_home.append(store)
            else:
                upad[0, padded, :] = (
                    upad[0, padded, :]
                    + pq[0, base - 1, 0:1, :] * lower
                    + pq[1, base - 1, 0:1, :] * run
                )
        if not last:
            edges = edges_out()

        for c in range(NCH):

            upward(c).wait_send()
            downward(c).wait_send()

            @pl.when(goes_up(c))
            def _():
                upward_on(c).wait_send()

            @pl.when(goes_down(c))
            def _():
                downward_on(c).wait_send()

    for copy in leaving:
        copy.wait_send()
    for copy in leaving_home:
        copy.wait()


def stepped(sheet, cond, scaling, u, kind, joule, z_edge, x_edge, y_edge):
    block = jax.ShapeDtypeStruct((CZ, CX, CY), F32)
    smem = pl.BlockSpec(memory_space=pltpu.SMEM)
    vmem = pl.BlockSpec(memory_space=pltpu.VMEM)
    dma = pltpu.SemaphoreType.DMA
    tall = pltpu.VMEM((CZ, CX, CY), F32)
    whole = pl.BlockSpec(memory_space=pl.ANY)
    return pl.pallas_call(
        adi_kernel,
        out_shape=block,
        in_specs=[smem] * 3 + [vmem] * 2 + [whole] * 4,
        out_specs=whole,
        scratch_shapes=[
            tall,
            pltpu.VMEM((CZ, CX, CY), jnp.int32),
            tall,
            pltpu.VMEM((CZ + 2, WIDE, CY), F32),
            pltpu.VMEM((CZ + 2, WIDE, CY), F32),
            tall,
            tall,
            tall,
            tall,
            pltpu.VMEM((CZ + 1, CX, CY), F32),
            tall,
            pltpu.VMEM((CZ, CX + 16, CX), BF16),
            pltpu.VMEM((CZ, CX + 16, CX), BF16),
            pltpu.VMEM((CZ, 2 * CY, 2 * CY), BF16),
            pltpu.VMEM((CZ, CY, 2 * CY), BF16),
            tall,
            tall,
            pltpu.VMEM((2, 8, 128), F32),
            pltpu.VMEM((2, 8, 128), F32),
            pltpu.VMEM((15, 8, 128), F32),
            pltpu.VMEM((NX, 4, 8, 128), F32),
            pltpu.VMEM((NY, 4, 8, 128), F32),
            pltpu.VMEM((2, PLANES + 2, 8, 128), F32),
            tall,
            tall,
            tall,
            pltpu.VMEM((CY, CX), F32),
            pltpu.VMEM((128, CX), F32),
            pltpu.VMEM((128, 2 * CY), F32),
            pltpu.VMEM((NZ, 2, 16, 128), F32),
            pltpu.VMEM((STEPS, NZ, 48, 128), F32),
            pltpu.VMEM((2, 8, CY), F32),
            pltpu.VMEM((2, 8, CY), F32),
            pltpu.VMEM((16, CX), F32),
            pltpu.VMEM((2, 16, CX), F32),
            pltpu.VMEM((STEPS, NX, 16, CY), F32),
            pltpu.VMEM((STEPS, NY, 16, CX), F32),
            pltpu.VMEM((STEPS, CX, CY), F32),
            pltpu.VMEM((STEPS, CX, CY), F32),
            pltpu.VMEM((STEPS, CX, CY), F32),
            pltpu.VMEM((STEPS, CX, CY), F32),
            pltpu.VMEM((STEPS, CX, CY), F32),
            dma((7,)),
            dma((2,)),
            dma((2,)),
            dma((2,)),
            dma((2,)),
            dma((STEPS, NX)),
            dma((STEPS, NX)),
            dma((STEPS, NY)),
            dma((STEPS, NY)),
            dma((STEPS, NZ)),
            dma((STEPS, NZ)),
            dma((STEPS, NCH)),
            dma((STEPS, NCH)),
            dma((STEPS, NCH)),
            dma((STEPS, NCH)),
            dma((STEPS, NCH)),
            dma((STEPS, NCH)),
            dma((STEPS, NCH)),
        ],
        compiler_params=pltpu.CompilerParams(
            collective_id=0, has_side_effects=True, vmem_limit_bytes=VMEM_BYTES
        ),
        name="steps",
    )(sheet, cond, scaling, x_edge, y_edge, u, kind, joule, z_edge)


def per_device(
    starting_warmth,
    sheet_stratum_number,
    stratum_heat_conduction,
    substance_kind,
    substance_kind_scaling,
    wire_piece_amperes,
    wire_piece_ohms_base,
    wire_piece_tile,
    wire_piece_voxel,
):
    shape = (SEGS // 128, 128)
    small = (sheet_stratum_number, stratum_heat_conduction, substance_kind_scaling)
    powers, columns, rows, *edges = spread_out(
        *small,
        wire_piece_amperes.reshape(shape),
        wire_piece_ohms_base.reshape(shape),
        wire_piece_tile.T,
        wire_piece_voxel.reshape(shape),
        starting_warmth,
        substance_kind,
    )
    joule = added(rows, powers, columns).reshape(CZ, CX, CY)
    rise = stepped(*small, starting_warmth, substance_kind, joule, *edges)
    warmed = starting_warmth + rise
    return warmed, (1.0 + WARMING_SLOPE * warmed) * joule


def solution(mesh):
    return jax.shard_map(
        per_device,
        mesh=mesh,
        in_specs=(
            P("gz", "gx", "gy"),
            P(),
            P(),
            P("gz", "gx", "gy"),
            P(),
            P(("gx", "gy", "gz")),
            P(("gx", "gy", "gz")),
            P(("gx", "gy", "gz"), None),
            P(("gx", "gy", "gz")),
        ),
        out_specs=(P("gz", "gx", "gy"), P("gz", "gx", "gy")),
        check_vma=False,
    )
```

```python
import functools

import jax
import jax.numpy as jnp
from jax import lax
from jax.experimental import pallas as pl
from jax.experimental.pallas import tpu as pltpu
from jax.sharding import PartitionSpec as P

STEPS = 2
HEAT_SPREADING = 1000.0
STIFF = 1.5
WARMING_SLOPE = 0.1
OHMIC_POWER = 8.0

F32 = jnp.float32
BF16 = jnp.bfloat16
MESH = pl.DeviceIdType.MESH

CZ, CX, CY = 8, 256, 128
LEN = 1024
PLANES = 32
NX, NY, NZ = 4, 8, 4
SEGS = 4096
TOP = 64
DEVS = 128
PAD = 8
WIDE = CX + 2 * PAD
NCH = 4
CH = CX // NCH
NACC = 8
DOUBLINGS = (8, 16, 32, 64, 128)
VMEM_BYTES = 60 * 1024 * 1024


def dot(a, b):
    return jnp.dot(a, b, preferred_element_type=F32)


def halves(x):
    high = x.astype(BF16)
    return high, (x - high.astype(F32)).astype(BF16)


def place_segments(amp_ref, ohm_ref, tile_ref, cell_ref, acc):
    width = 256
    row = lax.broadcasted_iota(jnp.int32, (width, width + DEVS), 0)
    col = lax.broadcasted_iota(jnp.int32, (width, width + DEVS), 1)
    before = jnp.where((row < col) | (col >= width), 1.0, 0.0).astype(BF16)
    owner = lax.broadcasted_iota(jnp.int32, (DEVS, width), 0)
    place = lax.broadcasted_iota(jnp.int32, (TOP, width), 0).astype(F32)
    acc[...] = jnp.zeros_like(acc)
    carry = jnp.zeros((DEVS, DEVS), F32)

    def line(ref, j):
        return jnp.concatenate([ref[2 * j : 2 * j + 1, :], ref[2 * j + 1 : 2 * j + 2, :]], axis=1)

    for j in range(SEGS // width):
        tile = tile_ref[:, width * j : width * (j + 1)]
        tile = ((tile & 3) << 5) + ((tile >> 5) << 3) + ((tile >> 2) & 7)
        mine = owner == tile
        hot = jnp.where(mine, 1.0, 0.0).astype(BF16)
        found = dot(hot, before)
        ahead = found[:, :width] + jnp.concatenate([carry, carry], axis=1)
        rank = jnp.sum(jnp.where(mine, ahead, 0.0), axis=0, keepdims=True)
        carry = carry + found[:, width:]
        amp = line(amp_ref, j)
        power = amp * amp * line(ohm_ref, j)
        p0 = power.astype(BF16).astype(F32)
        p1 = (power - p0).astype(BF16).astype(F32)
        p2 = power - p0 - p1
        cell = line(cell_ref, j)
        c0 = (cell >> 12).astype(F32)
        c1 = ((cell >> 6) & 63).astype(F32)
        c2 = (cell & 63).astype(F32)
        here = place == rank
        parts = jnp.concatenate(
            [jnp.where(here, part, 0.0).astype(BF16) for part in (p0, c0, p1, c1, p2, c2)], axis=0
        )
        acc[...] += lax.dot_general(
            hot, parts, (((1,), (1,)), ((), ())), preferred_element_type=F32
        )
    a, b, c = (acc[:, 128 * k : 128 * (k + 1)] for k in range(3))
    lane = lax.broadcasted_iota(jnp.int32, (DEVS, DEVS), 1)
    return jnp.where(lane < TOP, a + b + c, a * 4096.0 + b * 64.0 + c)


def around(me, shift, count):
    return lax.rem(me + shift + count, count)


def sent(src, dst, send, recv, axis, to):
    return pltpu.make_async_remote_copy(
        src_ref=src,
        dst_ref=dst,
        send_sem=send,
        recv_sem=recv,
        device_id={axis: to},
        device_id_type=MESH,
    )


def greet(places, beside=()):
    barrier = pltpu.get_barrier_semaphore()
    for axis, me, count in places:
        for shift in range(1, count):
            pl.semaphore_signal(
                barrier, inc=1, device_id={axis: around(me, shift, count)}, device_id_type=MESH
            )
    for to in beside:
        pl.semaphore_signal(barrier, inc=1, device_id=to, device_id_type=MESH)
    return barrier


def half_conductance(cond_ref, sheet_ref, scale_ref, kind, plane):
    here = (0.5 * HEAT_SPREADING) * cond_ref[sheet_ref[plane]]
    out = jnp.full(kind.shape, scale_ref[3] * here, F32)
    for category in range(3):
        out = jnp.where(kind == category, scale_ref[category] * here, out)
    return out


def edge_columns(planes):
    lane = lax.broadcasted_iota(jnp.int32, (CX, CY), 1)
    out = jnp.zeros((CX, CY), F32)
    for z, plane in enumerate(planes):
        out = jnp.where((lane >> 1) == z, pltpu.roll(plane, 2 * z + 1, 1), out)
    return jnp.transpose(out)[:16]


def spread_kernel(
    sheet_ref,
    cond_ref,
    scale_ref,
    amp_ref,
    ohm_ref,
    tile_ref,
    cell_ref,
    u_hbm,
    kind_hbm,
    power_ref,
    column_ref,
    row_ref,
    zr,
    xr,
    yr,
    c_hbm,
    u,
    kind,
    c,
    acc,
    one,
    three,
    four,
    five,
    zs,
    xs,
    ys,
    load_sem,
    one_send,
    one_recv,
    three_send,
    three_recv,
    zs_sem,
    zr_sem,
    xs_sem,
    xr_sem,
    ys_sem,
    yr_sem,
):
    kx, ky, kz = lax.axis_index("gx"), lax.axis_index("gy"), lax.axis_index("gz")
    slanted = [
        {"gx": around(kx, dx, NX), "gz": around(kz, dz, NZ)}
        for dz in range(1, NZ)
        for dx in range(1, NX)
    ]
    barrier = greet((("gx", kx, NX), ("gy", ky, NY), ("gz", kz, NZ)), slanted)
    loads = [
        pltpu.make_async_copy(u_hbm, u, load_sem.at[0]),
        pltpu.make_async_copy(kind_hbm, kind, load_sem.at[1]),
    ]
    for copy in loads:
        copy.start()
    one[...] = place_segments(amp_ref, ohm_ref, tile_ref, cell_ref, acc).reshape(
        NZ, NX, NY, DEVS
    )
    pl.semaphore_wait(barrier, NX * NZ + NY - 2)
    leaving = []

    copies = []
    for dz in range(NZ):
        for dx in range(NX):
            if dx or dz:
                tx, tz = around(kx, dx, NX), around(kz, dz, NZ)
                copies.append(
                    pltpu.make_async_remote_copy(
                        src_ref=one.at[tz, tx],
                        dst_ref=three.at[kz, kx],
                        send_sem=one_send.at[dz, dx],
                        recv_sem=one_recv.at[dz, dx],
                        device_id={"gx": tx, "gz": tz},
                        device_id_type=MESH,
                    )
                )
                copies[-1].start()
    leaving.extend(copies)
    three[kz, kx] = one[kz, kx]

    for copy in loads:
        copy.wait()
    for z in range(CZ):
        c[z] = half_conductance(cond_ref, sheet_ref, scale_ref, kind[z], CZ * kz + z)
    store = pltpu.make_async_copy(c, c_hbm, load_sem.at[2])
    store.start()
    for part, ref in ((0, u), (1, c)):
        zs[part, 0] = ref[CZ - 1]
        zs[part, 1] = ref[0]
        for side, to in ((0, 1), (1, -1)):
            leaving.append(
                sent(
                    zs.at[part, side],
                    zr.at[part, side],
                    zs_sem.at[part, side],
                    zr_sem.at[part, side],
                    "gz",
                    around(kz, to, NZ),
                )
            )
            leaving[-1].start()
    for part, ref in ((0, u), (1, c)):
        xs[0, pl.ds(8 * part, 8), :] = ref[:, CX - 1, :]
        xs[1, pl.ds(8 * part, 8), :] = ref[:, 0, :]
        ys[pl.ds(16 * part, 16), :] = edge_columns([ref[z] for z in range(CZ)])
    for side, to in ((0, 1), (1, -1)):
        leaving.append(
            sent(
                xs.at[side],
                xr.at[side],
                xs_sem.at[side],
                xr_sem.at[side],
                "gx",
                around(kx, to, NX),
            )
        )
        leaving.append(
            sent(ys, yr.at[side], ys_sem.at[side], yr_sem.at[side], "gy", around(ky, to, NY))
        )
    for copy in leaving[-4:]:
        copy.start()
    edges = leaving[-4:]
    for copy in copies:
        copy.wait_recv()
    for to in range(NY):
        four[to] = three[:, :, to, :].reshape(NX * NZ, DEVS)
    copies = []
    for shift in range(1, NY):
        to = around(ky, shift, NY)
        copies.append(
            sent(four.at[to], five.at[ky], three_send.at[shift], three_recv.at[shift], "gy", to)
        )
        copies[-1].start()
    leaving.extend(copies)
    five[ky] = four[ky]
    for copy in copies:
        copy.wait_recv()
    got = five[...].reshape(DEVS, DEVS)
    turned = pltpu.roll(got, TOP, 1)
    lane = lax.broadcasted_iota(jnp.int32, (DEVS // 2, DEVS), 1)
    left = lane < TOP
    power_ref[...] = jnp.where(left, got[: DEVS // 2], turned[DEVS // 2 :])
    cells = jnp.where(left, turned[: DEVS // 2], got[DEVS // 2 :]).astype(jnp.int32)
    column_ref[...] = cells & 127
    row_ref[...] = cells >> 7
    for part in range(2):
        for side, to in ((0, 1), (1, -1)):
            sent(
                zs.at[part, side],
                zr.at[part, side],
                zs_sem.at[part, side],
                zr_sem.at[part, side],
                "gz",
                around(kz, to, NZ),
            ).wait_recv()
    for copy in edges:
        copy.wait_recv()
    for copy in leaving:
        copy.wait_send()
    store.wait()


def spread_out(sheet, cond, scaling, amp, ohm, tile, cell, u, kind):
    smem = pl.BlockSpec(memory_space=pltpu.SMEM)
    vmem = pl.BlockSpec(memory_space=pltpu.VMEM)
    whole = pl.BlockSpec(memory_space=pl.ANY)
    dma = pltpu.SemaphoreType.DMA
    half = (DEVS // 2, DEVS)
    return pl.pallas_call(
        spread_kernel,
        out_shape=(
            jax.ShapeDtypeStruct(half, F32),
            jax.ShapeDtypeStruct(half, jnp.int32),
            jax.ShapeDtypeStruct(half, jnp.int32),
            jax.ShapeDtypeStruct((2, 2, CX, CY), F32),
            jax.ShapeDtypeStruct((2, 16, CY), F32),
            jax.ShapeDtypeStruct((2, 32, CX), F32),
            jax.ShapeDtypeStruct((CZ, CX, CY), F32),
        ),
        in_specs=[smem] * 3 + [vmem] * 4 + [whole] * 2,
        out_specs=(vmem,) * 6 + (whole,),
        scratch_shapes=[
            pltpu.VMEM((CZ, CX, CY), F32),
            pltpu.VMEM((CZ, CX, CY), jnp.int32),
            pltpu.VMEM((CZ, CX, CY), F32),
            pltpu.VMEM((DEVS, 384), F32),
            pltpu.VMEM((NZ, NX, NY, DEVS), F32),
            pltpu.VMEM((NZ, NX, NY, DEVS), F32),
            pltpu.VMEM((NY, NX * NZ, DEVS), F32),
            pltpu.VMEM((NY, NX * NZ, DEVS), F32),
            pltpu.VMEM((2, 2, CX, CY), F32),
            pltpu.VMEM((2, 16, CY), F32),
            pltpu.VMEM((32, CX), F32),
            dma((3,)),
            dma((NZ, NX)),
            dma((NZ, NX)),
            dma((NY,)),
            dma((NY,)),
            dma((2, 2)),
            dma((2, 2)),
            dma((2,)),
            dma((2,)),
            dma((2,)),
            dma((2,)),
        ],
        compiler_params=pltpu.CompilerParams(
            collective_id=1, has_side_effects=True, vmem_limit_bytes=VMEM_BYTES
        ),
        name="spread",
    )(sheet, cond, scaling, amp, ohm, tile, cell, u, kind)


def add_kernel(row_hbm, power_hbm, column_hbm, out_hbm, row_ref, power_ref, column_ref, spread, total, sem, *accs):
    loads = [
        pltpu.make_async_copy(src, dst, sem.at[k])
        for k, (src, dst) in enumerate(
            ((power_hbm, power_ref), (column_hbm, column_ref), (row_hbm, row_ref))
        )
    ]
    for copy in loads:
        copy.start()
    for acc in accs:
        acc[...] = jnp.zeros_like(acc)
    for copy in loads:
        copy.wait()
    sub = lax.broadcasted_iota(jnp.int32, (CY, 128), 0)
    for j in range(DEVS // 2):
        spread[128 * j : 128 * (j + 1), :] = jnp.transpose(
            jnp.where(sub == column_ref[j : j + 1, :], power_ref[j : j + 1, :], 0.0)
        )

    def some(i, carry):
        for k in range(128):
            acc = accs[k % NACC]
            acc[pl.ds(row_ref[i, k], 1), :] += spread[pl.ds(128 * i + k, 1), :]
        return carry

    lax.fori_loop(0, DEVS // 2, some, 0)
    stores = []
    for c in range(4):
        rows = pl.ds(CZ * CX // 4 * c, CZ * CX // 4)
        part = accs[0][rows, :]
        for acc in accs[1:]:
            part = part + acc[rows, :]
        total[rows, :] = part
        stores.append(pltpu.make_async_copy(total.at[rows, :], out_hbm.at[rows, :], sem.at[c]))
        stores[-1].start()
    for copy in stores:
        copy.wait()


def added(rows, powers, columns):
    whole = pl.BlockSpec(memory_space=pl.ANY)
    half = (DEVS // 2, DEVS)
    return pl.pallas_call(
        add_kernel,
        out_shape=jax.ShapeDtypeStruct((CZ * CX, CY), F32),
        in_specs=[whole] * 3,
        out_specs=whole,
        scratch_shapes=[
            pltpu.SMEM(half, jnp.int32),
            pltpu.VMEM(half, F32),
            pltpu.VMEM(half, jnp.int32),
            pltpu.VMEM((DEVS * TOP, 128), F32),
            pltpu.VMEM((CZ * CX, CY), F32),
            pltpu.SemaphoreType.DMA((4,)),
        ]
        + [pltpu.VMEM((CZ * CX, CY), F32)] * NACC,
        compiler_params=pltpu.CompilerParams(vmem_limit_bytes=VMEM_BYTES),
        name="add",
    )(rows, powers, columns)


def line_weights(theta, scale, me, count, length):
    whole = 2 * LEN
    out = []
    for m in range(count):

        def tile(exponent, keep):
            return jnp.where(keep, jnp.exp(-theta * exponent.astype(F32)) * scale, 0.0)

        lower, same = m < me, me == m
        gap = jnp.where(lower, me - m, m - me)
        near, far = length * (gap - 1) + 1, whole - length * gap - (length - 1)
        apart = jnp.logical_not(same)
        out.append(
            (
                tile(jnp.where(lower, near, far), apart),
                tile(length * (me + m) + 1, True),
                tile(whole - length * (me + m + 2) + 1, True),
                tile(jnp.where(lower, far, near), apart),
            )
        )
    return out


def adi_kernel(
    sheet_ref,
    cond_ref,
    x_edge,
    y_edge,
    u_hbm,
    c_hbm,
    joule_hbm,
    z_edge,
    rise_hbm,
    u_ref,
    joule_ref,
    upad,
    cpad,
    gxl,
    gxu,
    gyl,
    gyu,
    gz,
    gself,
    thi,
    tlo,
    y1,
    y2,
    lp,
    ln,
    rowp,
    rown,
    tables,
    xw,
    yw,
    pq,
    first,
    work,
    third,
    turn,
    mixed,
    rhs,
    coef,
    zm,
    xs,
    xr,
    ys,
    yr,
    xm,
    ym,
    yt,
    zup,
    zdown,
    zfar,
    sup,
    sdown,
    load_sem,
    xs_sem,
    xr_sem,
    ys_sem,
    yr_sem,
    xms_sem,
    xmr_sem,
    yms_sem,
    ymr_sem,
    yts_sem,
    ytr_sem,
    zms_sem,
    zmr_sem,
    ups_sem,
    upr_sem,
    dns_sem,
    dnr_sem,
    ons_sem,
    ond_sem,
    onr_sem,
):
    kx, ky, kz = lax.axis_index("gx"), lax.axis_index("gy"), lax.axis_index("gz")
    barrier = greet((("gx", kx, NX), ("gy", ky, NY), ("gz", kz, NZ)))
    inner = pl.ds(PAD, CX)
    loads = [
        pltpu.make_async_copy(src, dst, load_sem.at[k])
        for k, (src, dst) in enumerate(
            (
                (c_hbm, cpad.at[pl.ds(1, CZ), inner, :]),
                (u_hbm, upad.at[pl.ds(1, CZ), inner, :]),
                (z_edge.at[0, 0], upad.at[0, inner, :]),
                (z_edge.at[0, 1], upad.at[CZ + 1, inner, :]),
                (z_edge.at[1, 0], cpad.at[0, inner, :]),
                (z_edge.at[1, 1], cpad.at[CZ + 1, inner, :]),
                (joule_hbm, joule_ref),
                (u_hbm, u_ref),
            )
        )
    ]
    for copy in loads:
        copy.start()
    sub8 = lax.broadcasted_iota(jnp.int32, (8, 128), 0)
    lane8 = lax.broadcasted_iota(jnp.int32, (8, 128), 1)
    lane = lax.broadcasted_iota(jnp.int32, (CX, CY), 1)
    leaving = []
    leaving_home = []

    def edges_out():
        xs[0] = upad[1 : CZ + 1, PAD + CX - 1, :]
        xs[1] = upad[1 : CZ + 1, PAD, :]
        ys[...] = edge_columns([upad[z + 1, inner, :] for z in range(CZ)])
        copies = []
        for side, to in ((0, 1), (1, -1)):
            copies.append(
                sent(
                    xs.at[side],
                    xr.at[side],
                    xs_sem.at[side],
                    xr_sem.at[side],
                    "gx",
                    around(kx, to, NX),
                )
            )
            copies.append(
                sent(
                    ys, yr.at[side], ys_sem.at[side], yr_sem.at[side], "gy", around(ky, to, NY)
                )
            )
        for copy in copies:
            copy.start()
        leaving.extend(copies)
        return copies

    own = jnp.zeros((8, 128), F32)
    for z in range(CZ):
        own = jnp.where(sub8 == z, cond_ref[sheet_ref[CZ * kz + z]], own)

    def decay(plane_cond):
        a = HEAT_SPREADING * STIFF * plane_cond
        s = 0.5 * lax.rsqrt(a)
        s = 0.5 * (s + 0.25 / (a * s))
        s2 = s * s
        return a, 2.0 * s * (
            1.0 - s2 * (1.0 / 6.0 - s2 * (3.0 / 40.0 - s2 * (15.0 / 336.0)))
        )

    a, theta = decay(own)
    whole = jnp.exp(-theta * (2.0 * LEN))
    root = jnp.sqrt(a + 0.25)
    scale = 0.5 / (root * (1.0 - whole))
    tables[0] = theta
    tables[1] = scale
    tables[2] = scale * whole
    tables[3] = jnp.exp(-theta * (CX - 1.0))
    tables[4] = jnp.exp(-theta * (CY - 1.0))
    last_x, last_y = tables[3], tables[4]
    for k, hop in enumerate(DOUBLINGS):
        tables[5 + k] = jnp.exp(-theta * float(hop))
        tables[10 + k] = jnp.exp(theta * float(hop))
    for h in range(2):
        at = (lane8 + 128 * h).astype(F32)
        rowp[h] = jnp.exp(-theta * at)
        rown[h] = jnp.exp(theta * at)
    for m, tiles in enumerate(line_weights(theta, scale, kx, NX, CX)):
        for k, tile in enumerate(tiles):
            xw[m, k] = tile if k < 2 else tile * last_x
    for m, tiles in enumerate(line_weights(theta, scale, ky, NY, CY)):
        for k, tile in enumerate(tiles):
            yw[m, k] = tile if k < 2 else tile * last_y

    conds = [jnp.full((8, 128), cond_ref[sheet_ref[z]], F32) for z in range(PLANES)]
    stiff = HEAT_SPREADING * STIFF
    links = [0.5 * stiff * (conds[z] + conds[z + 1]) for z in range(PLANES - 1)]
    up = [1.0 + stiff * conds[0]]
    grow = [jnp.ones((8, 128), F32)]
    for z in range(PLANES - 1):
        grow.append(grow[z] * (1.0 + up[z] / links[z]))
        up.append(1.0 + links[z] * (up[z] / (up[z] + links[z])))
    down = [None] * PLANES
    down[-1] = jnp.ones((8, 128), F32)
    for z in range(PLANES - 2, -1, -1):
        down[z] = 1.0 + links[z] * (down[z + 1] / (down[z + 1] + links[z]))
    nothing = jnp.zeros((8, 128), F32)
    pq[0, 0] = nothing
    pq[1, 0] = nothing
    pq[0, PLANES + 1] = nothing
    pq[1, PLANES + 1] = nothing
    fade = [1.0 / ((up[z] + down[z] - 1.0) * grow[z]) for z in range(PLANES)]
    for z in range(PLANES):
        pq[0, z + 1] = fade[z]
        pq[1, z + 1] = grow[z]

    for m in range(NZ):
        cond, low, high = nothing, nothing, nothing
        for z in range(CZ):
            here = sub8 == z
            cond = jnp.where(here, conds[CZ * m + z], cond)
            low = jnp.where(here, grow[CZ * m + z], low)
            high = jnp.where(here, fade[CZ * m + z], high)
        _, th = decay(cond)
        low = jnp.where(m < kz, low, 0.0)
        high = jnp.where(m > kz, high, 0.0)
        for part in range(2):
            at = pl.ds(16 * m + 8 * part, 8)
            below_at = pl.ds(64 + 16 * m + 8 * part, 8)
            th = -th
            for h in range(2):
                wave = jnp.exp(th * (lane8 + 128 * h).astype(F32))
                mixed[at, pl.ds(128 * h, 128)] = wave
                if h == 0:
                    rhs[below_at, pl.ds(0, 128)] = low * wave
                    rhs[below_at, pl.ds(128, 128)] = high * wave
            coef[m, 0, pl.ds(8 * part, 8), :] = low
            coef[m, 1, pl.ds(8 * part, 8), :] = high

    sub16 = lax.broadcasted_iota(jnp.int32, (16, 128), 0)
    lane_y = lax.broadcasted_iota(jnp.int32, (CY, CY), 1)

    def weights(z, carry):
        one = pl.ds(z, 1)
        th = tables[0, one, :]
        fall = jnp.exp(-th * sub8.astype(F32))
        rise = jnp.exp(th * sub8.astype(F32))
        for k in range(len(DOUBLINGS)):
            fall = jnp.concatenate([fall, fall * tables[5 + k, one, :]], axis=0)
            rise = jnp.concatenate([rise, rise * tables[10 + k, one, :]], axis=0)
        lp[z] = fall
        ln[z] = rise
        c1, c2 = tables[1, one, :], tables[2, one, :]
        for h in range(2):
            x, y = fall * rown[h, one, :], rise * rowp[h, one, :]
            t = c1 * jnp.minimum(x, y) + c2 * jnp.maximum(x, y)
            cols = pl.ds(128 * h, 128)
            ends = jnp.where(
                sub16 == 0,
                tables[3, one, :] * rown[h, one, :],
                jnp.where(sub16 == 1, rowp[h, one, :], 0.0),
            )
            hi, lo = halves(t)
            thi[z, :CX, cols] = hi
            tlo[z, :CX, cols] = lo
            if h == 0:
                y1[z, :CY, :CY] = hi[:CY]
                y1[z, CY:, :CY] = hi[:CY]
                y2[z, :, :CY] = lo[:CY]
            hi, lo = halves(ends)
            thi[z, CX:, cols] = hi
            tlo[z, CX:, cols] = lo
        w = jnp.where(
            lane_y == z,
            rise[:CY] * tables[4, one, :],
            jnp.where(lane_y == z + 8, fall[:CY], 0.0),
        )
        hi, lo = halves(w)
        y1[z, :CY, CY:] = hi
        y1[z, CY:, CY:] = hi
        y2[z, :, CY:] = lo
        return carry

    lax.fori_loop(0, CZ, weights, 0)
    turn[...] = jnp.zeros_like(turn)

    def y_edges(low, high):
        odd = (lax.broadcasted_iota(jnp.int32, (16, CX), 0) & 1) == 1
        turn[:16, :] = jnp.where(odd, pltpu.roll(low, 1, 0), pltpu.roll(high, 15, 0))
        return jnp.transpose(turn[...])

    for copy in loads:
        copy.wait()
    cpad[1 : CZ + 1, PAD - 1, :] = jnp.where(
        kx == 0, -cpad[1 : CZ + 1, PAD, :], x_edge[0, 8:16, :]
    )
    cpad[1 : CZ + 1, PAD + CX, :] = jnp.where(
        kx == NX - 1, -cpad[1 : CZ + 1, PAD + CX - 1, :], x_edge[1, 8:16, :]
    )
    work[0] = y_edges(y_edge[0, 16:32, :], y_edge[1, 16:32, :])
    gz[0] = jnp.where(kz == 0, 0.0, (cpad[0, inner, :] + cpad[1, inner, :]))
    gz[CZ] = jnp.where(
        kz == NZ - 1, 0.0, (cpad[CZ, inner, :] + cpad[CZ + 1, inner, :])
    )
    for z in range(CZ - 1):
        gz[z + 1] = (cpad[z + 1, inner, :] + cpad[z + 2, inner, :])
    for z in range(CZ):
        c = cpad[z + 1, inner, :]
        edge = pltpu.roll(work[0], CY - (2 * z + 1), 1)
        low = jnp.where(lane == 0, jnp.where(ky == 0, -c, edge), pltpu.roll(c, 1, 1))
        high = jnp.where(
            lane == CY - 1, jnp.where(ky == NY - 1, -c, edge), pltpu.roll(c, CY - 1, 1)
        )
        xl = (c + cpad[z + 1, PAD - 1 : PAD + CX - 1, :])
        xu = (c + cpad[z + 1, PAD + 1 : PAD + CX + 1, :])
        yl, yu = (c + low), (c + high)
        gxl[z], gxu[z], gyl[z], gyu[z] = xl, xu, yl, yu
        every = xl + xu + yl + yu + gz[z] + gz[z + 1]
        if z == 0:
            every = every + jnp.where(kz == 0, 2.0 * c, 0.0)
        gself[z] = (OHMIC_POWER * WARMING_SLOPE) * joule_ref[z] - every

    for step in range(STEPS):
        if step:
            for copy in edges:
                copy.wait_recv()
            x_low, x_high, y_low, y_high = xr[0], xr[1], yr[0], yr[1]
        else:
            x_low, x_high = x_edge[0, 0:8, :], x_edge[1, 0:8, :]
            y_low, y_high = y_edge[0, 0:16, :], y_edge[1, 0:16, :]
        upad[1 : CZ + 1, PAD - 1, :] = x_low
        upad[1 : CZ + 1, PAD + CX, :] = x_high
        work[0] = y_edges(y_low, y_high)

        def source_and_x(z, carry):
            u = upad[z + 1, inner, :]
            edge = pltpu.roll(work[0], CY - (2 * z + 1), 1)
            low = jnp.where(lane == 0, edge, pltpu.roll(u, 1, 1))
            high = jnp.where(lane == CY - 1, edge, pltpu.roll(u, CY - 1, 1))
            b = gself[z] * u + OHMIC_POWER * joule_ref[z]
            b = b + gyl[z] * low + gyu[z] * high
            b = b + gxl[z] * upad[z + 1, PAD - 1 : PAD + CX - 1, :]
            b = b + gxu[z] * upad[z + 1, PAD + 1 : PAD + CX + 1, :]
            b = b + gz[z] * upad[z, inner, :] + gz[z + 1] * upad[z + 2, inner, :]
            hi, lo = halves(b)
            r = dot(thi[z], jnp.concatenate([hi, lo], axis=1))
            r = r[:, :CY] + r[:, CY:] + dot(tlo[z], hi)
            first[z] = r[:CX]
            xm[step, kx, pl.ds(z, 1), :] = r[CX : CX + 1]
            xm[step, kx, pl.ds(z + 8, 1), :] = r[CX + 1 : CX + 2]
            return carry

        for z in range(CZ):
            source_and_x(z, 0)

        if not step:
            pl.semaphore_wait(barrier, NX + NY + NZ - 3)
        moments = []
        for shift in range(1, NX):
            moments.append(
                sent(
                    xm.at[step, kx],
                    xm.at[step, kx],
                    xms_sem.at[step, shift],
                    xmr_sem.at[step, shift],
                    "gx",
                    around(kx, shift, NX),
                )
            )
            moments[-1].start()
        leaving.extend(moments)
        x_moments = moments

        def to_all_gy(buffer, send, recv):
            copies = []
            for shift in range(1, NY):
                copies.append(
                    sent(
                        buffer.at[step, ky],
                        buffer.at[step, ky],
                        send.at[step, shift],
                        recv.at[step, shift],
                        "gy",
                        around(ky, shift, NY),
                    )
                )
                copies[-1].start()
            leaving.extend(copies)
            return copies

        ends = jnp.zeros((CX, CY), F32)
        for z in range(CZ):
            hi, lo = halves(first[z])
            r = dot(jnp.concatenate([hi, lo], axis=1), y1[z]) + dot(hi, y2[z])
            work[z] = r[:, :CY]
            ends = ends + r[:, CY:]
        ym[step, ky] = jnp.transpose(ends)[:16]
        y_moments = to_all_gy(ym, yms_sem, ymr_sem)
        base = CZ * kz + 1

        def hop(source, target, send, recv, to, c):
            at = pl.ds(CH * c, CH)
            return sent(
                source.at[step, at, :],
                target.at[step, at, :],
                send.at[step, c],
                recv.at[step, c],
                "gz",
                around(kz, to, NZ),
            )

        def upward(c):
            return hop(sup, zup, ups_sem, upr_sem, 1, c)

        def downward(c):
            return hop(sdown, zdown, dns_sem, dnr_sem, -1, c)

        def upward_on(c):
            return hop(zup, zfar, ons_sem, onr_sem, 1, c)

        def downward_on(c):
            return hop(zdown, zfar, ond_sem, onr_sem, -1, c)

        def goes_up(c):
            return (kz == 2) | (kz == (1 if c < NCH // 2 else 0))

        def goes_down(c):
            return (kz == 1) | (kz == (2 if c < NCH // 2 else 3))

        for c in range(NCH):
            rows = slice(CH * c, CH * (c + 1))
            w = jnp.zeros((CH, CY), F32)
            v = jnp.zeros((CH, CY), F32)
            for z in range(CZ):
                value = work[z, rows, :]
                w = w + pq[1, base + z, 0:1, :] * value
                v = v + pq[0, base + z, 0:1, :] * value
            sup[step, rows, :] = jnp.where(kz == NZ - 1, v, w)
            sdown[step, rows, :] = jnp.where(kz == 0, w, v)
            upward(c).start()
            downward(c).start()

        for copy in x_moments:
            copy.wait_recv()
        below = jnp.zeros((8, CY), F32)
        above = jnp.zeros((8, CY), F32)
        for m in range(NX):
            plus, minus = xm[step, m, 0:8, :], xm[step, m, 8:16, :]
            below = below + xw[m, 0] * plus + xw[m, 1] * minus
            above = above + xw[m, 2] * plus + xw[m, 3] * minus
        both = jnp.concatenate([below, above], axis=0)
        r = jnp.zeros((16, 2 * CY), F32)
        for z in range(CZ):
            hi, lo = halves(jnp.where((sub16 & 7) == z, both, 0.0))
            r = r + dot(jnp.concatenate([hi, lo], axis=1), y1[z]) + dot(hi, y2[z])
        waves = r[:, :CY]
        zm[step, kz, 0:16, :] = waves

        def taken(rows, shift):
            return jnp.sum(
                jnp.where(lane8 == sub8 + shift, rows, 0.0), axis=1, keepdims=True
            )

        tile = jnp.zeros((8, 128), F32)
        for part in range(2):
            tile = jnp.where(lane8 == 2 * part, taken(r[:8, CY:], 8 * part), tile)
            tile = jnp.where(lane8 == 2 * part + 1, taken(r[8:, CY:], 8 * part), tile)
        yt[step, ky] = tile
        y_tiles = to_all_gy(yt, yts_sem, ytr_sem)

        for c in range(NCH):
            upward(c).wait_recv()

            @pl.when(goes_up(c))
            def _():
                upward_on(c).start()

            downward(c).wait_recv()

            @pl.when(goes_down(c))
            def _():
                downward_on(c).start()

        for copy in y_moments + y_tiles:
            copy.wait_recv()
        added_by = [jnp.zeros((8, 128), F32) for _ in range(4)]
        for m in range(NY):
            for k in range(4):
                added_by[k] = added_by[k] + yw[m, k] * yt[step, m]
        below = [jnp.zeros((8, 128), F32) for _ in range(2)]
        above = [jnp.zeros((8, 128), F32) for _ in range(2)]
        for m in range(NY):
            for h in range(2):
                cols = slice(128 * h, 128 * (h + 1))
                plus, minus = ym[step, m, 0:8, cols], ym[step, m, 8:16, cols]
                below[h] = below[h] + yw[m, 0] * plus + yw[m, 1] * minus
                above[h] = above[h] + yw[m, 2] * plus + yw[m, 3] * minus
        for h in range(2):
            for values, k in ((below, 0), (above, 2)):
                plus, minus = added_by[k], added_by[k + 1]
                values[h] = (
                    values[h]
                    + rowp[h] * (plus[:, 0:1] + minus[:, 2:3])
                    + rown[h] * (plus[:, 1:2] + minus[:, 3:4])
                )
            zm[step, kz, 16 + 16 * h : 24 + 16 * h, :] = below[h]
            zm[step, kz, 24 + 16 * h : 32 + 16 * h, :] = above[h]
        z_waves = []
        for shift in range(1, NZ):
            z_waves.append(
                sent(
                    zm.at[step, kz],
                    zm.at[step, kz],
                    zms_sem.at[step, shift],
                    zmr_sem.at[step, shift],
                    "gz",
                    around(kz, shift, NZ),
                )
            )
            z_waves[-1].start()
        leaving.extend(z_waves)
        for h in range(2):
            cols = slice(128 * h, 128 * (h + 1))
            turn[0:8, cols] = below[h]
            turn[8:16, cols] = above[h]
        columns = jnp.transpose(turn[...])
        for z in range(CZ):
            work[z] = (
                work[z]
                + lp[z] * waves[z : z + 1]
                + ln[z] * waves[z + 8 : z + 9]
                + columns[:, z : z + 1] * rowp[0, z : z + 1, :]
                + columns[:, z + 8 : z + 9] * rown[0, z : z + 1, :]
            )
        for copy in z_waves:
            copy.wait_recv()
        for m in range(NZ):
            for side in range(2):
                rhs[16 * m : 16 * m + 16, 128 * side : 128 * side + 128] = (
                    coef[m, side] * zm[step, m, 0:16, :]
                )
                mixed[64 + 16 * m : 80 + 16 * m, 128 * side : 128 * side + 128] = zm[
                    step, m, 16 + 16 * side : 32 + 16 * side, :
                ]
        hi, lo = halves(jnp.transpose(mixed[...]))
        rhi, rlo = halves(rhs[...])
        turn_in = (
            dot(jnp.concatenate([hi, lo], axis=1), jnp.concatenate([rhi, rhi], axis=0))
            + dot(hi, rlo)
        )

        last = step == STEPS - 1
        for c in range(NCH):
            rows = slice(CH * c, CH * (c + 1))
            padded = slice(PAD + CH * c, PAD + CH * (c + 1))
            downward_on(c).wait_recv()
            lower, upper = turn_in[rows, :CY], turn_in[rows, CY:]
            for buffer, least in ((zup, 1), (zdown, 3), (zfar, 2)):
                value = buffer[step, rows, :]
                lower = lower + jnp.where(kz >= least, value, 0.0)
                upper = upper + jnp.where(kz >= least, 0.0, value)
            run = lower
            for z in range(CZ):
                run = run + pq[1, base + z, 0:1, :] * work[z, rows, :]
                third[z, rows, :] = pq[0, base + z, 0:1, :] * run
            if not last:
                top = base + CZ
                upad[CZ + 1, padded, :] = (
                    upad[CZ + 1, padded, :]
                    + pq[0, top, 0:1, :] * run
                    + pq[1, top, 0:1, :] * upper
                )
            run = upper
            for z in range(CZ - 1, -1, -1):
                u = (
                    upad[z + 1, padded, :]
                    + third[z, rows, :]
                    + pq[1, base + z, 0:1, :] * run
                )
                run = run + pq[0, base + z, 0:1, :] * work[z, rows, :]
                if last:
                    third[z, rows, :] = u - u_ref[z, rows, :]
                else:
                    upad[z + 1, padded, :] = u
            if last:
                store = pltpu.make_async_copy(
                    third.at[:, pl.ds(CH * c, CH), :],
                    rise_hbm.at[:, pl.ds(CH * c, CH), :],
                    load_sem.at[c],
                )
                store.start()
                leaving_home.append(store)
            else:
                upad[0, padded, :] = (
                    upad[0, padded, :]
                    + pq[0, base - 1, 0:1, :] * lower
                    + pq[1, base - 1, 0:1, :] * run
                )
        if not last:
            edges = edges_out()

        for c in range(NCH):

            upward(c).wait_send()
            downward(c).wait_send()

            @pl.when(goes_up(c))
            def _():
                upward_on(c).wait_send()

            @pl.when(goes_down(c))
            def _():
                downward_on(c).wait_send()

    for copy in leaving:
        copy.wait_send()
    for copy in leaving_home:
        copy.wait()


def stepped(sheet, cond, u, joule, z_edge, x_edge, y_edge, c):
    block = jax.ShapeDtypeStruct((CZ, CX, CY), F32)
    smem = pl.BlockSpec(memory_space=pltpu.SMEM)
    vmem = pl.BlockSpec(memory_space=pltpu.VMEM)
    dma = pltpu.SemaphoreType.DMA
    tall = pltpu.VMEM((CZ, CX, CY), F32)
    whole = pl.BlockSpec(memory_space=pl.ANY)
    return pl.pallas_call(
        adi_kernel,
        out_shape=block,
        in_specs=[smem] * 2 + [vmem] * 2 + [whole] * 4,
        out_specs=whole,
        scratch_shapes=[
            tall,
            tall,
            pltpu.VMEM((CZ + 2, WIDE, CY), F32),
            pltpu.VMEM((CZ + 2, WIDE, CY), F32),
            tall,
            tall,
            tall,
            tall,
            pltpu.VMEM((CZ + 1, CX, CY), F32),
            tall,
            pltpu.VMEM((CZ, CX + 16, CX), BF16),
            pltpu.VMEM((CZ, CX + 16, CX), BF16),
            pltpu.VMEM((CZ, 2 * CY, 2 * CY), BF16),
            pltpu.VMEM((CZ, CY, 2 * CY), BF16),
            tall,
            tall,
            pltpu.VMEM((2, 8, 128), F32),
            pltpu.VMEM((2, 8, 128), F32),
            pltpu.VMEM((15, 8, 128), F32),
            pltpu.VMEM((NX, 4, 8, 128), F32),
            pltpu.VMEM((NY, 4, 8, 128), F32),
            pltpu.VMEM((2, PLANES + 2, 8, 128), F32),
            tall,
            tall,
            tall,
            pltpu.VMEM((CY, CX), F32),
            pltpu.VMEM((128, CX), F32),
            pltpu.VMEM((128, 2 * CY), F32),
            pltpu.VMEM((NZ, 2, 16, 128), F32),
            pltpu.VMEM((STEPS, NZ, 48, 128), F32),
            pltpu.VMEM((2, 8, CY), F32),
            pltpu.VMEM((2, 8, CY), F32),
            pltpu.VMEM((16, CX), F32),
            pltpu.VMEM((2, 16, CX), F32),
            pltpu.VMEM((STEPS, NX, 16, CY), F32),
            pltpu.VMEM((STEPS, NY, 16, CX), F32),
            pltpu.VMEM((STEPS, NY, 8, 128), F32),
            pltpu.VMEM((STEPS, CX, CY), F32),
            pltpu.VMEM((STEPS, CX, CY), F32),
            pltpu.VMEM((STEPS, CX, CY), F32),
            pltpu.VMEM((STEPS, CX, CY), F32),
            pltpu.VMEM((STEPS, CX, CY), F32),
            dma((8,)),
            dma((2,)),
            dma((2,)),
            dma((2,)),
            dma((2,)),
            dma((STEPS, NX)),
            dma((STEPS, NX)),
            dma((STEPS, NY)),
            dma((STEPS, NY)),
            dma((STEPS, NY)),
            dma((STEPS, NY)),
            dma((STEPS, NZ)),
            dma((STEPS, NZ)),
            dma((STEPS, NCH)),
            dma((STEPS, NCH)),
            dma((STEPS, NCH)),
            dma((STEPS, NCH)),
            dma((STEPS, NCH)),
            dma((STEPS, NCH)),
            dma((STEPS, NCH)),
        ],
        compiler_params=pltpu.CompilerParams(
            collective_id=0, has_side_effects=True, vmem_limit_bytes=VMEM_BYTES
        ),
        name="steps",
    )(sheet, cond, x_edge, y_edge, u, c, joule, z_edge)


def per_device(
    starting_warmth,
    sheet_stratum_number,
    stratum_heat_conduction,
    substance_kind,
    substance_kind_scaling,
    wire_piece_amperes,
    wire_piece_ohms_base,
    wire_piece_tile,
    wire_piece_voxel,
):
    shape = (SEGS // 128, 128)
    small = (sheet_stratum_number, stratum_heat_conduction, substance_kind_scaling)
    powers, columns, rows, *edges = spread_out(
        *small,
        wire_piece_amperes.reshape(shape),
        wire_piece_ohms_base.reshape(shape),
        wire_piece_tile.T,
        wire_piece_voxel.reshape(shape),
        starting_warmth,
        substance_kind,
    )
    joule = added(rows, powers, columns).reshape(CZ, CX, CY)
    rise = stepped(*small[:2], starting_warmth, joule, *edges)
    warmed = starting_warmth + rise
    return warmed, (1.0 + WARMING_SLOPE * warmed) * joule


def solution(mesh):
    return jax.shard_map(
        per_device,
        mesh=mesh,
        in_specs=(
            P("gz", "gx", "gy"),
            P(),
            P(),
            P("gz", "gx", "gy"),
            P(),
            P(("gx", "gy", "gz")),
            P(("gx", "gy", "gz")),
            P(("gx", "gy", "gz"), None),
            P(("gx", "gy", "gz")),
        ),
        out_specs=(P("gz", "gx", "gy"), P("gz", "gx", "gy")),
        check_vma=False,
    )
```

```python
import functools

import jax
import jax.numpy as jnp
from jax import lax
from jax.experimental import pallas as pl
from jax.experimental.pallas import tpu as pltpu
from jax.sharding import PartitionSpec as P

STEPS = 2
HEAT_SPREADING = 1000.0
STIFF = 1.5
WARMING_SLOPE = 0.1
OHMIC_POWER = 8.0

F32 = jnp.float32
BF16 = jnp.bfloat16
MESH = pl.DeviceIdType.MESH

CZ, CX, CY = 8, 256, 128
LEN = 1024
PLANES = 32
NX, NY, NZ = 4, 8, 4
SEGS = 4096
TOP = 64
DEVS = 128
PAD = 8
WIDE = CX + 2 * PAD
NCH = 4
CH = CX // NCH
NACC = 8
DOUBLINGS = (8, 16, 32, 64, 128)
VMEM_BYTES = 60 * 1024 * 1024


def dot(a, b):
    return jnp.dot(a, b, preferred_element_type=F32)


def halves(x):
    high = x.astype(BF16)
    return high, (x - high.astype(F32)).astype(BF16)


def place_segments(amp_ref, ohm_ref, tile_ref, cell_ref, acc):
    width = 256
    row = lax.broadcasted_iota(jnp.int32, (width, width + DEVS), 0)
    col = lax.broadcasted_iota(jnp.int32, (width, width + DEVS), 1)
    before = jnp.where((row < col) | (col >= width), 1.0, 0.0).astype(BF16)
    owner = lax.broadcasted_iota(jnp.int32, (DEVS, width), 0)
    place = lax.broadcasted_iota(jnp.int32, (TOP, width), 0).astype(F32)
    acc[...] = jnp.zeros_like(acc)
    carry = jnp.zeros((DEVS, DEVS), F32)

    def line(ref, j):
        return jnp.concatenate([ref[2 * j : 2 * j + 1, :], ref[2 * j + 1 : 2 * j + 2, :]], axis=1)

    for j in range(SEGS // width):
        tile = tile_ref[:, width * j : width * (j + 1)]
        tile = ((tile & 3) << 5) + ((tile >> 5) << 3) + ((tile >> 2) & 7)
        mine = owner == tile
        hot = jnp.where(mine, 1.0, 0.0).astype(BF16)
        found = dot(hot, before)
        ahead = found[:, :width] + jnp.concatenate([carry, carry], axis=1)
        rank = jnp.sum(jnp.where(mine, ahead, 0.0), axis=0, keepdims=True)
        carry = carry + found[:, width:]
        amp = line(amp_ref, j)
        power = amp * amp * line(ohm_ref, j)
        p0 = power.astype(BF16).astype(F32)
        p1 = (power - p0).astype(BF16).astype(F32)
        p2 = power - p0 - p1
        cell = line(cell_ref, j)
        c0 = (cell >> 12).astype(F32)
        c1 = ((cell >> 6) & 63).astype(F32)
        c2 = (cell & 63).astype(F32)
        here = place == rank
        parts = jnp.concatenate(
            [jnp.where(here, part, 0.0).astype(BF16) for part in (p0, c0, p1, c1, p2, c2)], axis=0
        )
        acc[...] += lax.dot_general(
            hot, parts, (((1,), (1,)), ((), ())), preferred_element_type=F32
        )
    a, b, c = (acc[:, 128 * k : 128 * (k + 1)] for k in range(3))
    lane = lax.broadcasted_iota(jnp.int32, (DEVS, DEVS), 1)
    return jnp.where(lane < TOP, a + b + c, a * 4096.0 + b * 64.0 + c)


def around(me, shift, count):
    return lax.rem(me + shift + count, count)


def sent(src, dst, send, recv, axis, to):
    return pltpu.make_async_remote_copy(
        src_ref=src,
        dst_ref=dst,
        send_sem=send,
        recv_sem=recv,
        device_id={axis: to},
        device_id_type=MESH,
    )


def greet(places, beside=()):
    barrier = pltpu.get_barrier_semaphore()
    for axis, me, count in places:
        for shift in range(1, count):
            pl.semaphore_signal(
                barrier, inc=1, device_id={axis: around(me, shift, count)}, device_id_type=MESH
            )
    for to in beside:
        pl.semaphore_signal(barrier, inc=1, device_id=to, device_id_type=MESH)
    return barrier


def half_conductance(cond_ref, sheet_ref, scale_ref, kind, plane):
    here = (0.5 * HEAT_SPREADING) * cond_ref[sheet_ref[plane]]
    out = jnp.full(kind.shape, scale_ref[3] * here, F32)
    for category in range(3):
        out = jnp.where(kind == category, scale_ref[category] * here, out)
    return out


def edge_columns(planes):
    lane = lax.broadcasted_iota(jnp.int32, (CX, CY), 1)
    out = jnp.zeros((CX, CY), F32)
    for z, plane in enumerate(planes):
        out = jnp.where((lane >> 1) == z, pltpu.roll(plane, 2 * z + 1, 1), out)
    return jnp.transpose(out)[:16]


def spread_kernel(
    sheet_ref,
    cond_ref,
    scale_ref,
    amp_ref,
    ohm_ref,
    tile_ref,
    cell_ref,
    u_hbm,
    kind_hbm,
    power_ref,
    column_ref,
    row_ref,
    zr,
    xr,
    yr,
    c_hbm,
    u,
    kind,
    c,
    acc,
    one,
    three,
    four,
    five,
    zs,
    xs,
    ys,
    load_sem,
    one_send,
    one_recv,
    three_send,
    three_recv,
    zs_sem,
    zr_sem,
    xs_sem,
    xr_sem,
    ys_sem,
    yr_sem,
):
    kx, ky, kz = lax.axis_index("gx"), lax.axis_index("gy"), lax.axis_index("gz")
    slanted = [
        {"gx": around(kx, dx, NX), "gz": around(kz, dz, NZ)}
        for dz in range(1, NZ)
        for dx in range(1, NX)
    ]
    barrier = greet((("gx", kx, NX), ("gy", ky, NY), ("gz", kz, NZ)), slanted)
    loads = [
        pltpu.make_async_copy(u_hbm, u, load_sem.at[0]),
        pltpu.make_async_copy(kind_hbm, kind, load_sem.at[1]),
    ]
    for copy in loads:
        copy.start()
    one[...] = place_segments(amp_ref, ohm_ref, tile_ref, cell_ref, acc).reshape(
        NZ, NX, NY, DEVS
    )
    pl.semaphore_wait(barrier, NX * NZ + NY - 2)
    leaving = []

    copies = []
    for dz in range(NZ):
        for dx in range(NX):
            if dx or dz:
                tx, tz = around(kx, dx, NX), around(kz, dz, NZ)
                copies.append(
                    pltpu.make_async_remote_copy(
                        src_ref=one.at[tz, tx],
                        dst_ref=three.at[kz, kx],
                        send_sem=one_send.at[dz, dx],
                        recv_sem=one_recv.at[dz, dx],
                        device_id={"gx": tx, "gz": tz},
                        device_id_type=MESH,
                    )
                )
                copies[-1].start()
    leaving.extend(copies)
    three[kz, kx] = one[kz, kx]

    for copy in loads:
        copy.wait()
    for z in range(CZ):
        c[z] = half_conductance(cond_ref, sheet_ref, scale_ref, kind[z], CZ * kz + z)
    store = pltpu.make_async_copy(c, c_hbm, load_sem.at[2])
    store.start()
    for part, ref in ((0, u), (1, c)):
        zs[part, 0] = ref[CZ - 1]
        zs[part, 1] = ref[0]
        for side, to in ((0, 1), (1, -1)):
            leaving.append(
                sent(
                    zs.at[part, side],
                    zr.at[part, side],
                    zs_sem.at[part, side],
                    zr_sem.at[part, side],
                    "gz",
                    around(kz, to, NZ),
                )
            )
            leaving[-1].start()
    for part, ref in ((0, u), (1, c)):
        xs[0, pl.ds(8 * part, 8), :] = ref[:, CX - 1, :]
        xs[1, pl.ds(8 * part, 8), :] = ref[:, 0, :]
        ys[pl.ds(16 * part, 16), :] = edge_columns([ref[z] for z in range(CZ)])
    for side, to in ((0, 1), (1, -1)):
        leaving.append(
            sent(
                xs.at[side],
                xr.at[side],
                xs_sem.at[side],
                xr_sem.at[side],
                "gx",
                around(kx, to, NX),
            )
        )
        leaving.append(
            sent(ys, yr.at[side], ys_sem.at[side], yr_sem.at[side], "gy", around(ky, to, NY))
        )
    for copy in leaving[-4:]:
        copy.start()
    edges = leaving[-4:]
    for copy in copies:
        copy.wait_recv()
    for to in range(NY):
        four[to] = three[:, :, to, :].reshape(NX * NZ, DEVS)
    copies = []
    for shift in range(1, NY):
        to = around(ky, shift, NY)
        copies.append(
            sent(four.at[to], five.at[ky], three_send.at[shift], three_recv.at[shift], "gy", to)
        )
        copies[-1].start()
    leaving.extend(copies)
    five[ky] = four[ky]
    for copy in copies:
        copy.wait_recv()
    got = five[...].reshape(DEVS, DEVS)
    turned = pltpu.roll(got, TOP, 1)
    lane = lax.broadcasted_iota(jnp.int32, (DEVS // 2, DEVS), 1)
    left = lane < TOP
    power_ref[...] = jnp.where(left, got[: DEVS // 2], turned[DEVS // 2 :])
    cells = jnp.where(left, turned[: DEVS // 2], got[DEVS // 2 :]).astype(jnp.int32)
    column_ref[...] = cells & 127
    row_ref[...] = cells >> 7
    for part in range(2):
        for side, to in ((0, 1), (1, -1)):
            sent(
                zs.at[part, side],
                zr.at[part, side],
                zs_sem.at[part, side],
                zr_sem.at[part, side],
                "gz",
                around(kz, to, NZ),
            ).wait_recv()
    for copy in edges:
        copy.wait_recv()
    for copy in leaving:
        copy.wait_send()
    store.wait()


def spread_out(sheet, cond, scaling, amp, ohm, tile, cell, u, kind):
    smem = pl.BlockSpec(memory_space=pltpu.SMEM)
    vmem = pl.BlockSpec(memory_space=pltpu.VMEM)
    whole = pl.BlockSpec(memory_space=pl.ANY)
    dma = pltpu.SemaphoreType.DMA
    half = (DEVS // 2, DEVS)
    return pl.pallas_call(
        spread_kernel,
        out_shape=(
            jax.ShapeDtypeStruct(half, F32),
            jax.ShapeDtypeStruct(half, jnp.int32),
            jax.ShapeDtypeStruct(half, jnp.int32),
            jax.ShapeDtypeStruct((2, 2, CX, CY), F32),
            jax.ShapeDtypeStruct((2, 16, CY), F32),
            jax.ShapeDtypeStruct((2, 32, CX), F32),
            jax.ShapeDtypeStruct((CZ, CX, CY), F32),
        ),
        in_specs=[smem] * 3 + [vmem] * 4 + [whole] * 2,
        out_specs=(vmem,) * 6 + (whole,),
        scratch_shapes=[
            pltpu.VMEM((CZ, CX, CY), F32),
            pltpu.VMEM((CZ, CX, CY), jnp.int32),
            pltpu.VMEM((CZ, CX, CY), F32),
            pltpu.VMEM((DEVS, 384), F32),
            pltpu.VMEM((NZ, NX, NY, DEVS), F32),
            pltpu.VMEM((NZ, NX, NY, DEVS), F32),
            pltpu.VMEM((NY, NX * NZ, DEVS), F32),
            pltpu.VMEM((NY, NX * NZ, DEVS), F32),
            pltpu.VMEM((2, 2, CX, CY), F32),
            pltpu.VMEM((2, 16, CY), F32),
            pltpu.VMEM((32, CX), F32),
            dma((3,)),
            dma((NZ, NX)),
            dma((NZ, NX)),
            dma((NY,)),
            dma((NY,)),
            dma((2, 2)),
            dma((2, 2)),
            dma((2,)),
            dma((2,)),
            dma((2,)),
            dma((2,)),
        ],
        compiler_params=pltpu.CompilerParams(
            collective_id=1, has_side_effects=True, vmem_limit_bytes=VMEM_BYTES
        ),
        name="spread",
    )(sheet, cond, scaling, amp, ohm, tile, cell, u, kind)


def add_kernel(row_hbm, power_hbm, column_hbm, out_hbm, row_ref, power_ref, column_ref, spread, total, sem, *accs):
    loads = [
        pltpu.make_async_copy(src, dst, sem.at[k])
        for k, (src, dst) in enumerate(
            ((power_hbm, power_ref), (column_hbm, column_ref), (row_hbm, row_ref))
        )
    ]
    for copy in loads:
        copy.start()
    for acc in accs:
        acc[...] = jnp.zeros_like(acc)
    for copy in loads:
        copy.wait()
    sub = lax.broadcasted_iota(jnp.int32, (CY, 128), 0)
    for j in range(DEVS // 2):
        spread[128 * j : 128 * (j + 1), :] = jnp.transpose(
            jnp.where(sub == column_ref[j : j + 1, :], power_ref[j : j + 1, :], 0.0)
        )

    def some(i, carry):
        for k in range(128):
            acc = accs[k % NACC]
            acc[pl.ds(row_ref[i, k], 1), :] += spread[pl.ds(128 * i + k, 1), :]
        return carry

    lax.fori_loop(0, DEVS // 2, some, 0)
    stores = []
    for c in range(4):
        rows = pl.ds(CZ * CX // 4 * c, CZ * CX // 4)
        part = accs[0][rows, :]
        for acc in accs[1:]:
            part = part + acc[rows, :]
        total[rows, :] = part
        stores.append(pltpu.make_async_copy(total.at[rows, :], out_hbm.at[rows, :], sem.at[c]))
        stores[-1].start()
    for copy in stores:
        copy.wait()


def added(rows, powers, columns):
    whole = pl.BlockSpec(memory_space=pl.ANY)
    half = (DEVS // 2, DEVS)
    return pl.pallas_call(
        add_kernel,
        out_shape=jax.ShapeDtypeStruct((CZ * CX, CY), F32),
        in_specs=[whole] * 3,
        out_specs=whole,
        scratch_shapes=[
            pltpu.SMEM(half, jnp.int32),
            pltpu.VMEM(half, F32),
            pltpu.VMEM(half, jnp.int32),
            pltpu.VMEM((DEVS * TOP, 128), F32),
            pltpu.VMEM((CZ * CX, CY), F32),
            pltpu.SemaphoreType.DMA((4,)),
        ]
        + [pltpu.VMEM((CZ * CX, CY), F32)] * NACC,
        compiler_params=pltpu.CompilerParams(vmem_limit_bytes=VMEM_BYTES),
        name="add",
    )(rows, powers, columns)


def line_weights(theta, scale, me, count, length):
    whole = 2 * LEN
    out = []
    for m in range(count):

        def tile(exponent, keep):
            return jnp.where(keep, jnp.exp(-theta * exponent.astype(F32)) * scale, 0.0)

        lower, same = m < me, me == m
        gap = jnp.where(lower, me - m, m - me)
        near, far = length * (gap - 1) + 1, whole - length * gap - (length - 1)
        apart = jnp.logical_not(same)
        out.append(
            (
                tile(jnp.where(lower, near, far), apart),
                tile(length * (me + m) + 1, True),
                tile(whole - length * (me + m + 2) + 1, True),
                tile(jnp.where(lower, far, near), apart),
            )
        )
    return out


def adi_kernel(
    sheet_ref,
    cond_ref,
    x_edge,
    y_edge,
    u_hbm,
    c_hbm,
    joule_hbm,
    z_edge,
    rise_hbm,
    rise,
    joule_ref,
    upad,
    cpad,
    gxl,
    gxu,
    gyl,
    gyu,
    gye,
    gz,
    gself,
    thi,
    tlo,
    y1,
    y2,
    lp,
    ln,
    rowp,
    rown,
    tables,
    xw,
    yw,
    pq,
    first,
    work,
    third,
    turn,
    mixed,
    rhs,
    coef,
    zm,
    xs,
    xr,
    ys,
    yr,
    xm,
    ym,
    yt,
    zup,
    zdown,
    zfar,
    sup,
    sdown,
    load_sem,
    xs_sem,
    xr_sem,
    ys_sem,
    yr_sem,
    xms_sem,
    xmr_sem,
    yms_sem,
    ymr_sem,
    yts_sem,
    ytr_sem,
    zms_sem,
    zmr_sem,
    ups_sem,
    upr_sem,
    dns_sem,
    dnr_sem,
    ons_sem,
    ond_sem,
    onr_sem,
):
    kx, ky, kz = lax.axis_index("gx"), lax.axis_index("gy"), lax.axis_index("gz")
    barrier = greet((("gx", kx, NX), ("gy", ky, NY), ("gz", kz, NZ)))
    inner = pl.ds(PAD, CX)
    loads = [
        pltpu.make_async_copy(src, dst, load_sem.at[k])
        for k, (src, dst) in enumerate(
            (
                (c_hbm, cpad.at[pl.ds(1, CZ), inner, :]),
                (u_hbm, upad.at[pl.ds(1, CZ), inner, :]),
                (z_edge.at[0, 0], upad.at[0, inner, :]),
                (z_edge.at[0, 1], upad.at[CZ + 1, inner, :]),
                (z_edge.at[1, 0], cpad.at[0, inner, :]),
                (z_edge.at[1, 1], cpad.at[CZ + 1, inner, :]),
                (joule_hbm, joule_ref),
            )
        )
    ]
    for copy in loads:
        copy.start()
    sub8 = lax.broadcasted_iota(jnp.int32, (8, 128), 0)
    lane8 = lax.broadcasted_iota(jnp.int32, (8, 128), 1)
    lane = lax.broadcasted_iota(jnp.int32, (CX, CY), 1)
    leaving = []
    leaving_home = []

    def edges_out():
        xs[0] = upad[1 : CZ + 1, PAD + CX - 1, :]
        xs[1] = upad[1 : CZ + 1, PAD, :]
        ys[...] = jnp.transpose(first[0])[:16]
        copies = []
        for side, to in ((0, 1), (1, -1)):
            copies.append(
                sent(
                    xs.at[side],
                    xr.at[side],
                    xs_sem.at[side],
                    xr_sem.at[side],
                    "gx",
                    around(kx, to, NX),
                )
            )
            copies.append(
                sent(
                    ys, yr.at[side], ys_sem.at[side], yr_sem.at[side], "gy", around(ky, to, NY)
                )
            )
        for copy in copies:
            copy.start()
        leaving.extend(copies)
        return copies

    own = jnp.zeros((8, 128), F32)
    for z in range(CZ):
        own = jnp.where(sub8 == z, cond_ref[sheet_ref[CZ * kz + z]], own)

    def decay(plane_cond):
        a = HEAT_SPREADING * STIFF * plane_cond
        s = 0.5 * lax.rsqrt(a)
        s = 0.5 * (s + 0.25 / (a * s))
        s2 = s * s
        return a, 2.0 * s * (
            1.0 - s2 * (1.0 / 6.0 - s2 * (3.0 / 40.0 - s2 * (15.0 / 336.0)))
        )

    a, theta = decay(own)
    whole = jnp.exp(-theta * (2.0 * LEN))
    root = jnp.sqrt(a + 0.25)
    scale = 0.5 / (root * (1.0 - whole))
    tables[0] = theta
    tables[1] = scale
    tables[2] = scale * whole
    tables[3] = jnp.exp(-theta * (CX - 1.0))
    tables[4] = jnp.exp(-theta * (CY - 1.0))
    last_x, last_y = tables[3], tables[4]
    for k, hop in enumerate(DOUBLINGS):
        tables[5 + k] = jnp.exp(-theta * float(hop))
        tables[10 + k] = jnp.exp(theta * float(hop))
    for h in range(2):
        at = (lane8 + 128 * h).astype(F32)
        rowp[h] = jnp.exp(-theta * at)
        rown[h] = jnp.exp(theta * at)
    for m, tiles in enumerate(line_weights(theta, scale, kx, NX, CX)):
        for k, tile in enumerate(tiles):
            xw[m, k] = tile if k < 2 else tile * last_x
    for m, tiles in enumerate(line_weights(theta, scale, ky, NY, CY)):
        for k, tile in enumerate(tiles):
            yw[m, k] = tile if k < 2 else tile * last_y

    conds = [jnp.full((8, 128), cond_ref[sheet_ref[z]], F32) for z in range(PLANES)]
    stiff = HEAT_SPREADING * STIFF
    links = [0.5 * stiff * (conds[z] + conds[z + 1]) for z in range(PLANES - 1)]
    up = [1.0 + stiff * conds[0]]
    grow = [jnp.ones((8, 128), F32)]
    for z in range(PLANES - 1):
        grow.append(grow[z] * (1.0 + up[z] / links[z]))
        up.append(1.0 + links[z] * (up[z] / (up[z] + links[z])))
    down = [None] * PLANES
    down[-1] = jnp.ones((8, 128), F32)
    for z in range(PLANES - 2, -1, -1):
        down[z] = 1.0 + links[z] * (down[z + 1] / (down[z + 1] + links[z]))
    nothing = jnp.zeros((8, 128), F32)
    pq[0, 0] = nothing
    pq[1, 0] = nothing
    pq[0, PLANES + 1] = nothing
    pq[1, PLANES + 1] = nothing
    fade = [1.0 / ((up[z] + down[z] - 1.0) * grow[z]) for z in range(PLANES)]
    for z in range(PLANES):
        pq[0, z + 1] = fade[z]
        pq[1, z + 1] = grow[z]

    for m in range(NZ):
        cond, low, high = nothing, nothing, nothing
        for z in range(CZ):
            here = sub8 == z
            cond = jnp.where(here, conds[CZ * m + z], cond)
            low = jnp.where(here, grow[CZ * m + z], low)
            high = jnp.where(here, fade[CZ * m + z], high)
        _, th = decay(cond)
        low = jnp.where(m < kz, low, 0.0)
        high = jnp.where(m > kz, high, 0.0)
        for part in range(2):
            at = pl.ds(16 * m + 8 * part, 8)
            below_at = pl.ds(64 + 16 * m + 8 * part, 8)
            th = -th
            for h in range(2):
                wave = jnp.exp(th * (lane8 + 128 * h).astype(F32))
                mixed[at, pl.ds(128 * h, 128)] = wave
                if h == 0:
                    rhs[below_at, pl.ds(0, 128)] = low * wave
                    rhs[below_at, pl.ds(128, 128)] = high * wave
            coef[m, 0, pl.ds(8 * part, 8), :] = low
            coef[m, 1, pl.ds(8 * part, 8), :] = high

    sub16 = lax.broadcasted_iota(jnp.int32, (16, 128), 0)
    lane_y = lax.broadcasted_iota(jnp.int32, (CY, CY), 1)

    def weights(z, carry):
        one = pl.ds(z, 1)
        th = tables[0, one, :]
        fall = jnp.exp(-th * sub8.astype(F32))
        rise = jnp.exp(th * sub8.astype(F32))
        for k in range(len(DOUBLINGS)):
            fall = jnp.concatenate([fall, fall * tables[5 + k, one, :]], axis=0)
            rise = jnp.concatenate([rise, rise * tables[10 + k, one, :]], axis=0)
        lp[z] = fall
        ln[z] = rise
        c1, c2 = tables[1, one, :], tables[2, one, :]
        for h in range(2):
            x, y = fall * rown[h, one, :], rise * rowp[h, one, :]
            t = c1 * jnp.minimum(x, y) + c2 * jnp.maximum(x, y)
            cols = pl.ds(128 * h, 128)
            hi, lo = halves(t)
            thi[z, :, cols] = hi
            tlo[z, :, cols] = lo
            if h == 0:
                y1[z, :CY, :CY] = hi[:CY]
                y1[z, CY:, :CY] = hi[:CY]
                y2[z, :, :CY] = lo[:CY]
        w = jnp.where(
            lane_y == z,
            rise[:CY] * tables[4, one, :],
            jnp.where(lane_y == z + 8, fall[:CY], 0.0),
        )
        hi, lo = halves(w)
        y1[z, :CY, CY:] = hi
        y1[z, CY:, CY:] = hi
        y2[z, :, CY:] = lo
        return carry

    lax.fori_loop(0, CZ, weights, 0)
    turn[...] = jnp.zeros_like(turn)

    def y_edges(low, high):
        odd = (lax.broadcasted_iota(jnp.int32, (16, CX), 0) & 1) == 1
        turn[:16, :] = jnp.where(odd, pltpu.roll(low, 1, 0), pltpu.roll(high, 15, 0))
        return jnp.transpose(turn[...])

    for copy in loads:
        copy.wait()
    cpad[1 : CZ + 1, PAD - 1, :] = jnp.where(
        kx == 0, -cpad[1 : CZ + 1, PAD, :], x_edge[0, 8:16, :]
    )
    cpad[1 : CZ + 1, PAD + CX, :] = jnp.where(
        kx == NX - 1, -cpad[1 : CZ + 1, PAD + CX - 1, :], x_edge[1, 8:16, :]
    )
    work[0] = y_edges(y_edge[0, 16:32, :], y_edge[1, 16:32, :])
    gz[0] = jnp.where(kz == 0, 0.0, (cpad[0, inner, :] + cpad[1, inner, :]))
    gz[CZ] = jnp.where(
        kz == NZ - 1, 0.0, (cpad[CZ, inner, :] + cpad[CZ + 1, inner, :])
    )
    for z in range(CZ - 1):
        gz[z + 1] = (cpad[z + 1, inner, :] + cpad[z + 2, inner, :])
    for z in range(CZ):
        c = cpad[z + 1, inner, :]
        edge = pltpu.roll(work[0], CY - (2 * z + 1), 1)
        low = jnp.where(lane == 0, jnp.where(ky == 0, -c, edge), pltpu.roll(c, 1, 1))
        high = jnp.where(
            lane == CY - 1, jnp.where(ky == NY - 1, -c, edge), pltpu.roll(c, CY - 1, 1)
        )
        xl = (c + cpad[z + 1, PAD - 1 : PAD + CX - 1, :])
        xu = (c + cpad[z + 1, PAD + 1 : PAD + CX + 1, :])
        yl, yu = (c + low), (c + high)
        gxl[z], gxu[z] = xl, xu
        gyl[z] = jnp.where(lane == 0, 0.0, yl)
        gyu[z] = jnp.where(lane == CY - 1, 0.0, yu)
        gye[z] = jnp.where(lane == 0, yl, jnp.where(lane == CY - 1, yu, 0.0))
        every = xl + xu + yl + yu + gz[z] + gz[z + 1]
        if z == 0:
            every = every + jnp.where(kz == 0, 2.0 * c, 0.0)
        gself[z] = (OHMIC_POWER * WARMING_SLOPE) * joule_ref[z] - every

    upad[1 : CZ + 1, PAD - 1, :] = jnp.zeros((8, CY), F32)
    upad[1 : CZ + 1, PAD + CX, :] = jnp.zeros((8, CY), F32)
    for step in range(STEPS):
        for z in range(CZ):
            u = upad[z + 1, inner, :]
            b = gself[z] * u + OHMIC_POWER * joule_ref[z]
            b = b + gyl[z] * pltpu.roll(u, 1, 1) + gyu[z] * pltpu.roll(u, CY - 1, 1)
            b = b + gxl[z] * upad[z + 1, PAD - 1 : PAD + CX - 1, :]
            b = b + gxu[z] * upad[z + 1, PAD + 1 : PAD + CX + 1, :]
            first[z] = b + gz[z] * upad[z, inner, :] + gz[z + 1] * upad[z + 2, inner, :]
        if step:
            for copy in edges:
                copy.wait_recv()
            x_low, x_high, y_low, y_high = xr[0], xr[1], yr[0], yr[1]
        else:
            x_low, x_high = x_edge[0, 0:8, :], x_edge[1, 0:8, :]
            y_low, y_high = y_edge[0, 0:16, :], y_edge[1, 0:16, :]
        first[:, 0, :] = first[:, 0, :] + gxl[:, 0, :] * x_low
        first[:, CX - 1, :] = first[:, CX - 1, :] + gxu[:, CX - 1, :] * x_high
        work[0] = y_edges(y_low, y_high)

        def folded(values):
            total = values[0:8]
            for at in range(8, CX, 8):
                total = total + values[at : at + 8]
            return jnp.sum(total, axis=0, keepdims=True)

        for z in range(CZ):
            b = first[z] + gye[z] * pltpu.roll(work[0], CY - (2 * z + 1), 1)
            first[z] = b
            xm[step, kx, z : z + 1, :] = folded(ln[z] * b) * tables[3, z : z + 1, :]
            xm[step, kx, z + 8 : z + 9, :] = folded(lp[z] * b)

        if not step:
            pl.semaphore_wait(barrier, NX + NY + NZ - 3)
        moments = []
        for shift in range(1, NX):
            moments.append(
                sent(
                    xm.at[step, kx],
                    xm.at[step, kx],
                    xms_sem.at[step, shift],
                    xmr_sem.at[step, shift],
                    "gx",
                    around(kx, shift, NX),
                )
            )
            moments[-1].start()
        leaving.extend(moments)
        x_moments = moments
        for z in range(CZ):
            hi, lo = halves(first[z])
            r = dot(thi[z], jnp.concatenate([hi, lo], axis=1))
            first[z] = r[:, :CY] + r[:, CY:] + dot(tlo[z], hi)

        def to_all_gy(buffer, send, recv):
            copies = []
            for shift in range(1, NY):
                copies.append(
                    sent(
                        buffer.at[step, ky],
                        buffer.at[step, ky],
                        send.at[step, shift],
                        recv.at[step, shift],
                        "gy",
                        around(ky, shift, NY),
                    )
                )
                copies[-1].start()
            leaving.extend(copies)
            return copies

        ends = jnp.zeros((CX, CY), F32)
        for z in range(CZ):
            hi, lo = halves(first[z])
            r = dot(jnp.concatenate([hi, lo], axis=1), y1[z]) + dot(hi, y2[z])
            work[z] = r[:, :CY]
            ends = ends + r[:, CY:]
        ym[step, ky] = jnp.transpose(ends)[:16]
        y_moments = to_all_gy(ym, yms_sem, ymr_sem)
        base = CZ * kz + 1

        def hop(source, target, send, recv, to, c):
            at = pl.ds(CH * c, CH)
            return sent(
                source.at[step, at, :],
                target.at[step, at, :],
                send.at[step, c],
                recv.at[step, c],
                "gz",
                around(kz, to, NZ),
            )

        def upward(c):
            return hop(sup, zup, ups_sem, upr_sem, 1, c)

        def downward(c):
            return hop(sdown, zdown, dns_sem, dnr_sem, -1, c)

        def upward_on(c):
            return hop(zup, zfar, ons_sem, onr_sem, 1, c)

        def downward_on(c):
            return hop(zdown, zfar, ond_sem, onr_sem, -1, c)

        def goes_up(c):
            return (kz == 2) | (kz == (1 if c < NCH // 2 else 0))

        def goes_down(c):
            return (kz == 1) | (kz == (2 if c < NCH // 2 else 3))

        for c in range(NCH):
            rows = slice(CH * c, CH * (c + 1))
            w = jnp.zeros((CH, CY), F32)
            v = jnp.zeros((CH, CY), F32)
            for z in range(CZ):
                value = work[z, rows, :]
                w = w + pq[1, base + z, 0:1, :] * value
                v = v + pq[0, base + z, 0:1, :] * value
            sup[step, rows, :] = jnp.where(kz == NZ - 1, v, w)
            sdown[step, rows, :] = jnp.where(kz == 0, w, v)
            upward(c).start()
            downward(c).start()

        for copy in x_moments:
            copy.wait_recv()
        below = jnp.zeros((8, CY), F32)
        above = jnp.zeros((8, CY), F32)
        for m in range(NX):
            plus, minus = xm[step, m, 0:8, :], xm[step, m, 8:16, :]
            below = below + xw[m, 0] * plus + xw[m, 1] * minus
            above = above + xw[m, 2] * plus + xw[m, 3] * minus
        tile = jnp.zeros((8, 128), F32)
        for part, weight in ((0, tables[4] * rown[0]), (1, rowp[0])):
            for k, rows in ((0, below), (1, above)):
                value = jnp.sum(weight * rows, axis=1, keepdims=True)
                tile = jnp.where(lane8 == 2 * part + k, value, tile)
        yt[step, ky] = tile
        y_tiles = to_all_gy(yt, yts_sem, ytr_sem)
        both = jnp.concatenate([below, above], axis=0)
        r = jnp.zeros((16, CY), F32)
        for z in range(CZ):
            hi, lo = halves(jnp.where((sub16 & 7) == z, both, 0.0))
            r = r + dot(jnp.concatenate([hi, lo], axis=1), y1[z, :, :CY]) + dot(hi, y2[z, :, :CY])
        waves = r
        zm[step, kz, 0:16, :] = waves

        for c in range(NCH):
            upward(c).wait_recv()

            @pl.when(goes_up(c))
            def _():
                upward_on(c).start()

            downward(c).wait_recv()

            @pl.when(goes_down(c))
            def _():
                downward_on(c).start()

        for copy in y_moments + y_tiles:
            copy.wait_recv()
        added_by = [jnp.zeros((8, 128), F32) for _ in range(4)]
        for m in range(NY):
            for k in range(4):
                added_by[k] = added_by[k] + yw[m, k] * yt[step, m]
        below = [jnp.zeros((8, 128), F32) for _ in range(2)]
        above = [jnp.zeros((8, 128), F32) for _ in range(2)]
        for m in range(NY):
            for h in range(2):
                cols = slice(128 * h, 128 * (h + 1))
                plus, minus = ym[step, m, 0:8, cols], ym[step, m, 8:16, cols]
                below[h] = below[h] + yw[m, 0] * plus + yw[m, 1] * minus
                above[h] = above[h] + yw[m, 2] * plus + yw[m, 3] * minus
        for h in range(2):
            for values, k in ((below, 0), (above, 2)):
                plus, minus = added_by[k], added_by[k + 1]
                values[h] = (
                    values[h]
                    + rowp[h] * (plus[:, 0:1] + minus[:, 2:3])
                    + rown[h] * (plus[:, 1:2] + minus[:, 3:4])
                )
            zm[step, kz, 16 + 16 * h : 24 + 16 * h, :] = below[h]
            zm[step, kz, 24 + 16 * h : 32 + 16 * h, :] = above[h]
        z_waves = []
        for shift in range(1, NZ):
            z_waves.append(
                sent(
                    zm.at[step, kz],
                    zm.at[step, kz],
                    zms_sem.at[step, shift],
                    zmr_sem.at[step, shift],
                    "gz",
                    around(kz, shift, NZ),
                )
            )
            z_waves[-1].start()
        leaving.extend(z_waves)
        for h in range(2):
            cols = slice(128 * h, 128 * (h + 1))
            turn[0:8, cols] = below[h]
            turn[8:16, cols] = above[h]
        columns = jnp.transpose(turn[...])
        for z in range(CZ):
            work[z] = (
                work[z]
                + lp[z] * waves[z : z + 1]
                + ln[z] * waves[z + 8 : z + 9]
                + columns[:, z : z + 1] * rowp[0, z : z + 1, :]
                + columns[:, z + 8 : z + 9] * rown[0, z : z + 1, :]
            )
        for copy in z_waves:
            copy.wait_recv()
        for m in range(NZ):
            for side in range(2):
                rhs[16 * m : 16 * m + 16, 128 * side : 128 * side + 128] = (
                    coef[m, side] * zm[step, m, 0:16, :]
                )
                mixed[64 + 16 * m : 80 + 16 * m, 128 * side : 128 * side + 128] = zm[
                    step, m, 16 + 16 * side : 32 + 16 * side, :
                ]
        hi, lo = halves(jnp.transpose(mixed[...]))
        rhi, rlo = halves(rhs[...])
        turn_in = (
            dot(jnp.concatenate([hi, lo], axis=1), jnp.concatenate([rhi, rhi], axis=0))
            + dot(hi, rlo)
        )

        last = step == STEPS - 1
        for c in range(NCH):
            rows = slice(CH * c, CH * (c + 1))
            padded = slice(PAD + CH * c, PAD + CH * (c + 1))
            downward_on(c).wait_recv()
            lower, upper = turn_in[rows, :CY], turn_in[rows, CY:]
            for buffer, least in ((zup, 1), (zdown, 3), (zfar, 2)):
                value = buffer[step, rows, :]
                lower = lower + jnp.where(kz >= least, value, 0.0)
                upper = upper + jnp.where(kz >= least, 0.0, value)
            run = lower
            for z in range(CZ):
                run = run + pq[1, base + z, 0:1, :] * work[z, rows, :]
                third[z, rows, :] = pq[0, base + z, 0:1, :] * run
            if not last:
                top = base + CZ
                upad[CZ + 1, padded, :] = (
                    upad[CZ + 1, padded, :]
                    + pq[0, top, 0:1, :] * run
                    + pq[1, top, 0:1, :] * upper
                )
            run = upper
            columns = jnp.zeros((CH, CY), F32)
            for z in range(CZ - 1, -1, -1):
                more = third[z, rows, :] + pq[1, base + z, 0:1, :] * run
                run = run + pq[0, base + z, 0:1, :] * work[z, rows, :]
                if last:
                    third[z, rows, :] = more + rise[z, rows, :]
                else:
                    rise[z, rows, :] = more
                    u = upad[z + 1, padded, :] + more
                    upad[z + 1, padded, :] = u
                    columns = jnp.where(
                        (lane[:CH] >> 1) == z, pltpu.roll(u, 2 * z + 1, 1), columns
                    )
            if last:
                store = pltpu.make_async_copy(
                    third.at[:, pl.ds(CH * c, CH), :],
                    rise_hbm.at[:, pl.ds(CH * c, CH), :],
                    load_sem.at[c],
                )
                store.start()
                leaving_home.append(store)
            else:
                first[0, rows, :] = columns
                upad[0, padded, :] = (
                    upad[0, padded, :]
                    + pq[0, base - 1, 0:1, :] * lower
                    + pq[1, base - 1, 0:1, :] * run
                )
        if not last:
            edges = edges_out()

        for c in range(NCH):

            upward(c).wait_send()
            downward(c).wait_send()

            @pl.when(goes_up(c))
            def _():
                upward_on(c).wait_send()

            @pl.when(goes_down(c))
            def _():
                downward_on(c).wait_send()

    for copy in leaving:
        copy.wait_send()
    for copy in leaving_home:
        copy.wait()


def stepped(sheet, cond, u, joule, z_edge, x_edge, y_edge, c):
    block = jax.ShapeDtypeStruct((CZ, CX, CY), F32)
    smem = pl.BlockSpec(memory_space=pltpu.SMEM)
    vmem = pl.BlockSpec(memory_space=pltpu.VMEM)
    dma = pltpu.SemaphoreType.DMA
    tall = pltpu.VMEM((CZ, CX, CY), F32)
    whole = pl.BlockSpec(memory_space=pl.ANY)
    return pl.pallas_call(
        adi_kernel,
        out_shape=block,
        in_specs=[smem] * 2 + [vmem] * 2 + [whole] * 4,
        out_specs=whole,
        scratch_shapes=[
            tall,
            tall,
            pltpu.VMEM((CZ + 2, WIDE, CY), F32),
            pltpu.VMEM((CZ + 2, WIDE, CY), F32),
            tall,
            tall,
            tall,
            tall,
            tall,
            pltpu.VMEM((CZ + 1, CX, CY), F32),
            tall,
            pltpu.VMEM((CZ, CX, CX), BF16),
            pltpu.VMEM((CZ, CX, CX), BF16),
            pltpu.VMEM((CZ, 2 * CY, 2 * CY), BF16),
            pltpu.VMEM((CZ, CY, 2 * CY), BF16),
            tall,
            tall,
            pltpu.VMEM((2, 8, 128), F32),
            pltpu.VMEM((2, 8, 128), F32),
            pltpu.VMEM((15, 8, 128), F32),
            pltpu.VMEM((NX, 4, 8, 128), F32),
            pltpu.VMEM((NY, 4, 8, 128), F32),
            pltpu.VMEM((2, PLANES + 2, 8, 128), F32),
            tall,
            tall,
            tall,
            pltpu.VMEM((CY, CX), F32),
            pltpu.VMEM((128, CX), F32),
            pltpu.VMEM((128, 2 * CY), F32),
            pltpu.VMEM((NZ, 2, 16, 128), F32),
            pltpu.VMEM((STEPS, NZ, 48, 128), F32),
            pltpu.VMEM((2, 8, CY), F32),
            pltpu.VMEM((2, 8, CY), F32),
            pltpu.VMEM((16, CX), F32),
            pltpu.VMEM((2, 16, CX), F32),
            pltpu.VMEM((STEPS, NX, 16, CY), F32),
            pltpu.VMEM((STEPS, NY, 16, CX), F32),
            pltpu.VMEM((STEPS, NY, 8, 128), F32),
            pltpu.VMEM((STEPS, CX, CY), F32),
            pltpu.VMEM((STEPS, CX, CY), F32),
            pltpu.VMEM((STEPS, CX, CY), F32),
            pltpu.VMEM((STEPS, CX, CY), F32),
            pltpu.VMEM((STEPS, CX, CY), F32),
            dma((7,)),
            dma((2,)),
            dma((2,)),
            dma((2,)),
            dma((2,)),
            dma((STEPS, NX)),
            dma((STEPS, NX)),
            dma((STEPS, NY)),
            dma((STEPS, NY)),
            dma((STEPS, NY)),
            dma((STEPS, NY)),
            dma((STEPS, NZ)),
            dma((STEPS, NZ)),
            dma((STEPS, NCH)),
            dma((STEPS, NCH)),
            dma((STEPS, NCH)),
            dma((STEPS, NCH)),
            dma((STEPS, NCH)),
            dma((STEPS, NCH)),
            dma((STEPS, NCH)),
        ],
        compiler_params=pltpu.CompilerParams(
            collective_id=0, has_side_effects=True, vmem_limit_bytes=VMEM_BYTES
        ),
        name="steps",
    )(sheet, cond, x_edge, y_edge, u, c, joule, z_edge)


def per_device(
    starting_warmth,
    sheet_stratum_number,
    stratum_heat_conduction,
    substance_kind,
    substance_kind_scaling,
    wire_piece_amperes,
    wire_piece_ohms_base,
    wire_piece_tile,
    wire_piece_voxel,
):
    shape = (SEGS // 128, 128)
    small = (sheet_stratum_number, stratum_heat_conduction, substance_kind_scaling)
    powers, columns, rows, *edges = spread_out(
        *small,
        wire_piece_amperes.reshape(shape),
        wire_piece_ohms_base.reshape(shape),
        wire_piece_tile.T,
        wire_piece_voxel.reshape(shape),
        starting_warmth,
        substance_kind,
    )
    joule = added(rows, powers, columns).reshape(CZ, CX, CY)
    rise = stepped(*small[:2], starting_warmth, joule, *edges)
    warmed = starting_warmth + rise
    return warmed, (1.0 + WARMING_SLOPE * warmed) * joule


def solution(mesh):
    return jax.shard_map(
        per_device,
        mesh=mesh,
        in_specs=(
            P("gz", "gx", "gy"),
            P(),
            P(),
            P("gz", "gx", "gy"),
            P(),
            P(("gx", "gy", "gz")),
            P(("gx", "gy", "gz")),
            P(("gx", "gy", "gz"), None),
            P(("gx", "gy", "gz")),
        ),
        out_specs=(P("gz", "gx", "gy"), P("gz", "gx", "gy")),
        check_vma=False,
    )
```
